256 devices in a mesh: section: 8 (over z_hi, x), dp: 32 (over z_lo, y, core).
Axes of the slice: x: 4, y: 4, z: 8 (z_hi: 2, z_lo: 4; z = z_hi * 4 + z_lo), core: 2. Of those that a mesh axis runs over, the one named last changes fastest.
Arguments:
- states: bfloat16 [128, 128, 2048], P('dp'), may hold values from -6 to 6
- outage: int32 [128, 128], P('dp'), may hold values 0 or 1
- targets: float32 [128, 128], P('dp'), may hold values from -6 to 6
- pattern: int32 [8, 2], replicated, may hold values from 0 to 3, as said below
- weights: bfloat16 [8, 2048, 2048], P('section'), may hold values from -0.75 to 0.75
- readout: float32 [2048], replicated, may hold values from -0.125 to 0.125
Outputs:
- grad_weights: float32 [8, 2048, 2048], P('section', 'dp')
The draws below stay inside these ranges and needn't reach their ends.
Inputs may be any that keep to these rules, and one draw needn't show every extreme that they name: `pattern`: rows 0 to 3 are the pairs (k, k); row 4 + k pairs block k with a block other than k.
All inputs are finite; a program needn't handle non-finite values. No bound on the sum of `outage` on one device may be relied on, other than what follows from the above.
Results may differ from the reference program's by a relative error of at most 0.006.
Values may be sent and summed in bfloat16 or wider, within the bound.
A program may use at most 128 MiB of HBM per device.

```python
import jax
import jax.numpy as jnp
from jax import lax

D = 2048
HEADS = 16
BUSES = 128
BLOCK = 32
NBLK = 4
SAMPLES = 128
SECTIONS = 8


def draw_pattern(key, part):
    diagonal = jnp.arange(NBLK, dtype=jnp.int32)
    offsets = jax.random.randint(key, (NBLK,), 1, NBLK, dtype=jnp.int32)
    partner = (diagonal + offsets) % NBLK
    own_pairs = jnp.stack([diagonal, diagonal], axis=1)
    cross_pairs = jnp.stack([diagonal, partner], axis=1)
    return jnp.concatenate([own_pairs, cross_pairs], axis=0).astype(jnp.int32)


def place_ends(entries, rng, least, largest):
    spot = [jax.random.randint(jax.random.fold_in(rng, axis), (), 0, length) for axis, length in enumerate(entries.shape)]
    longest = entries.shape.index(max(entries.shape))
    neighbour = spot[:longest] + [(spot[longest] + 1) % entries.shape[longest]] + spot[longest + 1:]
    return entries.at[tuple(spot)].set(least).at[tuple(neighbour)].set(largest)


def strengthened(array, stream_key, source, target, parts, factor):
    owner, partner = [(jnp.arange(array.shape[dim]) // (array.shape[dim] // parts)).reshape([-1 if axis == dim else 1 for axis in range(array.ndim)]) for dim in (source, target)]
    chosen = jax.random.permutation(stream_key, parts)[partner]
    strong = (owner == chosen) | (owner == (partner + parts // 2) % parts)
    return jnp.where(strong, factor * array, array)


def level_of(stream_key, shape, pieces, least, top_value):
    gain = 1.0
    for dim, parts in pieces:
        heights = jax.random.uniform(jax.random.fold_in(jax.random.fold_in(stream_key, 6), dim), (parts,), jnp.float32, least / len(pieces), top_value / len(pieces))
        gain = gain * jnp.repeat(jnp.exp(heights), shape[dim] // parts).reshape((-1,) + (1,) * (len(shape) - 1 - dim))
    return gain


def gaussian(rng, extent, spread, most, pieces=(), kind=jnp.bfloat16):
    drawn = jax.random.normal(rng, extent, jnp.float32) * spread
    if len(pieces) > 0:
        drawn = level_of(rng, extent, pieces, -0.22, 0.18) * drawn
    return jnp.clip(drawn, min=-most, max=most).astype(kind)


def heavy_noise(rng, shape, deviation, limit, cuts, heavy, kind=jnp.bfloat16):
    entries = deviation * jax.random.normal(rng, shape, jnp.float32)
    if cuts:
        entries = entries * level_of(rng, shape, cuts, -0.22, 0.18)
    return jnp.clip(strengthened(entries, jax.random.fold_in(rng, 3), *heavy), -limit, limit).astype(kind)


def setup_inputs(seed: int = 0) -> dict:
    key_of = jax.random.split(jax.random.key(seed), 7)
    return {
        "states": heavy_noise(key_of[0], (SAMPLES, BUSES, D), 1.0, 6.0, ((0, 32),), (0, 2, 32, 2.75)),
        "outage": place_ends((jax.random.randint(key_of[1], (SAMPLES, BUSES), 0, 8) < 7).astype(jnp.int32), jax.random.fold_in(key_of[1], 1), 0, 1),
        "targets": gaussian(key_of[2], (SAMPLES, BUSES), 1.0, 6.0, ((0, 32),), jnp.float32),
        "pattern": draw_pattern(jax.random.fold_in(key_of[6], 71), 0),
        "weights": gaussian(key_of[4], (SECTIONS, D, D), (D // 32) ** -0.5, 0.75, ((0, 8),)),
        "readout": gaussian(key_of[5], (D,), D ** -0.5, 0.125, (), jnp.float32),
    }


epsilon = 1e-05

def allowed_pairs(pattern, outage):
    buses = outage.shape[-1]
    block_count = buses // BLOCK
    block_ids = jnp.arange(block_count, dtype=jnp.int32)
    pair_hits = (pattern[:, 0][None, None, :] == block_ids[:, None, None]) & (pattern[:, 1][None, None, :] == block_ids[None, :, None])
    block_table = lax.optimization_barrier(jnp.max(pair_hits.astype(jnp.float32), axis=2))
    member = ((jnp.arange(buses, dtype=jnp.int32) // BLOCK)[:, None] == block_ids[None, :]).astype(jnp.float32)
    pair_mask = jnp.dot(jnp.dot(member, block_table, precision=lax.Precision.HIGHEST), member.T, precision=lax.Precision.HIGHEST)
    in_service = outage.astype(jnp.float32)
    self_mask = jnp.eye(buses, dtype=jnp.float32)
    return pair_mask[None] * jnp.maximum(in_service[:, None, :], self_mask[None])

def layer_forward(hidden, weight, allowed):
    num_states, buses, width = hidden.shape
    split_shape = (num_states, buses, HEADS, width // HEADS)
    hidden_f = hidden.astype(jnp.float32)
    centred = hidden_f - lax.optimization_barrier(jnp.mean(hidden_f, axis=-1, keepdims=True))
    inverse_std = lax.rsqrt(lax.optimization_barrier(jnp.mean(centred * centred, axis=-1, keepdims=True)) + epsilon)
    scaled = centred * inverse_std
    normed = scaled.astype(jnp.bfloat16)
    values_b = jnp.dot(normed.reshape(-1, width), weight, preferred_element_type=jnp.float32).astype(jnp.bfloat16).reshape(split_shape)
    features = lax.optimization_barrier((jax.nn.elu(values_b.astype(jnp.float32)) + 1.0).astype(jnp.bfloat16))
    features_f = features.astype(jnp.float32)
    kernel = jnp.einsum('nihc,njhc->nhij', features_f, features_f, precision=lax.Precision.HIGHEST) * allowed[:, None]
    totals = lax.optimization_barrier(jnp.sum(kernel, axis=-1, keepdims=True))
    attention = kernel / totals
    attention_b = lax.optimization_barrier(attention.astype(jnp.bfloat16))
    gathered = jnp.einsum('nhij,njhc->nihc', attention_b.astype(jnp.float32), values_b.astype(jnp.float32), precision=lax.Precision.HIGHEST)
    output = (hidden_f + gathered.reshape(num_states, buses, width)).astype(jnp.bfloat16)
    return (output, (scaled, inverse_std, values_b, attention, totals))

def layer_backward(upstream, weight, allowed, kept_parts):
    scaled, inverse_std, values_b, attention, totals = kept_parts
    num_states, buses, width = upstream.shape
    grad_f = upstream.astype(jnp.float32)
    grad_heads = grad_f.reshape(values_b.shape)
    values_f = values_b.astype(jnp.float32)
    features_f = lax.optimization_barrier((jax.nn.elu(values_f) + 1.0).astype(jnp.bfloat16)).astype(jnp.float32)
    attention_f = lax.optimization_barrier(attention.astype(jnp.bfloat16)).astype(jnp.float32)
    value_grad = jnp.einsum('nhij,nihc->njhc', attention_f, grad_heads, precision=lax.Precision.HIGHEST)
    attention_grad = jnp.einsum('nihc,njhc->nhij', grad_heads, values_f, precision=lax.Precision.HIGHEST)
    row_terms = lax.optimization_barrier(jnp.sum(attention_grad * attention, axis=-1, keepdims=True))
    kernel_grad = ((attention_grad - row_terms) / totals * allowed[:, None]).astype(jnp.bfloat16)
    kernel_f = lax.optimization_barrier(kernel_grad).astype(jnp.float32)
    feature_grad = jnp.einsum('nhij,njhc->nihc', kernel_f, features_f, precision=lax.Precision.HIGHEST)
    feature_grad = feature_grad + jnp.einsum('nhji,njhc->nihc', kernel_f, features_f, precision=lax.Precision.HIGHEST)
    slope = jnp.where(values_f > 0.0, 1.0, jnp.exp(jnp.minimum(values_f, 0.0)))
    value_total = (value_grad + feature_grad * slope).astype(jnp.bfloat16).reshape(num_states, buses, width)
    normed = scaled.astype(jnp.bfloat16)
    flat_total = value_total.reshape(-1, width)
    weight_grad = lax.dot_general(normed.reshape(-1, width), flat_total, (((0,), (0,)), ((), ())), preferred_element_type=jnp.float32)
    normed_grad = lax.dot_general(flat_total, weight, (((1,), (1,)), ((), ())), preferred_element_type=jnp.float32).reshape(num_states, buses, width)
    mean_grad = lax.optimization_barrier(jnp.mean(normed_grad, axis=-1, keepdims=True))
    mean_cross = lax.optimization_barrier(jnp.mean(normed_grad * scaled, axis=-1, keepdims=True))
    lower = (grad_f + inverse_std * (normed_grad - mean_grad - scaled * mean_cross)).astype(jnp.bfloat16)
    return (lower, weight_grad)

def reference(states, outage, targets, pattern, weights, readout):
    allowed = allowed_pairs(pattern, outage)
    layer_total = weights.shape[0]
    layer_inputs = []
    hidden = states
    for layer_index in range(layer_total):
        layer_inputs.append(hidden)
        hidden, unused = layer_forward(hidden, weights[layer_index], allowed)
    predicted = lax.optimization_barrier(jnp.sum(hidden.astype(jnp.float32) * readout, axis=-1))
    misfit = predicted - targets
    upstream = (misfit[..., None] * readout).astype(jnp.bfloat16)
    collected = []
    for layer_index in reversed(range(layer_total)):
        unused, kept_parts = layer_forward(layer_inputs[layer_index], weights[layer_index], allowed)
        upstream, weight_grad = layer_backward(upstream, weights[layer_index], allowed, kept_parts)
        collected.append(weight_grad)
    return jnp.stack(collected[::-1])
```

```python
import jax
import jax.numpy as jnp
from jax import lax
from jax.sharding import Mesh, PartitionSpec as P

HEADS = 16
BLOCK = 32


epsilon = 1e-05


def passed_along(block, axis, distance):
    devices = range(lax.axis_size(axis))
    route = [(i - distance, i) for i in devices if i - distance in devices]
    return lax.ppermute(block, axis, route)


def allowed_pairs(pattern, outage):
    buses = outage.shape[-1]
    block_count = buses // BLOCK
    block_ids = jnp.arange(block_count, dtype=jnp.int32)
    pair_hits = (pattern[:, 0][None, None, :] == block_ids[:, None, None]) & (
        pattern[:, 1][None, None, :] == block_ids[None, :, None]
    )
    block_table = jnp.max(pair_hits.astype(jnp.float32), axis=2)
    member = ((jnp.arange(buses, dtype=jnp.int32) // BLOCK)[:, None] == block_ids[None, :]).astype(
        jnp.float32
    )
    pair_mask = jnp.dot(
        jnp.dot(member, block_table, precision=lax.Precision.HIGHEST),
        member.T,
        precision=lax.Precision.HIGHEST,
    )
    in_service = outage.astype(jnp.float32)
    self_mask = jnp.eye(buses, dtype=jnp.float32)
    return pair_mask[None] * jnp.maximum(in_service[:, None, :], self_mask[None])


def layer_forward(hidden, weight, allowed):
    num_states, buses, width = hidden.shape
    split_shape = (num_states, buses, HEADS, width // HEADS)
    hidden_f = hidden.astype(jnp.float32)
    centred = hidden_f - jnp.mean(hidden_f, axis=-1, keepdims=True)
    inverse_std = lax.rsqrt(jnp.mean(centred * centred, axis=-1, keepdims=True) + epsilon)
    scaled = centred * inverse_std
    normed = scaled.astype(jnp.bfloat16)
    values_b = (
        jnp.dot(normed.reshape(-1, width), weight, preferred_element_type=jnp.float32)
        .astype(jnp.bfloat16)
        .reshape(split_shape)
    )
    features = (jax.nn.elu(values_b.astype(jnp.float32)) + 1.0).astype(jnp.bfloat16)
    kernel = (
        jnp.einsum("nihc,njhc->nhij", features, features, preferred_element_type=jnp.float32)
        * allowed[:, None]
    )
    totals = jnp.sum(kernel, axis=-1, keepdims=True)
    attention = kernel / totals
    attention_b = attention.astype(jnp.bfloat16)
    gathered = jnp.einsum(
        "nhij,njhc->nihc", attention_b, values_b, preferred_element_type=jnp.float32
    )
    output = (hidden_f + gathered.reshape(num_states, buses, width)).astype(jnp.bfloat16)
    return (output, (scaled, inverse_std, values_b, attention, totals))


def layer_backward(upstream, weight, allowed, kept_parts):
    scaled, inverse_std, values_b, attention, totals = kept_parts
    num_states, buses, width = upstream.shape
    grad_f = upstream.astype(jnp.float32)
    grad_heads = upstream.reshape(values_b.shape)
    values_f = values_b.astype(jnp.float32)
    features = (jax.nn.elu(values_f) + 1.0).astype(jnp.bfloat16)
    attention_b = attention.astype(jnp.bfloat16)
    value_grad = jnp.einsum(
        "nhij,nihc->njhc", attention_b, grad_heads, preferred_element_type=jnp.float32
    )
    attention_grad = jnp.einsum(
        "nihc,njhc->nhij", grad_heads, values_b, preferred_element_type=jnp.float32
    )
    row_terms = jnp.sum(attention_grad * attention, axis=-1, keepdims=True)
    kernel_grad = ((attention_grad - row_terms) / totals * allowed[:, None]).astype(jnp.bfloat16)
    feature_grad = jnp.einsum(
        "nhij,njhc->nihc", kernel_grad, features, preferred_element_type=jnp.float32
    )
    feature_grad = feature_grad + jnp.einsum(
        "nhji,njhc->nihc", kernel_grad, features, preferred_element_type=jnp.float32
    )
    slope = jnp.where(values_f > 0.0, 1.0, jnp.exp(jnp.minimum(values_f, 0.0)))
    value_total = (
        (value_grad + feature_grad * slope).astype(jnp.bfloat16).reshape(num_states, buses, width)
    )
    normed_grad = lax.dot_general(
        value_total.reshape(-1, width),
        weight,
        (((1,), (1,)), ((), ())),
        preferred_element_type=jnp.float32,
    ).reshape(num_states, buses, width)
    mean_grad = jnp.mean(normed_grad, axis=-1, keepdims=True)
    mean_cross = jnp.mean(normed_grad * scaled, axis=-1, keepdims=True)
    lower = (grad_f + inverse_std * (normed_grad - mean_grad - scaled * mean_cross)).astype(
        jnp.bfloat16
    )
    return (lower, value_total)


def per_device(states, outage, targets, pattern, weights, readout):
    sections = lax.axis_size("section")
    rank = lax.axis_index("section")
    micro, buses, width = states.shape
    weight = weights[0]
    allowed = allowed_pairs(pattern, outage)
    head_size = width // HEADS
    steps_total = sections + micro - 1
    zero_rows = jnp.zeros((buses, width), jnp.bfloat16)
    stash_init = (
        jnp.zeros((micro, buses, width), jnp.float32),
        jnp.zeros((micro, buses, 1), jnp.float32),
        jnp.zeros((micro, buses, HEADS, head_size), jnp.bfloat16),
        jnp.zeros((micro, HEADS, buses, buses), jnp.float32),
        jnp.zeros((micro, HEADS, buses, 1), jnp.float32),
    )
    upstream_init = jnp.zeros((micro, buses, width), jnp.bfloat16)

    def forward_step(step, carry):
        incoming, stashed, upstream_stash = carry
        slot_raw = step - rank
        active = (slot_raw >= 0) & (slot_raw < micro)
        slot = jnp.clip(slot_raw, 0, micro - 1)
        first_state = lax.dynamic_index_in_dim(states, slot, 0, keepdims=True)
        source = jnp.where(rank == 0, first_state, incoming[None])
        allowed_slot = lax.dynamic_index_in_dim(allowed, slot, 0, keepdims=True)

        def forward_do_work(stash_in, upstream_in):
            output, kept_parts = layer_forward(source, weight, allowed_slot)
            stash_out = tuple(
                (
                    lax.dynamic_update_index_in_dim(whole_array, new_piece, slot, 0)
                    for whole_array, new_piece in zip(stash_in, kept_parts)
                )
            )
            predicted = jnp.sum(output.astype(jnp.float32) * readout, axis=-1)
            misfit = predicted - lax.dynamic_index_in_dim(targets, slot, 0, keepdims=True)
            cotangent = (misfit[..., None] * readout).astype(jnp.bfloat16)
            upstream_out = lax.dynamic_update_index_in_dim(upstream_in, cotangent, slot, 0)
            return (output[0], stash_out, upstream_out)

        def forward_no_work(stash_in, upstream_in):
            return (zero_rows, stash_in, upstream_in)

        output, stashed, upstream_stash = lax.cond(
            active, forward_do_work, forward_no_work, stashed, upstream_stash
        )
        passed = passed_along(output, "section", 1)
        return (passed, stashed, upstream_stash)

    unused_rows, stashed, upstream_stash = lax.fori_loop(
        0, steps_total, forward_step, (zero_rows, stash_init, upstream_init)
    )
    totals_init = jnp.zeros((micro, buses, width), jnp.bfloat16)

    def backward_step(step, carry):
        incoming, collected = carry
        slot_raw = step - (sections - 1 - rank)
        active = (slot_raw >= 0) & (slot_raw < micro)
        slot = jnp.clip(slot_raw, 0, micro - 1)
        last_grad = lax.dynamic_index_in_dim(upstream_stash, slot, 0, keepdims=True)
        upstream = jnp.where(rank == sections - 1, last_grad, incoming[None])
        allowed_slot = lax.dynamic_index_in_dim(allowed, slot, 0, keepdims=True)

        def backward_do_work(collected_in):
            kept_parts = tuple(
                (
                    lax.dynamic_index_in_dim(whole_array, slot, 0, keepdims=True)
                    for whole_array in stashed
                )
            )
            lower, value_total = layer_backward(upstream, weight, allowed_slot, kept_parts)
            collected_out = lax.dynamic_update_index_in_dim(collected_in, value_total, slot, 0)
            return (lower[0], collected_out)

        def backward_no_work(collected_in):
            return (zero_rows, collected_in)

        lower, collected = lax.cond(active, backward_do_work, backward_no_work, collected)
        passed = passed_along(lower, "section", -1)
        return (passed, collected)

    unused_rows, collected = lax.fori_loop(0, steps_total, backward_step, (zero_rows, totals_init))
    cores = lax.axis_size("core")
    groups = lax.axis_size("dp_hi")
    rows_each = width // (groups * cores)
    normed_all = stashed[0].astype(jnp.bfloat16).reshape(micro * buses, groups, cores, rows_each)
    normed_all = jnp.swapaxes(normed_all, 1, 2).reshape(micro * buses, width)
    grad = lax.dot_general(
        normed_all,
        collected.reshape(micro * buses, width),
        (((0,), (0,)), ((), ())),
        preferred_element_type=jnp.float32,
    )
    half = lax.psum_scatter(grad, "core", scatter_dimension=0, tiled=True)
    summed = lax.psum_scatter(half, "dp_hi", scatter_dimension=0, tiled=True)
    return summed[None]


def solution(mesh):
    sections, dp = mesh.devices.shape
    split = Mesh(mesh.devices.reshape(sections, dp // 2, 2), ("section", "dp_hi", "core"))
    rows = ("dp_hi", "core")
    in_specs = (
        P(rows, None, None),
        P(rows, None),
        P(rows, None),
        P(),
        P("section", None, None),
        P(),
    )
    out_specs = P("section", rows, None)
    return jax.shard_map(
        per_device, mesh=split, in_specs=in_specs, out_specs=out_specs, check_vma=False
    )
```

```python
import jax
import jax.numpy as jnp
from jax import lax
from jax.sharding import Mesh, PartitionSpec as P

HEADS = 16
BLOCK = 32


epsilon = 1e-05


def passed_along(block, axis, distance):
    devices = range(lax.axis_size(axis))
    route = [(i - distance, i) for i in devices if i - distance in devices]
    return lax.ppermute(block, axis, route)


def allowed_pairs(pattern, outage):
    buses = outage.shape[-1]
    block_count = buses // BLOCK
    block_ids = jnp.arange(block_count, dtype=jnp.int32)
    pair_hits = (pattern[:, 0][None, None, :] == block_ids[:, None, None]) & (
        pattern[:, 1][None, None, :] == block_ids[None, :, None]
    )
    block_table = jnp.max(pair_hits.astype(jnp.float32), axis=2)
    member = ((jnp.arange(buses, dtype=jnp.int32) // BLOCK)[:, None] == block_ids[None, :]).astype(
        jnp.float32
    )
    pair_mask = jnp.dot(
        jnp.dot(member, block_table, precision=lax.Precision.HIGHEST),
        member.T,
        precision=lax.Precision.HIGHEST,
    )
    in_service = outage.astype(jnp.float32)
    self_mask = jnp.eye(buses, dtype=jnp.float32)
    return pair_mask[None] * jnp.maximum(in_service[:, None, :], self_mask[None])


def layer_forward(hidden, weight, allowed):
    num_states, buses, width = hidden.shape
    split_shape = (num_states, buses, HEADS, width // HEADS)
    hidden_f = hidden.astype(jnp.float32)
    centred = hidden_f - jnp.mean(hidden_f, axis=-1, keepdims=True)
    inverse_std = lax.rsqrt(jnp.mean(centred * centred, axis=-1, keepdims=True) + epsilon)
    scaled = centred * inverse_std
    normed = scaled.astype(jnp.bfloat16)
    values_b = (
        jnp.dot(normed.reshape(-1, width), weight, preferred_element_type=jnp.float32)
        .astype(jnp.bfloat16)
        .reshape(split_shape)
    )
    features = (jax.nn.elu(values_b.astype(jnp.float32)) + 1.0).astype(jnp.bfloat16)
    kernel = (
        jnp.einsum("nihc,njhc->nhij", features, features, preferred_element_type=jnp.float32)
        * allowed[:, None]
    )
    totals = jnp.sum(kernel, axis=-1, keepdims=True)
    attention = kernel / totals
    attention_b = attention.astype(jnp.bfloat16)
    gathered = jnp.einsum(
        "nhij,njhc->nihc", attention_b, values_b, preferred_element_type=jnp.float32
    )
    output = (hidden_f + gathered.reshape(num_states, buses, width)).astype(jnp.bfloat16)
    return (output, (scaled, inverse_std, values_b, attention, totals))


def layer_backward(upstream, weight, allowed, kept_parts):
    scaled, inverse_std, values_b, attention, totals = kept_parts
    num_states, buses, width = upstream.shape
    grad_f = upstream.astype(jnp.float32)
    grad_heads = upstream.reshape(values_b.shape)
    values_f = values_b.astype(jnp.float32)
    features = (jax.nn.elu(values_f) + 1.0).astype(jnp.bfloat16)
    attention_b = attention.astype(jnp.bfloat16)
    value_grad = jnp.einsum(
        "nhij,nihc->njhc", attention_b, grad_heads, preferred_element_type=jnp.float32
    )
    attention_grad = jnp.einsum(
        "nihc,njhc->nhij", grad_heads, values_b, preferred_element_type=jnp.float32
    )
    row_terms = jnp.sum(attention_grad * attention, axis=-1, keepdims=True)
    kernel_grad = ((attention_grad - row_terms) / totals * allowed[:, None]).astype(jnp.bfloat16)
    feature_grad = jnp.einsum(
        "nhij,njhc->nihc", kernel_grad, features, preferred_element_type=jnp.float32
    )
    feature_grad = feature_grad + jnp.einsum(
        "nhji,njhc->nihc", kernel_grad, features, preferred_element_type=jnp.float32
    )
    slope = jnp.where(values_f > 0.0, 1.0, jnp.exp(jnp.minimum(values_f, 0.0)))
    value_total = (
        (value_grad + feature_grad * slope).astype(jnp.bfloat16).reshape(num_states, buses, width)
    )
    normed_grad = lax.dot_general(
        value_total.reshape(-1, width),
        weight,
        (((1,), (1,)), ((), ())),
        preferred_element_type=jnp.float32,
    ).reshape(num_states, buses, width)
    mean_grad = jnp.mean(normed_grad, axis=-1, keepdims=True)
    mean_cross = jnp.mean(normed_grad * scaled, axis=-1, keepdims=True)
    lower = (grad_f + inverse_std * (normed_grad - mean_grad - scaled * mean_cross)).astype(
        jnp.bfloat16
    )
    return (lower, value_total)


def per_device(states, outage, targets, pattern, weights, readout):
    sections = lax.axis_size("section")
    rank = lax.axis_index("section")
    micro, buses, width = states.shape
    weight = weights[0]
    allowed = allowed_pairs(pattern, outage)
    head_size = width // HEADS
    steps_total = sections + micro - 1
    zero_rows = jnp.zeros((buses, width), jnp.bfloat16)
    stash_init = (
        jnp.zeros((micro, buses, width), jnp.float32),
        jnp.zeros((micro, buses, 1), jnp.float32),
        jnp.zeros((micro, buses, HEADS, head_size), jnp.bfloat16),
        jnp.zeros((micro, HEADS, buses, buses), jnp.float32),
        jnp.zeros((micro, HEADS, buses, 1), jnp.float32),
    )
    upstream_init = jnp.zeros((micro, buses, width), jnp.bfloat16)

    def forward_step(step, carry):
        incoming, stashed, upstream_stash = carry
        slot_raw = step - rank
        active = (slot_raw >= 0) & (slot_raw < micro)
        slot = jnp.clip(slot_raw, 0, micro - 1)
        first_state = lax.dynamic_index_in_dim(states, slot, 0, keepdims=True)
        source = jnp.where(rank == 0, first_state, incoming[None])
        allowed_slot = lax.dynamic_index_in_dim(allowed, slot, 0, keepdims=True)

        def forward_do_work(stash_in, upstream_in):
            output, kept_parts = layer_forward(source, weight, allowed_slot)
            stash_out = tuple(
                (
                    lax.dynamic_update_index_in_dim(whole_array, new_piece, slot, 0)
                    for whole_array, new_piece in zip(stash_in, kept_parts)
                )
            )
            predicted = jnp.sum(output.astype(jnp.float32) * readout, axis=-1)
            misfit = predicted - lax.dynamic_index_in_dim(targets, slot, 0, keepdims=True)
            cotangent = (misfit[..., None] * readout).astype(jnp.bfloat16)
            upstream_out = lax.dynamic_update_index_in_dim(upstream_in, cotangent, slot, 0)
            return (output[0], stash_out, upstream_out)

        def forward_no_work(stash_in, upstream_in):
            return (zero_rows, stash_in, upstream_in)

        output, stashed, upstream_stash = lax.cond(
            active, forward_do_work, forward_no_work, stashed, upstream_stash
        )
        passed = passed_along(output, "section", 1)
        return (passed, stashed, upstream_stash)

    unused_rows, stashed, upstream_stash = lax.fori_loop(
        0, steps_total, forward_step, (zero_rows, stash_init, upstream_init)
    )
    totals_init = jnp.zeros((micro, buses, width), jnp.bfloat16)

    def backward_step(step, carry):
        incoming, collected = carry
        slot_raw = step - (sections - 1 - rank)
        active = (slot_raw >= 0) & (slot_raw < micro)
        slot = jnp.clip(slot_raw, 0, micro - 1)
        last_grad = lax.dynamic_index_in_dim(upstream_stash, slot, 0, keepdims=True)
        upstream = jnp.where(rank == sections - 1, last_grad, incoming[None])
        allowed_slot = lax.dynamic_index_in_dim(allowed, slot, 0, keepdims=True)

        def backward_do_work(collected_in):
            kept_parts = tuple(
                (
                    lax.dynamic_index_in_dim(whole_array, slot, 0, keepdims=True)
                    for whole_array in stashed
                )
            )
            lower, value_total = layer_backward(upstream, weight, allowed_slot, kept_parts)
            collected_out = lax.dynamic_update_index_in_dim(collected_in, value_total, slot, 0)
            return (lower[0], collected_out)

        def backward_no_work(collected_in):
            return (zero_rows, collected_in)

        lower, collected = lax.cond(active, backward_do_work, backward_no_work, collected)
        passed = passed_along(lower, "section", -1)
        return (passed, collected)

    unused_rows, collected = lax.fori_loop(0, steps_total, backward_step, (zero_rows, totals_init))
    cores = lax.axis_size("core")
    groups = lax.axis_size("dp_hi")
    rows_each = width // (groups * cores)
    normed_all = stashed[0].astype(jnp.bfloat16).reshape(micro * buses, groups, cores, rows_each)
    normed_all = jnp.swapaxes(normed_all, 1, 2).reshape(micro * buses, width)
    grad = lax.dot_general(
        normed_all,
        collected.reshape(micro * buses, width),
        (((0,), (0,)), ((), ())),
        preferred_element_type=jnp.float32,
    )
    core = lax.axis_index("core")
    pieces = grad.reshape(cores, width // cores, width)
    kept = lax.dynamic_index_in_dim(pieces, core, 0, keepdims=False)
    sent = lax.dynamic_index_in_dim(pieces, 1 - core, 0, keepdims=False)
    half = kept + lax.ppermute(sent, "core", [(0, 1), (1, 0)])
    summed = lax.psum_scatter(half, "dp_hi", scatter_dimension=0, tiled=True)
    return summed[None]


def solution(mesh):
    sections, dp = mesh.devices.shape
    split = Mesh(mesh.devices.reshape(sections, dp // 2, 2), ("section", "dp_hi", "core"))
    rows = ("dp_hi", "core")
    in_specs = (
        P(rows, None, None),
        P(rows, None),
        P(rows, None),
        P(),
        P("section", None, None),
        P(),
    )
    out_specs = P("section", rows, None)
    return jax.shard_map(
        per_device, mesh=split, in_specs=in_specs, out_specs=out_specs, check_vma=False
    )
```

```python
import jax
import jax.numpy as jnp
from jax import lax
from jax.sharding import Mesh, PartitionSpec as P

HEADS = 16
BLOCK = 32


epsilon = 1e-05


def passed_along(block, axis, distance):
    devices = range(lax.axis_size(axis))
    route = [(i - distance, i) for i in devices if i - distance in devices]
    return lax.ppermute(block, axis, route)


def scatter_sum(block, axis):
    count = lax.axis_size(axis)
    me = lax.axis_index(axis)
    pieces = block.reshape(count, block.shape[0] // count, block.shape[1])
    total = lax.dynamic_index_in_dim(pieces, me, 0, keepdims=False)
    for shift in range(1, count):
        sent = lax.dynamic_index_in_dim(pieces, (me + shift) % count, 0, keepdims=False)
        route = [(i, (i + shift) % count) for i in range(count)]
        total = total + lax.ppermute(sent, axis, route)
    return total


def allowed_pairs(pattern, outage):
    buses = outage.shape[-1]
    block_count = buses // BLOCK
    block_ids = jnp.arange(block_count, dtype=jnp.int32)
    pair_hits = (pattern[:, 0][None, None, :] == block_ids[:, None, None]) & (
        pattern[:, 1][None, None, :] == block_ids[None, :, None]
    )
    block_table = jnp.max(pair_hits.astype(jnp.float32), axis=2)
    member = ((jnp.arange(buses, dtype=jnp.int32) // BLOCK)[:, None] == block_ids[None, :]).astype(
        jnp.float32
    )
    pair_mask = jnp.dot(
        jnp.dot(member, block_table, precision=lax.Precision.HIGHEST),
        member.T,
        precision=lax.Precision.HIGHEST,
    )
    in_service = outage.astype(jnp.float32)
    self_mask = jnp.eye(buses, dtype=jnp.float32)
    return pair_mask[None] * jnp.maximum(in_service[:, None, :], self_mask[None])


def layer_forward(hidden, weight, allowed):
    num_states, buses, width = hidden.shape
    split_shape = (num_states, buses, HEADS, width // HEADS)
    hidden_f = hidden.astype(jnp.float32)
    centred = hidden_f - jnp.mean(hidden_f, axis=-1, keepdims=True)
    inverse_std = lax.rsqrt(jnp.mean(centred * centred, axis=-1, keepdims=True) + epsilon)
    scaled = centred * inverse_std
    normed = scaled.astype(jnp.bfloat16)
    values_b = (
        jnp.dot(normed.reshape(-1, width), weight, preferred_element_type=jnp.float32)
        .astype(jnp.bfloat16)
        .reshape(split_shape)
    )
    features = (jax.nn.elu(values_b.astype(jnp.float32)) + 1.0).astype(jnp.bfloat16)
    kernel = (
        jnp.einsum("nihc,njhc->nhij", features, features, preferred_element_type=jnp.float32)
        * allowed[:, None]
    )
    totals = jnp.sum(kernel, axis=-1, keepdims=True)
    attention = kernel / totals
    attention_b = attention.astype(jnp.bfloat16)
    gathered = jnp.einsum(
        "nhij,njhc->nihc", attention_b, values_b, preferred_element_type=jnp.float32
    )
    output = (hidden_f + gathered.reshape(num_states, buses, width)).astype(jnp.bfloat16)
    return (output, (scaled, inverse_std, values_b, attention, totals))


def layer_backward(upstream, weight, allowed, kept_parts):
    scaled, inverse_std, values_b, attention, totals = kept_parts
    num_states, buses, width = upstream.shape
    grad_f = upstream.astype(jnp.float32)
    grad_heads = upstream.reshape(values_b.shape)
    values_f = values_b.astype(jnp.float32)
    features = (jax.nn.elu(values_f) + 1.0).astype(jnp.bfloat16)
    attention_b = attention.astype(jnp.bfloat16)
    value_grad = jnp.einsum(
        "nhij,nihc->njhc", attention_b, grad_heads, preferred_element_type=jnp.float32
    )
    attention_grad = jnp.einsum(
        "nihc,njhc->nhij", grad_heads, values_b, preferred_element_type=jnp.float32
    )
    row_terms = jnp.sum(attention_grad * attention, axis=-1, keepdims=True)
    kernel_grad = ((attention_grad - row_terms) / totals * allowed[:, None]).astype(jnp.bfloat16)
    feature_grad = jnp.einsum(
        "nhij,njhc->nihc", kernel_grad, features, preferred_element_type=jnp.float32
    )
    feature_grad = feature_grad + jnp.einsum(
        "nhji,njhc->nihc", kernel_grad, features, preferred_element_type=jnp.float32
    )
    slope = jnp.where(values_f > 0.0, 1.0, jnp.exp(jnp.minimum(values_f, 0.0)))
    value_total = (
        (value_grad + feature_grad * slope).astype(jnp.bfloat16).reshape(num_states, buses, width)
    )
    normed_grad = lax.dot_general(
        value_total.reshape(-1, width),
        weight,
        (((1,), (1,)), ((), ())),
        preferred_element_type=jnp.float32,
    ).reshape(num_states, buses, width)
    mean_grad = jnp.mean(normed_grad, axis=-1, keepdims=True)
    mean_cross = jnp.mean(normed_grad * scaled, axis=-1, keepdims=True)
    lower = (grad_f + inverse_std * (normed_grad - mean_grad - scaled * mean_cross)).astype(
        jnp.bfloat16
    )
    return (lower, value_total)


def per_device(states, outage, targets, pattern, weights, readout):
    sections = lax.axis_size("section")
    rank = lax.axis_index("section")
    micro, buses, width = states.shape
    weight = weights[0]
    allowed = allowed_pairs(pattern, outage)
    head_size = width // HEADS
    steps_total = sections + micro - 1
    zero_rows = jnp.zeros((buses, width), jnp.bfloat16)
    stash_init = (
        jnp.zeros((micro, buses, width), jnp.float32),
        jnp.zeros((micro, buses, 1), jnp.float32),
        jnp.zeros((micro, buses, HEADS, head_size), jnp.bfloat16),
        jnp.zeros((micro, HEADS, buses, buses), jnp.float32),
        jnp.zeros((micro, HEADS, buses, 1), jnp.float32),
    )
    upstream_init = jnp.zeros((micro, buses, width), jnp.bfloat16)

    def forward_step(step, carry):
        incoming, stashed, upstream_stash = carry
        slot_raw = step - rank
        active = (slot_raw >= 0) & (slot_raw < micro)
        slot = jnp.clip(slot_raw, 0, micro - 1)
        first_state = lax.dynamic_index_in_dim(states, slot, 0, keepdims=True)
        source = jnp.where(rank == 0, first_state, incoming[None])
        allowed_slot = lax.dynamic_index_in_dim(allowed, slot, 0, keepdims=True)

        def forward_do_work(stash_in, upstream_in):
            output, kept_parts = layer_forward(source, weight, allowed_slot)
            stash_out = tuple(
                (
                    lax.dynamic_update_index_in_dim(whole_array, new_piece, slot, 0)
                    for whole_array, new_piece in zip(stash_in, kept_parts)
                )
            )
            predicted = jnp.sum(output.astype(jnp.float32) * readout, axis=-1)
            misfit = predicted - lax.dynamic_index_in_dim(targets, slot, 0, keepdims=True)
            cotangent = (misfit[..., None] * readout).astype(jnp.bfloat16)
            upstream_out = lax.dynamic_update_index_in_dim(upstream_in, cotangent, slot, 0)
            return (output[0], stash_out, upstream_out)

        def forward_no_work(stash_in, upstream_in):
            return (zero_rows, stash_in, upstream_in)

        output, stashed, upstream_stash = lax.cond(
            active, forward_do_work, forward_no_work, stashed, upstream_stash
        )
        passed = passed_along(output, "section", 1)
        return (passed, stashed, upstream_stash)

    unused_rows, stashed, upstream_stash = lax.fori_loop(
        0, steps_total, forward_step, (zero_rows, stash_init, upstream_init)
    )
    totals_init = jnp.zeros((micro, buses, width), jnp.bfloat16)

    def backward_step(step, carry):
        incoming, collected = carry
        slot_raw = step - (sections - 1 - rank)
        active = (slot_raw >= 0) & (slot_raw < micro)
        slot = jnp.clip(slot_raw, 0, micro - 1)
        last_grad = lax.dynamic_index_in_dim(upstream_stash, slot, 0, keepdims=True)
        upstream = jnp.where(rank == sections - 1, last_grad, incoming[None])
        allowed_slot = lax.dynamic_index_in_dim(allowed, slot, 0, keepdims=True)

        def backward_do_work(collected_in):
            kept_parts = tuple(
                (
                    lax.dynamic_index_in_dim(whole_array, slot, 0, keepdims=True)
                    for whole_array in stashed
                )
            )
            lower, value_total = layer_backward(upstream, weight, allowed_slot, kept_parts)
            collected_out = lax.dynamic_update_index_in_dim(collected_in, value_total, slot, 0)
            return (lower[0], collected_out)

        def backward_no_work(collected_in):
            return (zero_rows, collected_in)

        lower, collected = lax.cond(active, backward_do_work, backward_no_work, collected)
        passed = passed_along(lower, "section", -1)
        return (passed, collected)

    unused_rows, collected = lax.fori_loop(0, steps_total, backward_step, (zero_rows, totals_init))
    cores = lax.axis_size("core")
    ys = lax.axis_size("y")
    zs = lax.axis_size("z")
    rows_each = width // (zs * ys * cores)
    normed_all = stashed[0].astype(jnp.bfloat16).reshape(micro * buses, zs, ys, cores, rows_each)
    normed_all = jnp.transpose(normed_all, (0, 3, 2, 1, 4)).reshape(micro * buses, width)
    grad = lax.dot_general(
        normed_all,
        collected.reshape(micro * buses, width),
        (((0,), (0,)), ((), ())),
        preferred_element_type=jnp.float32,
    )
    summed = grad
    for axis in ("core", "y", "z"):
        summed = scatter_sum(summed, axis)
    return summed[None]


def solution(mesh):
    sections, dp = mesh.devices.shape
    split = Mesh(mesh.devices.reshape(sections, 4, dp // 8, 2), ("section", "z", "y", "core"))
    rows = ("z", "y", "core")
    in_specs = (
        P(rows, None, None),
        P(rows, None),
        P(rows, None),
        P(),
        P("section", None, None),
        P(),
    )
    out_specs = P("section", rows, None)
    return jax.shard_map(
        per_device, mesh=split, in_specs=in_specs, out_specs=out_specs, check_vma=False
    )
```

```python
import jax
import jax.numpy as jnp
from jax import lax
from jax.sharding import Mesh, PartitionSpec as P

HEADS = 16
BLOCK = 32


epsilon = 1e-05


def passed_along(block, axis, distance):
    devices = range(lax.axis_size(axis))
    route = [(i - distance, i) for i in devices if i - distance in devices]
    return lax.ppermute(block, axis, route)


def allowed_pairs(pattern, outage):
    buses = outage.shape[-1]
    block_count = buses // BLOCK
    block_ids = jnp.arange(block_count, dtype=jnp.int32)
    pair_hits = (pattern[:, 0][None, None, :] == block_ids[:, None, None]) & (
        pattern[:, 1][None, None, :] == block_ids[None, :, None]
    )
    block_table = jnp.max(pair_hits.astype(jnp.float32), axis=2)
    member = ((jnp.arange(buses, dtype=jnp.int32) // BLOCK)[:, None] == block_ids[None, :]).astype(
        jnp.float32
    )
    pair_mask = jnp.dot(
        jnp.dot(member, block_table, precision=lax.Precision.HIGHEST),
        member.T,
        precision=lax.Precision.HIGHEST,
    )
    in_service = outage.astype(jnp.float32)
    self_mask = jnp.eye(buses, dtype=jnp.float32)
    return pair_mask[None] * jnp.maximum(in_service[:, None, :], self_mask[None])


def layer_forward(hidden, weight, allowed):
    num_states, buses, width = hidden.shape
    split_shape = (num_states, buses, HEADS, width // HEADS)
    hidden_f = hidden.astype(jnp.float32)
    centred = hidden_f - jnp.mean(hidden_f, axis=-1, keepdims=True)
    inverse_std = lax.rsqrt(jnp.mean(centred * centred, axis=-1, keepdims=True) + epsilon)
    scaled = centred * inverse_std
    normed = scaled.astype(jnp.bfloat16)
    values_b = (
        jnp.dot(normed.reshape(-1, width), weight, preferred_element_type=jnp.float32)
        .astype(jnp.bfloat16)
        .reshape(split_shape)
    )
    features = (jax.nn.elu(values_b.astype(jnp.float32)) + 1.0).astype(jnp.bfloat16)
    kernel = (
        jnp.einsum("nihc,njhc->nhij", features, features, preferred_element_type=jnp.float32)
        * allowed[:, None]
    )
    totals = jnp.sum(kernel, axis=-1, keepdims=True)
    attention = kernel / totals
    attention_b = attention.astype(jnp.bfloat16)
    gathered = jnp.einsum(
        "nhij,njhc->nihc", attention_b, values_b, preferred_element_type=jnp.float32
    )
    output = (hidden_f + gathered.reshape(num_states, buses, width)).astype(jnp.bfloat16)
    return (output, (scaled, inverse_std, values_b, attention, totals))


def layer_backward(upstream, weight, allowed, kept_parts):
    scaled, inverse_std, values_b, attention, totals = kept_parts
    num_states, buses, width = upstream.shape
    grad_f = upstream.astype(jnp.float32)
    grad_heads = upstream.reshape(values_b.shape)
    values_f = values_b.astype(jnp.float32)
    features = (jax.nn.elu(values_f) + 1.0).astype(jnp.bfloat16)
    attention_b = attention.astype(jnp.bfloat16)
    value_grad = jnp.einsum(
        "nhij,nihc->njhc", attention_b, grad_heads, preferred_element_type=jnp.float32
    )
    attention_grad = jnp.einsum(
        "nihc,njhc->nhij", grad_heads, values_b, preferred_element_type=jnp.float32
    )
    row_terms = jnp.sum(attention_grad * attention, axis=-1, keepdims=True)
    kernel_grad = ((attention_grad - row_terms) / totals * allowed[:, None]).astype(jnp.bfloat16)
    feature_grad = jnp.einsum(
        "nhij,njhc->nihc", kernel_grad, features, preferred_element_type=jnp.float32
    )
    feature_grad = feature_grad + jnp.einsum(
        "nhji,njhc->nihc", kernel_grad, features, preferred_element_type=jnp.float32
    )
    slope = jnp.where(values_f > 0.0, 1.0, jnp.exp(jnp.minimum(values_f, 0.0)))
    value_total = (
        (value_grad + feature_grad * slope).astype(jnp.bfloat16).reshape(num_states, buses, width)
    )
    normed_grad = lax.dot_general(
        value_total.reshape(-1, width),
        weight,
        (((1,), (1,)), ((), ())),
        preferred_element_type=jnp.float32,
    ).reshape(num_states, buses, width)
    mean_grad = jnp.mean(normed_grad, axis=-1, keepdims=True)
    mean_cross = jnp.mean(normed_grad * scaled, axis=-1, keepdims=True)
    lower = (grad_f + inverse_std * (normed_grad - mean_grad - scaled * mean_cross)).astype(
        jnp.bfloat16
    )
    return (lower, value_total)


def per_device(states, outage, targets, pattern, weights, readout):
    sections = lax.axis_size("section")
    rank = lax.axis_index("section")
    micro, buses, width = states.shape
    weight = weights[0]
    allowed = allowed_pairs(pattern, outage)
    head_size = width // HEADS
    steps_total = sections + micro - 1
    zero_rows = jnp.zeros((buses, width), jnp.bfloat16)
    stash_init = (
        jnp.zeros((micro, buses, width), jnp.float32),
        jnp.zeros((micro, buses, 1), jnp.float32),
        jnp.zeros((micro, buses, HEADS, head_size), jnp.bfloat16),
        jnp.zeros((micro, HEADS, buses, buses), jnp.float32),
        jnp.zeros((micro, HEADS, buses, 1), jnp.float32),
    )
    upstream_init = jnp.zeros((micro, buses, width), jnp.bfloat16)

    def forward_step(step, carry):
        incoming, stashed, upstream_stash = carry
        slot_raw = step - rank
        active = (slot_raw >= 0) & (slot_raw < micro)
        slot = jnp.clip(slot_raw, 0, micro - 1)
        first_state = lax.dynamic_index_in_dim(states, slot, 0, keepdims=True)
        source = jnp.where(rank == 0, first_state, incoming[None])
        allowed_slot = lax.dynamic_index_in_dim(allowed, slot, 0, keepdims=True)

        def forward_do_work(stash_in, upstream_in):
            output, kept_parts = layer_forward(source, weight, allowed_slot)
            stash_out = tuple(
                (
                    lax.dynamic_update_index_in_dim(whole_array, new_piece, slot, 0)
                    for whole_array, new_piece in zip(stash_in, kept_parts)
                )
            )
            predicted = jnp.sum(output.astype(jnp.float32) * readout, axis=-1)
            misfit = predicted - lax.dynamic_index_in_dim(targets, slot, 0, keepdims=True)
            cotangent = (misfit[..., None] * readout).astype(jnp.bfloat16)
            upstream_out = lax.dynamic_update_index_in_dim(upstream_in, cotangent, slot, 0)
            return (output[0], stash_out, upstream_out)

        def forward_no_work(stash_in, upstream_in):
            return (zero_rows, stash_in, upstream_in)

        output, stashed, upstream_stash = lax.cond(
            active, forward_do_work, forward_no_work, stashed, upstream_stash
        )
        passed = passed_along(output, "section", 1)
        return (passed, stashed, upstream_stash)

    unused_rows, stashed, upstream_stash = lax.fori_loop(
        0, steps_total, forward_step, (zero_rows, stash_init, upstream_init)
    )
    totals_init = jnp.zeros((micro, buses, width), jnp.bfloat16)

    def backward_step(step, carry):
        incoming, collected = carry
        slot_raw = step - (sections - 1 - rank)
        active = (slot_raw >= 0) & (slot_raw < micro)
        slot = jnp.clip(slot_raw, 0, micro - 1)
        last_grad = lax.dynamic_index_in_dim(upstream_stash, slot, 0, keepdims=True)
        upstream = jnp.where(rank == sections - 1, last_grad, incoming[None])
        allowed_slot = lax.dynamic_index_in_dim(allowed, slot, 0, keepdims=True)

        def backward_do_work(collected_in):
            kept_parts = tuple(
                (
                    lax.dynamic_index_in_dim(whole_array, slot, 0, keepdims=True)
                    for whole_array in stashed
                )
            )
            lower, value_total = layer_backward(upstream, weight, allowed_slot, kept_parts)
            collected_out = lax.dynamic_update_index_in_dim(collected_in, value_total, slot, 0)
            return (lower[0], collected_out)

        def backward_no_work(collected_in):
            return (zero_rows, collected_in)

        lower, collected = lax.cond(active, backward_do_work, backward_no_work, collected)
        passed = passed_along(lower, "section", -1)
        return (passed, collected)

    unused_rows, collected = lax.fori_loop(0, steps_total, backward_step, (zero_rows, totals_init))
    cores = lax.axis_size("core")
    groups = lax.axis_size("dp_hi")
    core = lax.axis_index("core")
    rows_each = width // (groups * cores)
    normed_all = stashed[0].astype(jnp.bfloat16).reshape(micro * buses, groups, cores, rows_each)
    totals_all = collected.reshape(micro * buses, width)

    def partial_grad(which):
        chosen = lax.dynamic_index_in_dim(normed_all, which, 2, keepdims=False)
        return lax.dot_general(
            chosen.reshape(micro * buses, groups * rows_each),
            totals_all,
            (((0,), (0,)), ((), ())),
            preferred_element_type=jnp.float32,
        )

    received = lax.ppermute(partial_grad(1 - core), "core", [(0, 1), (1, 0)])
    half = lax.optimization_barrier(partial_grad(core)) + received
    summed = lax.psum_scatter(
        half.astype(jnp.bfloat16), "dp_hi", scatter_dimension=0, tiled=True
    ).astype(jnp.float32)
    return summed[None]


def solution(mesh):
    sections, dp = mesh.devices.shape
    split = Mesh(mesh.devices.reshape(sections, dp // 2, 2), ("section", "dp_hi", "core"))
    rows = ("dp_hi", "core")
    in_specs = (
        P(rows, None, None),
        P(rows, None),
        P(rows, None),
        P(),
        P("section", None, None),
        P(),
    )
    out_specs = P("section", rows, None)
    return jax.shard_map(
        per_device, mesh=split, in_specs=in_specs, out_specs=out_specs, check_vma=False
    )
```

```python
import jax
import jax.numpy as jnp
from jax import lax
from jax.sharding import Mesh, PartitionSpec as P

HEADS = 16
BLOCK = 32


epsilon = 1e-05


def passed_along(block, axis, distance):
    devices = range(lax.axis_size(axis))
    route = [(i - distance, i) for i in devices if i - distance in devices]
    return lax.ppermute(block, axis, route)


def allowed_pairs(pattern, outage):
    buses = outage.shape[-1]
    block_count = buses // BLOCK
    block_ids = jnp.arange(block_count, dtype=jnp.int32)
    pair_hits = (pattern[:, 0][None, None, :] == block_ids[:, None, None]) & (
        pattern[:, 1][None, None, :] == block_ids[None, :, None]
    )
    block_table = jnp.max(pair_hits.astype(jnp.float32), axis=2)
    member = ((jnp.arange(buses, dtype=jnp.int32) // BLOCK)[:, None] == block_ids[None, :]).astype(
        jnp.float32
    )
    pair_mask = jnp.dot(
        jnp.dot(member, block_table, precision=lax.Precision.HIGHEST),
        member.T,
        precision=lax.Precision.HIGHEST,
    )
    in_service = outage.astype(jnp.float32)
    self_mask = jnp.eye(buses, dtype=jnp.float32)
    return pair_mask[None] * jnp.maximum(in_service[:, None, :], self_mask[None])


def layer_forward(hidden, weight, allowed):
    num_states, buses, width = hidden.shape
    split_shape = (num_states, buses, HEADS, width // HEADS)
    hidden_f = hidden.astype(jnp.float32)
    centred = hidden_f - jnp.mean(hidden_f, axis=-1, keepdims=True)
    inverse_std = lax.rsqrt(jnp.mean(centred * centred, axis=-1, keepdims=True) + epsilon)
    scaled = centred * inverse_std
    normed = scaled.astype(jnp.bfloat16)
    values_b = (
        jnp.dot(normed.reshape(-1, width), weight, preferred_element_type=jnp.float32)
        .astype(jnp.bfloat16)
        .reshape(split_shape)
    )
    features = (jax.nn.elu(values_b.astype(jnp.float32)) + 1.0).astype(jnp.bfloat16)
    kernel = (
        jnp.einsum("nihc,njhc->nhij", features, features, preferred_element_type=jnp.float32)
        * allowed[:, None]
    )
    totals = jnp.sum(kernel, axis=-1, keepdims=True)
    attention = kernel / totals
    attention_b = attention.astype(jnp.bfloat16)
    gathered = jnp.einsum(
        "nhij,njhc->nihc", attention_b, values_b, preferred_element_type=jnp.float32
    )
    output = (hidden_f + gathered.reshape(num_states, buses, width)).astype(jnp.bfloat16)
    return (output, (scaled, inverse_std, values_b, attention, totals))


def layer_backward(upstream, weight, allowed, kept_parts):
    scaled, inverse_std, values_b, attention, totals = kept_parts
    num_states, buses, width = upstream.shape
    grad_f = upstream.astype(jnp.float32)
    grad_heads = upstream.reshape(values_b.shape)
    values_f = values_b.astype(jnp.float32)
    features = (jax.nn.elu(values_f) + 1.0).astype(jnp.bfloat16)
    attention_b = attention.astype(jnp.bfloat16)
    value_grad = jnp.einsum(
        "nhij,nihc->njhc", attention_b, grad_heads, preferred_element_type=jnp.float32
    )
    attention_grad = jnp.einsum(
        "nihc,njhc->nhij", grad_heads, values_b, preferred_element_type=jnp.float32
    )
    row_terms = jnp.sum(attention_grad * attention, axis=-1, keepdims=True)
    kernel_grad = ((attention_grad - row_terms) / totals * allowed[:, None]).astype(jnp.bfloat16)
    feature_grad = jnp.einsum(
        "nhij,njhc->nihc", kernel_grad, features, preferred_element_type=jnp.float32
    )
    feature_grad = feature_grad + jnp.einsum(
        "nhji,njhc->nihc", kernel_grad, features, preferred_element_type=jnp.float32
    )
    slope = jnp.where(values_f > 0.0, 1.0, jnp.exp(jnp.minimum(values_f, 0.0)))
    value_total = (
        (value_grad + feature_grad * slope).astype(jnp.bfloat16).reshape(num_states, buses, width)
    )
    normed_grad = lax.dot_general(
        value_total.reshape(-1, width),
        weight,
        (((1,), (1,)), ((), ())),
        preferred_element_type=jnp.float32,
    ).reshape(num_states, buses, width)
    mean_grad = jnp.mean(normed_grad, axis=-1, keepdims=True)
    mean_cross = jnp.mean(normed_grad * scaled, axis=-1, keepdims=True)
    lower = (grad_f + inverse_std * (normed_grad - mean_grad - scaled * mean_cross)).astype(
        jnp.bfloat16
    )
    return (lower, value_total)


def per_device(states, outage, targets, pattern, weights, readout):
    sections = lax.axis_size("section")
    rank = lax.axis_index("section")
    micro, buses, width = states.shape
    weight = weights[0]
    allowed = allowed_pairs(pattern, outage)
    head_size = width // HEADS
    steps_total = sections + micro - 1
    zero_rows = jnp.zeros((buses, width), jnp.bfloat16)
    stash_init = (
        jnp.zeros((micro, buses, width), jnp.float32),
        jnp.zeros((micro, buses, 1), jnp.float32),
        jnp.zeros((micro, buses, HEADS, head_size), jnp.bfloat16),
        jnp.zeros((micro, HEADS, buses, buses), jnp.float32),
        jnp.zeros((micro, HEADS, buses, 1), jnp.float32),
    )
    upstream_init = jnp.zeros((micro, buses, width), jnp.bfloat16)

    def forward_step(step, carry):
        incoming, stashed, upstream_stash = carry
        slot_raw = step - rank
        active = (slot_raw >= 0) & (slot_raw < micro)
        slot = jnp.clip(slot_raw, 0, micro - 1)
        first_state = lax.dynamic_index_in_dim(states, slot, 0, keepdims=True)
        source = jnp.where(rank == 0, first_state, incoming[None])
        allowed_slot = lax.dynamic_index_in_dim(allowed, slot, 0, keepdims=True)

        def forward_do_work(stash_in, upstream_in):
            output, kept_parts = layer_forward(source, weight, allowed_slot)
            stash_out = tuple(
                (
                    lax.dynamic_update_index_in_dim(whole_array, new_piece, slot, 0)
                    for whole_array, new_piece in zip(stash_in, kept_parts)
                )
            )
            predicted = jnp.sum(output.astype(jnp.float32) * readout, axis=-1)
            misfit = predicted - lax.dynamic_index_in_dim(targets, slot, 0, keepdims=True)
            cotangent = (misfit[..., None] * readout).astype(jnp.bfloat16)
            upstream_out = lax.dynamic_update_index_in_dim(upstream_in, cotangent, slot, 0)
            return (output[0], stash_out, upstream_out)

        def forward_no_work(stash_in, upstream_in):
            return (zero_rows, stash_in, upstream_in)

        output, stashed, upstream_stash = lax.cond(
            active, forward_do_work, forward_no_work, stashed, upstream_stash
        )
        passed = passed_along(output, "section", 1)
        return (passed, stashed, upstream_stash)

    unused_rows, stashed, upstream_stash = lax.fori_loop(
        0, steps_total, forward_step, (zero_rows, stash_init, upstream_init)
    )
    totals_init = jnp.zeros((micro, buses, width), jnp.bfloat16)

    def backward_step(step, carry):
        incoming, collected = carry
        slot_raw = step - (sections - 1 - rank)
        active = (slot_raw >= 0) & (slot_raw < micro)
        slot = jnp.clip(slot_raw, 0, micro - 1)
        last_grad = lax.dynamic_index_in_dim(upstream_stash, slot, 0, keepdims=True)
        upstream = jnp.where(rank == sections - 1, last_grad, incoming[None])
        allowed_slot = lax.dynamic_index_in_dim(allowed, slot, 0, keepdims=True)

        def backward_do_work(collected_in):
            kept_parts = tuple(
                (
                    lax.dynamic_index_in_dim(whole_array, slot, 0, keepdims=True)
                    for whole_array in stashed
                )
            )
            lower, value_total = layer_backward(upstream, weight, allowed_slot, kept_parts)
            collected_out = lax.dynamic_update_index_in_dim(collected_in, value_total, slot, 0)
            return (lower[0], collected_out)

        def backward_no_work(collected_in):
            return (zero_rows, collected_in)

        lower, collected = lax.cond(active, backward_do_work, backward_no_work, collected)
        passed = passed_along(lower, "section", -1)
        return (passed, collected)

    unused_rows, collected = lax.fori_loop(0, steps_total, backward_step, (zero_rows, totals_init))
    cores = lax.axis_size("core")
    groups = lax.axis_size("dp_hi")
    core = lax.axis_index("core")
    rows_each = width // (groups * cores)
    normed_all = stashed[0].astype(jnp.bfloat16).reshape(micro * buses, groups, cores, rows_each)
    totals_all = collected.reshape(micro * buses, width)

    def partial_grad(which):
        chosen = lax.dynamic_index_in_dim(normed_all, which, 2, keepdims=False)
        return lax.dot_general(
            chosen.reshape(micro * buses, groups * rows_each),
            totals_all,
            (((0,), (0,)), ((), ())),
            preferred_element_type=jnp.float32,
        )

    received = lax.ppermute(partial_grad(1 - core), "core", [(0, 1), (1, 0)])
    half = lax.optimization_barrier(partial_grad(core)) + received
    swapped = lax.all_to_all(half.astype(jnp.bfloat16), "dp_hi", 0, 0, tiled=True)
    summed = jnp.sum(swapped.reshape(groups, rows_each, width).astype(jnp.float32), axis=0)
    return summed[None]


def solution(mesh):
    sections, dp = mesh.devices.shape
    split = Mesh(mesh.devices.reshape(sections, dp // 2, 2), ("section", "dp_hi", "core"))
    rows = ("dp_hi", "core")
    in_specs = (
        P(rows, None, None),
        P(rows, None),
        P(rows, None),
        P(),
        P("section", None, None),
        P(),
    )
    out_specs = P("section", rows, None)
    return jax.shard_map(
        per_device, mesh=split, in_specs=in_specs, out_specs=out_specs, check_vma=False
    )
```

```python
import jax
import jax.numpy as jnp
from jax import lax
from jax.sharding import Mesh, PartitionSpec as P

HEADS = 16
BLOCK = 32


epsilon = 1e-05


def passed_along(block, axis, distance):
    devices = range(lax.axis_size(axis))
    route = [(i - distance, i) for i in devices if i - distance in devices]
    return lax.ppermute(block, axis, route)


def scatter_sum(block, axis):
    count = lax.axis_size(axis)
    me = lax.axis_index(axis)
    pieces = block.reshape(count, block.shape[0] // count, block.shape[1])
    total = lax.dynamic_index_in_dim(pieces, me, 0, keepdims=False)
    for shift in range(1, count):
        sent = lax.dynamic_index_in_dim(pieces, (me + shift) % count, 0, keepdims=False)
        route = [(i, (i + shift) % count) for i in range(count)]
        received = lax.ppermute(sent.astype(jnp.bfloat16), axis, route)
        total = total + received.astype(jnp.float32)
    return total


def allowed_pairs(pattern, outage):
    buses = outage.shape[-1]
    block_count = buses // BLOCK
    block_ids = jnp.arange(block_count, dtype=jnp.int32)
    pair_hits = (pattern[:, 0][None, None, :] == block_ids[:, None, None]) & (
        pattern[:, 1][None, None, :] == block_ids[None, :, None]
    )
    block_table = jnp.max(pair_hits.astype(jnp.float32), axis=2)
    member = ((jnp.arange(buses, dtype=jnp.int32) // BLOCK)[:, None] == block_ids[None, :]).astype(
        jnp.float32
    )
    pair_mask = jnp.dot(
        jnp.dot(member, block_table, precision=lax.Precision.HIGHEST),
        member.T,
        precision=lax.Precision.HIGHEST,
    )
    in_service = outage.astype(jnp.float32)
    self_mask = jnp.eye(buses, dtype=jnp.float32)
    return pair_mask[None] * jnp.maximum(in_service[:, None, :], self_mask[None])


def layer_forward(hidden, weight, allowed):
    num_states, buses, width = hidden.shape
    split_shape = (num_states, buses, HEADS, width // HEADS)
    hidden_f = hidden.astype(jnp.float32)
    centred = hidden_f - jnp.mean(hidden_f, axis=-1, keepdims=True)
    inverse_std = lax.rsqrt(jnp.mean(centred * centred, axis=-1, keepdims=True) + epsilon)
    scaled = centred * inverse_std
    normed = scaled.astype(jnp.bfloat16)
    values_b = (
        jnp.dot(normed.reshape(-1, width), weight, preferred_element_type=jnp.float32)
        .astype(jnp.bfloat16)
        .reshape(split_shape)
    )
    features = (jax.nn.elu(values_b.astype(jnp.float32)) + 1.0).astype(jnp.bfloat16)
    kernel = (
        jnp.einsum("nihc,njhc->nhij", features, features, preferred_element_type=jnp.float32)
        * allowed[:, None]
    )
    totals = jnp.sum(kernel, axis=-1, keepdims=True)
    attention = kernel / totals
    attention_b = attention.astype(jnp.bfloat16)
    gathered = jnp.einsum(
        "nhij,njhc->nihc", attention_b, values_b, preferred_element_type=jnp.float32
    )
    output = (hidden_f + gathered.reshape(num_states, buses, width)).astype(jnp.bfloat16)
    return (output, (scaled, inverse_std, values_b, attention, totals))


def layer_backward(upstream, weight, allowed, kept_parts):
    scaled, inverse_std, values_b, attention, totals = kept_parts
    num_states, buses, width = upstream.shape
    grad_f = upstream.astype(jnp.float32)
    grad_heads = upstream.reshape(values_b.shape)
    values_f = values_b.astype(jnp.float32)
    features = (jax.nn.elu(values_f) + 1.0).astype(jnp.bfloat16)
    attention_b = attention.astype(jnp.bfloat16)
    value_grad = jnp.einsum(
        "nhij,nihc->njhc", attention_b, grad_heads, preferred_element_type=jnp.float32
    )
    attention_grad = jnp.einsum(
        "nihc,njhc->nhij", grad_heads, values_b, preferred_element_type=jnp.float32
    )
    row_terms = jnp.sum(attention_grad * attention, axis=-1, keepdims=True)
    kernel_grad = ((attention_grad - row_terms) / totals * allowed[:, None]).astype(jnp.bfloat16)
    feature_grad = jnp.einsum(
        "nhij,njhc->nihc", kernel_grad, features, preferred_element_type=jnp.float32
    )
    feature_grad = feature_grad + jnp.einsum(
        "nhji,njhc->nihc", kernel_grad, features, preferred_element_type=jnp.float32
    )
    slope = jnp.where(values_f > 0.0, 1.0, jnp.exp(jnp.minimum(values_f, 0.0)))
    value_total = (
        (value_grad + feature_grad * slope).astype(jnp.bfloat16).reshape(num_states, buses, width)
    )
    normed_grad = lax.dot_general(
        value_total.reshape(-1, width),
        weight,
        (((1,), (1,)), ((), ())),
        preferred_element_type=jnp.float32,
    ).reshape(num_states, buses, width)
    mean_grad = jnp.mean(normed_grad, axis=-1, keepdims=True)
    mean_cross = jnp.mean(normed_grad * scaled, axis=-1, keepdims=True)
    lower = (grad_f + inverse_std * (normed_grad - mean_grad - scaled * mean_cross)).astype(
        jnp.bfloat16
    )
    return (lower, value_total)


def per_device(states, outage, targets, pattern, weights, readout):
    sections = lax.axis_size("section")
    rank = lax.axis_index("section")
    micro, buses, width = states.shape
    weight = weights[0]
    allowed = allowed_pairs(pattern, outage)
    head_size = width // HEADS
    steps_total = sections + micro - 1
    zero_rows = jnp.zeros((buses, width), jnp.bfloat16)
    stash_init = (
        jnp.zeros((micro, buses, width), jnp.float32),
        jnp.zeros((micro, buses, 1), jnp.float32),
        jnp.zeros((micro, buses, HEADS, head_size), jnp.bfloat16),
        jnp.zeros((micro, HEADS, buses, buses), jnp.float32),
        jnp.zeros((micro, HEADS, buses, 1), jnp.float32),
    )
    upstream_init = jnp.zeros((micro, buses, width), jnp.bfloat16)

    def forward_step(step, carry):
        incoming, stashed, upstream_stash = carry
        slot_raw = step - rank
        active = (slot_raw >= 0) & (slot_raw < micro)
        slot = jnp.clip(slot_raw, 0, micro - 1)
        first_state = lax.dynamic_index_in_dim(states, slot, 0, keepdims=True)
        source = jnp.where(rank == 0, first_state, incoming[None])
        allowed_slot = lax.dynamic_index_in_dim(allowed, slot, 0, keepdims=True)

        def forward_do_work(stash_in, upstream_in):
            output, kept_parts = layer_forward(source, weight, allowed_slot)
            stash_out = tuple(
                (
                    lax.dynamic_update_index_in_dim(whole_array, new_piece, slot, 0)
                    for whole_array, new_piece in zip(stash_in, kept_parts)
                )
            )
            predicted = jnp.sum(output.astype(jnp.float32) * readout, axis=-1)
            misfit = predicted - lax.dynamic_index_in_dim(targets, slot, 0, keepdims=True)
            cotangent = (misfit[..., None] * readout).astype(jnp.bfloat16)
            upstream_out = lax.dynamic_update_index_in_dim(upstream_in, cotangent, slot, 0)
            return (output[0], stash_out, upstream_out)

        def forward_no_work(stash_in, upstream_in):
            return (zero_rows, stash_in, upstream_in)

        output, stashed, upstream_stash = lax.cond(
            active, forward_do_work, forward_no_work, stashed, upstream_stash
        )
        passed = passed_along(output, "section", 1)
        return (passed, stashed, upstream_stash)

    unused_rows, stashed, upstream_stash = lax.fori_loop(
        0, steps_total, forward_step, (zero_rows, stash_init, upstream_init)
    )
    totals_init = jnp.zeros((micro, buses, width), jnp.bfloat16)

    def backward_step(step, carry):
        incoming, collected = carry
        slot_raw = step - (sections - 1 - rank)
        active = (slot_raw >= 0) & (slot_raw < micro)
        slot = jnp.clip(slot_raw, 0, micro - 1)
        last_grad = lax.dynamic_index_in_dim(upstream_stash, slot, 0, keepdims=True)
        upstream = jnp.where(rank == sections - 1, last_grad, incoming[None])
        allowed_slot = lax.dynamic_index_in_dim(allowed, slot, 0, keepdims=True)

        def backward_do_work(collected_in):
            kept_parts = tuple(
                (
                    lax.dynamic_index_in_dim(whole_array, slot, 0, keepdims=True)
                    for whole_array in stashed
                )
            )
            lower, value_total = layer_backward(upstream, weight, allowed_slot, kept_parts)
            collected_out = lax.dynamic_update_index_in_dim(collected_in, value_total, slot, 0)
            return (lower[0], collected_out)

        def backward_no_work(collected_in):
            return (zero_rows, collected_in)

        lower, collected = lax.cond(active, backward_do_work, backward_no_work, collected)
        passed = passed_along(lower, "section", -1)
        return (passed, collected)

    unused_rows, collected = lax.fori_loop(0, steps_total, backward_step, (zero_rows, totals_init))
    cores = lax.axis_size("core")
    groups = lax.axis_size("dp_hi")
    core = lax.axis_index("core")
    rows_each = width // (groups * cores)
    normed_all = stashed[0].astype(jnp.bfloat16).reshape(micro * buses, groups, cores, rows_each)
    totals_all = collected.reshape(micro * buses, width)

    def partial_grad(which):
        chosen = lax.dynamic_index_in_dim(normed_all, which, 2, keepdims=False)
        return lax.dot_general(
            chosen.reshape(micro * buses, groups * rows_each),
            totals_all,
            (((0,), (0,)), ((), ())),
            preferred_element_type=jnp.float32,
        )

    received = lax.ppermute(partial_grad(1 - core), "core", [(0, 1), (1, 0)])
    half = lax.optimization_barrier(partial_grad(core)) + received
    summed = scatter_sum(half, "dp_hi")
    return summed[None]


def solution(mesh):
    sections, dp = mesh.devices.shape
    split = Mesh(mesh.devices.reshape(sections, dp // 2, 2), ("section", "dp_hi", "core"))
    rows = ("dp_hi", "core")
    in_specs = (
        P(rows, None, None),
        P(rows, None),
        P(rows, None),
        P(),
        P("section", None, None),
        P(),
    )
    out_specs = P("section", rows, None)
    return jax.shard_map(
        per_device, mesh=split, in_specs=in_specs, out_specs=out_specs, check_vma=False
    )
```

```python
import jax
import jax.numpy as jnp
from jax import lax
from jax.sharding import Mesh, PartitionSpec as P

HEADS = 16
BLOCK = 32


epsilon = 1e-05


def passed_along(block, axis, distance, senders):
    if not senders:
        return jnp.zeros_like(block)
    return lax.ppermute(block, axis, [(i, i + distance) for i in senders])


def allowed_pairs(pattern, outage):
    buses = outage.shape[-1]
    block_count = buses // BLOCK
    block_ids = jnp.arange(block_count, dtype=jnp.int32)
    pair_hits = (pattern[:, 0][None, None, :] == block_ids[:, None, None]) & (
        pattern[:, 1][None, None, :] == block_ids[None, :, None]
    )
    block_table = jnp.max(pair_hits.astype(jnp.float32), axis=2)
    member = ((jnp.arange(buses, dtype=jnp.int32) // BLOCK)[:, None] == block_ids[None, :]).astype(
        jnp.float32
    )
    pair_mask = jnp.dot(
        jnp.dot(member, block_table, precision=lax.Precision.HIGHEST),
        member.T,
        precision=lax.Precision.HIGHEST,
    )
    in_service = outage.astype(jnp.float32)
    self_mask = jnp.eye(buses, dtype=jnp.float32)
    return pair_mask[None] * jnp.maximum(in_service[:, None, :], self_mask[None])


def layer_forward(hidden, weight, allowed):
    num_states, buses, width = hidden.shape
    split_shape = (num_states, buses, HEADS, width // HEADS)
    hidden_f = hidden.astype(jnp.float32)
    centred = hidden_f - jnp.mean(hidden_f, axis=-1, keepdims=True)
    inverse_std = lax.rsqrt(jnp.mean(centred * centred, axis=-1, keepdims=True) + epsilon)
    scaled = centred * inverse_std
    normed = scaled.astype(jnp.bfloat16)
    values_b = (
        jnp.dot(normed.reshape(-1, width), weight, preferred_element_type=jnp.float32)
        .astype(jnp.bfloat16)
        .reshape(split_shape)
    )
    features = (jax.nn.elu(values_b.astype(jnp.float32)) + 1.0).astype(jnp.bfloat16)
    kernel = (
        jnp.einsum("nihc,njhc->nhij", features, features, preferred_element_type=jnp.float32)
        * allowed[:, None]
    )
    totals = jnp.sum(kernel, axis=-1, keepdims=True)
    attention = kernel / totals
    attention_b = attention.astype(jnp.bfloat16)
    gathered = jnp.einsum(
        "nhij,njhc->nihc", attention_b, values_b, preferred_element_type=jnp.float32
    )
    output = (hidden_f + gathered.reshape(num_states, buses, width)).astype(jnp.bfloat16)
    return (output, (scaled, inverse_std, values_b, attention, totals))


def layer_backward(upstream, weight, allowed, kept_parts):
    scaled, inverse_std, values_b, attention, totals = kept_parts
    num_states, buses, width = upstream.shape
    grad_f = upstream.astype(jnp.float32)
    grad_heads = upstream.reshape(values_b.shape)
    values_f = values_b.astype(jnp.float32)
    features = (jax.nn.elu(values_f) + 1.0).astype(jnp.bfloat16)
    attention_b = attention.astype(jnp.bfloat16)
    value_grad = jnp.einsum(
        "nhij,nihc->njhc", attention_b, grad_heads, preferred_element_type=jnp.float32
    )
    attention_grad = jnp.einsum(
        "nihc,njhc->nhij", grad_heads, values_b, preferred_element_type=jnp.float32
    )
    row_terms = jnp.sum(attention_grad * attention, axis=-1, keepdims=True)
    kernel_grad = ((attention_grad - row_terms) / totals * allowed[:, None]).astype(jnp.bfloat16)
    feature_grad = jnp.einsum(
        "nhij,njhc->nihc", kernel_grad, features, preferred_element_type=jnp.float32
    )
    feature_grad = feature_grad + jnp.einsum(
        "nhji,njhc->nihc", kernel_grad, features, preferred_element_type=jnp.float32
    )
    slope = jnp.where(values_f > 0.0, 1.0, jnp.exp(jnp.minimum(values_f, 0.0)))
    value_total = (
        (value_grad + feature_grad * slope).astype(jnp.bfloat16).reshape(num_states, buses, width)
    )
    normed_grad = lax.dot_general(
        value_total.reshape(-1, width),
        weight,
        (((1,), (1,)), ((), ())),
        preferred_element_type=jnp.float32,
    ).reshape(num_states, buses, width)
    mean_grad = jnp.mean(normed_grad, axis=-1, keepdims=True)
    mean_cross = jnp.mean(normed_grad * scaled, axis=-1, keepdims=True)
    lower = (grad_f + inverse_std * (normed_grad - mean_grad - scaled * mean_cross)).astype(
        jnp.bfloat16
    )
    return (lower, value_total)


def per_device(states, outage, targets, pattern, weights, readout):
    sections = lax.axis_size("section")
    rank = lax.axis_index("section")
    micro, buses, width = states.shape
    weight = weights[0]
    allowed = allowed_pairs(pattern, outage)
    head_size = width // HEADS
    steps_total = sections + micro - 1
    zero_rows = jnp.zeros((buses, width), jnp.bfloat16)
    stash_init = (
        jnp.zeros((micro, buses, width), jnp.float32),
        jnp.zeros((micro, buses, 1), jnp.float32),
        jnp.zeros((micro, buses, HEADS, head_size), jnp.bfloat16),
        jnp.zeros((micro, HEADS, buses, buses), jnp.float32),
        jnp.zeros((micro, HEADS, buses, 1), jnp.float32),
    )
    upstream_init = jnp.zeros((micro, buses, width), jnp.bfloat16)

    def forward_step(step, carry):
        incoming, stashed, upstream_stash = carry
        slot_raw = step - rank
        active = (slot_raw >= 0) & (slot_raw < micro)
        slot = jnp.clip(slot_raw, 0, micro - 1)
        first_state = lax.dynamic_index_in_dim(states, slot, 0, keepdims=True)
        source = jnp.where(rank == 0, first_state, incoming[None])
        allowed_slot = lax.dynamic_index_in_dim(allowed, slot, 0, keepdims=True)

        def forward_do_work(stash_in, upstream_in):
            output, kept_parts = layer_forward(source, weight, allowed_slot)
            stash_out = tuple(
                (
                    lax.dynamic_update_index_in_dim(whole_array, new_piece, slot, 0)
                    for whole_array, new_piece in zip(stash_in, kept_parts)
                )
            )
            predicted = jnp.sum(output.astype(jnp.float32) * readout, axis=-1)
            misfit = predicted - lax.dynamic_index_in_dim(targets, slot, 0, keepdims=True)
            cotangent = (misfit[..., None] * readout).astype(jnp.bfloat16)
            upstream_out = lax.dynamic_update_index_in_dim(upstream_in, cotangent, slot, 0)
            return (output[0], stash_out, upstream_out)

        def forward_no_work(stash_in, upstream_in):
            return (zero_rows, stash_in, upstream_in)

        output, stashed, upstream_stash = lax.cond(
            active, forward_do_work, forward_no_work, stashed, upstream_stash
        )
        senders = [r for r in range(sections - 1) if 0 <= step - r < micro]
        passed = passed_along(output, "section", 1, senders)
        return (passed, stashed, upstream_stash)

    carry = (zero_rows, stash_init, upstream_init)
    for step in range(steps_total):
        carry = forward_step(step, carry)
    unused_rows, stashed, upstream_stash = carry
    totals_init = jnp.zeros((micro, buses, width), jnp.bfloat16)

    def backward_step(step, carry):
        incoming, collected = carry
        slot_raw = step - (sections - 1 - rank)
        active = (slot_raw >= 0) & (slot_raw < micro)
        slot = jnp.clip(slot_raw, 0, micro - 1)
        last_grad = lax.dynamic_index_in_dim(upstream_stash, slot, 0, keepdims=True)
        upstream = jnp.where(rank == sections - 1, last_grad, incoming[None])
        allowed_slot = lax.dynamic_index_in_dim(allowed, slot, 0, keepdims=True)

        def backward_do_work(collected_in):
            kept_parts = tuple(
                (
                    lax.dynamic_index_in_dim(whole_array, slot, 0, keepdims=True)
                    for whole_array in stashed
                )
            )
            lower, value_total = layer_backward(upstream, weight, allowed_slot, kept_parts)
            collected_out = lax.dynamic_update_index_in_dim(collected_in, value_total, slot, 0)
            return (lower[0], collected_out)

        def backward_no_work(collected_in):
            return (zero_rows, collected_in)

        lower, collected = lax.cond(active, backward_do_work, backward_no_work, collected)
        senders = [r for r in range(1, sections) if 0 <= step - (sections - 1 - r) < micro]
        passed = passed_along(lower, "section", -1, senders)
        return (passed, collected)

    carry = (zero_rows, totals_init)
    for step in range(steps_total):
        carry = backward_step(step, carry)
    unused_rows, collected = carry
    cores = lax.axis_size("core")
    groups = lax.axis_size("dp_hi")
    core = lax.axis_index("core")
    rows_each = width // (groups * cores)
    normed_all = stashed[0].astype(jnp.bfloat16).reshape(micro * buses, groups, cores, rows_each)
    totals_all = collected.reshape(micro * buses, width)

    def partial_grad(which):
        chosen = lax.dynamic_index_in_dim(normed_all, which, 2, keepdims=False)
        return lax.dot_general(
            chosen.reshape(micro * buses, groups * rows_each),
            totals_all,
            (((0,), (0,)), ((), ())),
            preferred_element_type=jnp.float32,
        )

    received = lax.ppermute(partial_grad(1 - core), "core", [(0, 1), (1, 0)])
    half = lax.optimization_barrier(partial_grad(core)) + received
    swapped = lax.all_to_all(half.astype(jnp.bfloat16), "dp_hi", 0, 0, tiled=True)
    summed = jnp.sum(swapped.reshape(groups, rows_each, width).astype(jnp.float32), axis=0)
    return summed[None]


def solution(mesh):
    sections, dp = mesh.devices.shape
    split = Mesh(mesh.devices.reshape(sections, dp // 2, 2), ("section", "dp_hi", "core"))
    rows = ("dp_hi", "core")
    in_specs = (
        P(rows, None, None),
        P(rows, None),
        P(rows, None),
        P(),
        P("section", None, None),
        P(),
    )
    out_specs = P("section", rows, None)
    return jax.shard_map(
        per_device, mesh=split, in_specs=in_specs, out_specs=out_specs, check_vma=False
    )
```

```python
import jax
import jax.numpy as jnp
from jax import lax
from jax.experimental import pallas as pl
from jax.experimental.pallas import tpu as pltpu
from jax.sharding import Mesh, PartitionSpec as P

HEADS = 16
BLOCK = 32


epsilon = 1e-05


def passed_along(block, axis, distance):
    devices = range(lax.axis_size(axis))
    route = [(i - distance, i) for i in devices if i - distance in devices]
    return lax.ppermute(block, axis, route)


def allowed_pairs(pattern, outage):
    buses = outage.shape[-1]
    block_count = buses // BLOCK
    block_ids = jnp.arange(block_count, dtype=jnp.int32)
    pair_hits = (pattern[:, 0][None, None, :] == block_ids[:, None, None]) & (
        pattern[:, 1][None, None, :] == block_ids[None, :, None]
    )
    block_table = jnp.max(pair_hits.astype(jnp.float32), axis=2)
    member = ((jnp.arange(buses, dtype=jnp.int32) // BLOCK)[:, None] == block_ids[None, :]).astype(
        jnp.float32
    )
    pair_mask = jnp.dot(
        jnp.dot(member, block_table, precision=lax.Precision.HIGHEST),
        member.T,
        precision=lax.Precision.HIGHEST,
    )
    in_service = outage.astype(jnp.float32)
    self_mask = jnp.eye(buses, dtype=jnp.float32)
    return pair_mask[None] * jnp.maximum(in_service[:, None, :], self_mask[None])


def feature_map(values):
    return jnp.where(values > 0.0, values + 1.0, jnp.exp(jnp.minimum(values, 0.0)))


def attention_forward_kernel(values_ref, hidden_ref, allowed_ref, out_ref, att_ref, tot_ref):
    allowed = allowed_ref[...]
    size = values_ref.shape[1] // HEADS

    def head(h, carry):
        cols = pl.ds(pl.multiple_of(h * size, size), size)
        values = values_ref[:, cols]
        features = feature_map(values.astype(jnp.float32)).astype(jnp.bfloat16)
        kernel = (
            lax.dot_general(
                features, features, (((1,), (1,)), ((), ())), preferred_element_type=jnp.float32
            )
            * allowed
        )
        totals = jnp.sum(kernel, axis=-1, keepdims=True)
        attention = kernel / totals
        att_ref[h] = attention
        tot_ref[h] = totals
        gathered = jnp.dot(
            attention.astype(jnp.bfloat16), values, preferred_element_type=jnp.float32
        )
        out_ref[:, cols] = (hidden_ref[:, cols].astype(jnp.float32) + gathered).astype(
            jnp.bfloat16
        )
        return carry

    lax.fori_loop(0, HEADS, head, 0)


def attention_backward_kernel(up_ref, values_ref, att_ref, tot_ref, allowed_ref, out_ref):
    allowed = allowed_ref[...]
    size = values_ref.shape[1] // HEADS

    def head(h, carry):
        cols = pl.ds(pl.multiple_of(h * size, size), size)
        grads = up_ref[:, cols]
        values = values_ref[:, cols]
        values_f = values.astype(jnp.float32)
        features = feature_map(values_f).astype(jnp.bfloat16)
        attention = att_ref[h]
        value_grad = jnp.dot(
            attention.T.astype(jnp.bfloat16), grads, preferred_element_type=jnp.float32
        )
        attention_grad = lax.dot_general(
            grads, values, (((1,), (1,)), ((), ())), preferred_element_type=jnp.float32
        )
        row_terms = jnp.sum(attention_grad * attention, axis=-1, keepdims=True)
        kernel_grad = (attention_grad - row_terms) / tot_ref[h] * allowed
        feature_grad = jnp.dot(
            kernel_grad.astype(jnp.bfloat16), features, preferred_element_type=jnp.float32
        ) + jnp.dot(
            kernel_grad.T.astype(jnp.bfloat16), features, preferred_element_type=jnp.float32
        )
        slope = jnp.where(values_f > 0.0, 1.0, jnp.exp(jnp.minimum(values_f, 0.0)))
        out_ref[:, cols] = (value_grad + feature_grad * slope).astype(jnp.bfloat16)
        return carry

    lax.fori_loop(0, HEADS, head, 0)


def attention_forward(values, hidden, allowed):
    buses, width = values.shape
    return pl.pallas_call(
        attention_forward_kernel,
        out_shape=(
            jax.ShapeDtypeStruct((buses, width), jnp.bfloat16),
            jax.ShapeDtypeStruct((HEADS, buses, buses), jnp.float32),
            jax.ShapeDtypeStruct((HEADS, buses, 1), jnp.float32),
        ),
        in_specs=[pl.BlockSpec(memory_space=pltpu.VMEM)] * 3,
        out_specs=[pl.BlockSpec(memory_space=pltpu.VMEM)] * 3,
    )(values, hidden, allowed)


def attention_backward(upstream, values, attention, totals, allowed):
    buses, width = values.shape
    return pl.pallas_call(
        attention_backward_kernel,
        out_shape=jax.ShapeDtypeStruct((buses, width), jnp.bfloat16),
        in_specs=[pl.BlockSpec(memory_space=pltpu.VMEM)] * 5,
        out_specs=pl.BlockSpec(memory_space=pltpu.VMEM),
    )(upstream, values, attention, totals, allowed)


def layer_forward(hidden, weight, allowed):
    num_states, buses, width = hidden.shape
    split_shape = (num_states, buses, HEADS, width // HEADS)
    hidden_f = hidden.astype(jnp.float32)
    centred = hidden_f - jnp.mean(hidden_f, axis=-1, keepdims=True)
    inverse_std = lax.rsqrt(jnp.mean(centred * centred, axis=-1, keepdims=True) + epsilon)
    scaled = centred * inverse_std
    normed = scaled.astype(jnp.bfloat16)
    values_b = jnp.dot(
        normed.reshape(-1, width), weight, preferred_element_type=jnp.float32
    ).astype(jnp.bfloat16)
    output, attention, totals = attention_forward(values_b, hidden[0], allowed[0])
    return (
        output[None],
        (scaled, inverse_std, values_b.reshape(split_shape), attention[None], totals[None]),
    )


def layer_backward(upstream, weight, allowed, kept_parts):
    scaled, inverse_std, values_b, attention, totals = kept_parts
    num_states, buses, width = upstream.shape
    grad_f = upstream.astype(jnp.float32)
    value_total = attention_backward(
        upstream[0], values_b.reshape(buses, width), attention[0], totals[0], allowed[0]
    )[None]
    normed_grad = lax.dot_general(
        value_total.reshape(-1, width),
        weight,
        (((1,), (1,)), ((), ())),
        preferred_element_type=jnp.float32,
    ).reshape(num_states, buses, width)
    mean_grad = jnp.mean(normed_grad, axis=-1, keepdims=True)
    mean_cross = jnp.mean(normed_grad * scaled, axis=-1, keepdims=True)
    lower = (grad_f + inverse_std * (normed_grad - mean_grad - scaled * mean_cross)).astype(
        jnp.bfloat16
    )
    return (lower, value_total)


def per_device(states, outage, targets, pattern, weights, readout):
    sections = lax.axis_size("section")
    rank = lax.axis_index("section")
    micro, buses, width = states.shape
    weight = weights[0]
    allowed = allowed_pairs(pattern, outage)
    head_size = width // HEADS
    steps_total = sections + micro - 1
    zero_rows = jnp.zeros((buses, width), jnp.bfloat16)
    stash_init = (
        jnp.zeros((micro, buses, width), jnp.float32),
        jnp.zeros((micro, buses, 1), jnp.float32),
        jnp.zeros((micro, buses, HEADS, head_size), jnp.bfloat16),
        jnp.zeros((micro, HEADS, buses, buses), jnp.float32),
        jnp.zeros((micro, HEADS, buses, 1), jnp.float32),
    )
    upstream_init = jnp.zeros((micro, buses, width), jnp.bfloat16)

    def forward_step(step, carry):
        incoming, stashed, upstream_stash = carry
        slot_raw = step - rank
        active = (slot_raw >= 0) & (slot_raw < micro)
        slot = jnp.clip(slot_raw, 0, micro - 1)
        first_state = lax.dynamic_index_in_dim(states, slot, 0, keepdims=True)
        source = jnp.where(rank == 0, first_state, incoming[None])
        allowed_slot = lax.dynamic_index_in_dim(allowed, slot, 0, keepdims=True)

        def forward_do_work(stash_in, upstream_in):
            output, kept_parts = layer_forward(source, weight, allowed_slot)
            stash_out = tuple(
                (
                    lax.dynamic_update_index_in_dim(whole_array, new_piece, slot, 0)
                    for whole_array, new_piece in zip(stash_in, kept_parts)
                )
            )
            predicted = jnp.sum(output.astype(jnp.float32) * readout, axis=-1)
            misfit = predicted - lax.dynamic_index_in_dim(targets, slot, 0, keepdims=True)
            cotangent = (misfit[..., None] * readout).astype(jnp.bfloat16)
            upstream_out = lax.dynamic_update_index_in_dim(upstream_in, cotangent, slot, 0)
            return (output[0], stash_out, upstream_out)

        def forward_no_work(stash_in, upstream_in):
            return (zero_rows, stash_in, upstream_in)

        output, stashed, upstream_stash = lax.cond(
            active, forward_do_work, forward_no_work, stashed, upstream_stash
        )
        passed = passed_along(output, "section", 1)
        return (passed, stashed, upstream_stash)

    unused_rows, stashed, upstream_stash = lax.fori_loop(
        0, steps_total, forward_step, (zero_rows, stash_init, upstream_init)
    )
    totals_init = jnp.zeros((micro, buses, width), jnp.bfloat16)

    def backward_step(step, carry):
        incoming, collected = carry
        slot_raw = step - (sections - 1 - rank)
        active = (slot_raw >= 0) & (slot_raw < micro)
        slot = jnp.clip(slot_raw, 0, micro - 1)
        last_grad = lax.dynamic_index_in_dim(upstream_stash, slot, 0, keepdims=True)
        upstream = jnp.where(rank == sections - 1, last_grad, incoming[None])
        allowed_slot = lax.dynamic_index_in_dim(allowed, slot, 0, keepdims=True)

        def backward_do_work(collected_in):
            kept_parts = tuple(
                (
                    lax.dynamic_index_in_dim(whole_array, slot, 0, keepdims=True)
                    for whole_array in stashed
                )
            )
            lower, value_total = layer_backward(upstream, weight, allowed_slot, kept_parts)
            collected_out = lax.dynamic_update_index_in_dim(collected_in, value_total, slot, 0)
            return (lower[0], collected_out)

        def backward_no_work(collected_in):
            return (zero_rows, collected_in)

        lower, collected = lax.cond(active, backward_do_work, backward_no_work, collected)
        passed = passed_along(lower, "section", -1)
        return (passed, collected)

    unused_rows, collected = lax.fori_loop(0, steps_total, backward_step, (zero_rows, totals_init))
    cores = lax.axis_size("core")
    groups = lax.axis_size("dp_hi")
    core = lax.axis_index("core")
    rows_each = width // (groups * cores)
    normed_all = stashed[0].astype(jnp.bfloat16).reshape(micro * buses, groups, cores, rows_each)
    totals_all = collected.reshape(micro * buses, width)

    def partial_grad(which):
        chosen = lax.dynamic_index_in_dim(normed_all, which, 2, keepdims=False)
        return lax.dot_general(
            chosen.reshape(micro * buses, groups * rows_each),
            totals_all,
            (((0,), (0,)), ((), ())),
            preferred_element_type=jnp.float32,
        )

    received = lax.ppermute(partial_grad(1 - core), "core", [(0, 1), (1, 0)])
    half = lax.optimization_barrier(partial_grad(core)) + received
    swapped = lax.all_to_all(half.astype(jnp.bfloat16), "dp_hi", 0, 0, tiled=True)
    summed = jnp.sum(swapped.reshape(groups, rows_each, width).astype(jnp.float32), axis=0)
    return summed[None]


def solution(mesh):
    sections, dp = mesh.devices.shape
    split = Mesh(mesh.devices.reshape(sections, dp // 2, 2), ("section", "dp_hi", "core"))
    rows = ("dp_hi", "core")
    in_specs = (
        P(rows, None, None),
        P(rows, None),
        P(rows, None),
        P(),
        P("section", None, None),
        P(),
    )
    out_specs = P("section", rows, None)
    return jax.shard_map(
        per_device, mesh=split, in_specs=in_specs, out_specs=out_specs, check_vma=False
    )
```

```python
import functools

import jax
import jax.numpy as jnp
from jax import lax
from jax.sharding import Mesh, PartitionSpec as P

HEADS = 16
BLOCK = 32


epsilon = 1e-05


def passed_along(block, axis, distance, senders):
    return lax.ppermute(block, axis, [(i, i + distance) for i in senders])


def phases(sections, micro):
    middle = sections // 2
    bounds = [0, middle - 1, middle - 1 + micro, sections + micro - 1]
    return [(lo, hi) for lo, hi in zip(bounds[:-1], bounds[1:]) if hi > lo]


def allowed_pairs(pattern, outage):
    buses = outage.shape[-1]
    block_count = buses // BLOCK
    block_ids = jnp.arange(block_count, dtype=jnp.int32)
    pair_hits = (pattern[:, 0][None, None, :] == block_ids[:, None, None]) & (
        pattern[:, 1][None, None, :] == block_ids[None, :, None]
    )
    block_table = jnp.max(pair_hits.astype(jnp.float32), axis=2)
    member = ((jnp.arange(buses, dtype=jnp.int32) // BLOCK)[:, None] == block_ids[None, :]).astype(
        jnp.float32
    )
    pair_mask = jnp.dot(
        jnp.dot(member, block_table, precision=lax.Precision.HIGHEST),
        member.T,
        precision=lax.Precision.HIGHEST,
    )
    in_service = outage.astype(jnp.float32)
    self_mask = jnp.eye(buses, dtype=jnp.float32)
    return pair_mask[None] * jnp.maximum(in_service[:, None, :], self_mask[None])


def layer_forward(hidden, weight, allowed):
    num_states, buses, width = hidden.shape
    split_shape = (num_states, buses, HEADS, width // HEADS)
    hidden_f = hidden.astype(jnp.float32)
    centred = hidden_f - jnp.mean(hidden_f, axis=-1, keepdims=True)
    inverse_std = lax.rsqrt(jnp.mean(centred * centred, axis=-1, keepdims=True) + epsilon)
    scaled = centred * inverse_std
    normed = scaled.astype(jnp.bfloat16)
    values_b = (
        jnp.dot(normed.reshape(-1, width), weight, preferred_element_type=jnp.float32)
        .astype(jnp.bfloat16)
        .reshape(split_shape)
    )
    features = (jax.nn.elu(values_b.astype(jnp.float32)) + 1.0).astype(jnp.bfloat16)
    kernel = (
        jnp.einsum("nihc,njhc->nhij", features, features, preferred_element_type=jnp.float32)
        * allowed[:, None]
    )
    totals = jnp.sum(kernel, axis=-1, keepdims=True)
    attention = kernel / totals
    attention_b = attention.astype(jnp.bfloat16)
    gathered = jnp.einsum(
        "nhij,njhc->nihc", attention_b, values_b, preferred_element_type=jnp.float32
    )
    output = (hidden_f + gathered.reshape(num_states, buses, width)).astype(jnp.bfloat16)
    return (output, (scaled, inverse_std, values_b, attention, totals))


def layer_backward(upstream, weight, allowed, kept_parts):
    scaled, inverse_std, values_b, attention, totals = kept_parts
    num_states, buses, width = upstream.shape
    grad_f = upstream.astype(jnp.float32)
    grad_heads = upstream.reshape(values_b.shape)
    values_f = values_b.astype(jnp.float32)
    features = (jax.nn.elu(values_f) + 1.0).astype(jnp.bfloat16)
    attention_b = attention.astype(jnp.bfloat16)
    value_grad = jnp.einsum(
        "nhij,nihc->njhc", attention_b, grad_heads, preferred_element_type=jnp.float32
    )
    attention_grad = jnp.einsum(
        "nihc,njhc->nhij", grad_heads, values_b, preferred_element_type=jnp.float32
    )
    row_terms = jnp.sum(attention_grad * attention, axis=-1, keepdims=True)
    kernel_grad = ((attention_grad - row_terms) / totals * allowed[:, None]).astype(jnp.bfloat16)
    feature_grad = jnp.einsum(
        "nhij,njhc->nihc", kernel_grad, features, preferred_element_type=jnp.float32
    )
    feature_grad = feature_grad + jnp.einsum(
        "nhji,njhc->nihc", kernel_grad, features, preferred_element_type=jnp.float32
    )
    slope = jnp.where(values_f > 0.0, 1.0, jnp.exp(jnp.minimum(values_f, 0.0)))
    value_total = (
        (value_grad + feature_grad * slope).astype(jnp.bfloat16).reshape(num_states, buses, width)
    )
    normed_grad = lax.dot_general(
        value_total.reshape(-1, width),
        weight,
        (((1,), (1,)), ((), ())),
        preferred_element_type=jnp.float32,
    ).reshape(num_states, buses, width)
    mean_grad = jnp.mean(normed_grad, axis=-1, keepdims=True)
    mean_cross = jnp.mean(normed_grad * scaled, axis=-1, keepdims=True)
    lower = (grad_f + inverse_std * (normed_grad - mean_grad - scaled * mean_cross)).astype(
        jnp.bfloat16
    )
    return (lower, value_total)


def per_device(states, outage, targets, pattern, weights, readout):
    sections = lax.axis_size("section")
    rank = lax.axis_index("section")
    micro, buses, width = states.shape
    weight = weights[0]
    allowed = allowed_pairs(pattern, outage)
    head_size = width // HEADS
    steps_total = sections + micro - 1
    zero_rows = jnp.zeros((buses, width), jnp.bfloat16)
    stash_init = (
        jnp.zeros((micro, buses, width), jnp.float32),
        jnp.zeros((micro, buses, 1), jnp.float32),
        jnp.zeros((micro, buses, HEADS, head_size), jnp.bfloat16),
        jnp.zeros((micro, HEADS, buses, buses), jnp.float32),
        jnp.zeros((micro, HEADS, buses, 1), jnp.float32),
    )
    upstream_init = jnp.zeros((micro, buses, width), jnp.bfloat16)

    def forward_step(senders, step, carry):
        incoming, stashed, upstream_stash = carry
        slot_raw = step - rank
        active = (slot_raw >= 0) & (slot_raw < micro)
        slot = jnp.clip(slot_raw, 0, micro - 1)
        first_state = lax.dynamic_index_in_dim(states, slot, 0, keepdims=True)
        source = jnp.where(rank == 0, first_state, incoming[None])
        allowed_slot = lax.dynamic_index_in_dim(allowed, slot, 0, keepdims=True)

        def forward_do_work(stash_in, upstream_in):
            output, kept_parts = layer_forward(source, weight, allowed_slot)
            stash_out = tuple(
                (
                    lax.dynamic_update_index_in_dim(whole_array, new_piece, slot, 0)
                    for whole_array, new_piece in zip(stash_in, kept_parts)
                )
            )
            predicted = jnp.sum(output.astype(jnp.float32) * readout, axis=-1)
            misfit = predicted - lax.dynamic_index_in_dim(targets, slot, 0, keepdims=True)
            cotangent = (misfit[..., None] * readout).astype(jnp.bfloat16)
            upstream_out = lax.dynamic_update_index_in_dim(upstream_in, cotangent, slot, 0)
            return (output[0], stash_out, upstream_out)

        def forward_no_work(stash_in, upstream_in):
            return (zero_rows, stash_in, upstream_in)

        output, stashed, upstream_stash = lax.cond(
            active, forward_do_work, forward_no_work, stashed, upstream_stash
        )
        passed = passed_along(output, "section", 1, senders)
        return (passed, stashed, upstream_stash)

    carry = (zero_rows, stash_init, upstream_init)
    for lo, hi in phases(sections, micro):
        senders = [r for r in range(sections - 1) if any(0 <= t - r < micro for t in range(lo, hi))]
        carry = lax.fori_loop(lo, hi, functools.partial(forward_step, senders), carry)
    unused_rows, stashed, upstream_stash = carry
    totals_init = jnp.zeros((micro, buses, width), jnp.bfloat16)

    def backward_step(senders, step, carry):
        incoming, collected = carry
        slot_raw = step - (sections - 1 - rank)
        active = (slot_raw >= 0) & (slot_raw < micro)
        slot = jnp.clip(slot_raw, 0, micro - 1)
        last_grad = lax.dynamic_index_in_dim(upstream_stash, slot, 0, keepdims=True)
        upstream = jnp.where(rank == sections - 1, last_grad, incoming[None])
        allowed_slot = lax.dynamic_index_in_dim(allowed, slot, 0, keepdims=True)

        def backward_do_work(collected_in):
            kept_parts = tuple(
                (
                    lax.dynamic_index_in_dim(whole_array, slot, 0, keepdims=True)
                    for whole_array in stashed
                )
            )
            lower, value_total = layer_backward(upstream, weight, allowed_slot, kept_parts)
            collected_out = lax.dynamic_update_index_in_dim(collected_in, value_total, slot, 0)
            return (lower[0], collected_out)

        def backward_no_work(collected_in):
            return (zero_rows, collected_in)

        lower, collected = lax.cond(active, backward_do_work, backward_no_work, collected)
        passed = passed_along(lower, "section", -1, senders)
        return (passed, collected)

    carry = (zero_rows, totals_init)
    for lo, hi in phases(sections, micro):
        senders = [
            r
            for r in range(1, sections)
            if any(0 <= t - (sections - 1 - r) < micro for t in range(lo, hi))
        ]
        carry = lax.fori_loop(lo, hi, functools.partial(backward_step, senders), carry)
    unused_rows, collected = carry
    cores = lax.axis_size("core")
    groups = lax.axis_size("dp_hi")
    core = lax.axis_index("core")
    rows_each = width // (groups * cores)
    normed_all = stashed[0].astype(jnp.bfloat16).reshape(micro * buses, groups, cores, rows_each)
    totals_all = collected.reshape(micro * buses, width)

    def partial_grad(which):
        chosen = lax.dynamic_index_in_dim(normed_all, which, 2, keepdims=False)
        return lax.dot_general(
            chosen.reshape(micro * buses, groups * rows_each),
            totals_all,
            (((0,), (0,)), ((), ())),
            preferred_element_type=jnp.float32,
        )

    received = lax.ppermute(partial_grad(1 - core), "core", [(0, 1), (1, 0)])
    half = lax.optimization_barrier(partial_grad(core)) + received
    swapped = lax.all_to_all(half.astype(jnp.bfloat16), "dp_hi", 0, 0, tiled=True)
    summed = jnp.sum(swapped.reshape(groups, rows_each, width).astype(jnp.float32), axis=0)
    return summed[None]


def solution(mesh):
    sections, dp = mesh.devices.shape
    split = Mesh(mesh.devices.reshape(sections, dp // 2, 2), ("section", "dp_hi", "core"))
    rows = ("dp_hi", "core")
    in_specs = (
        P(rows, None, None),
        P(rows, None),
        P(rows, None),
        P(),
        P("section", None, None),
        P(),
    )
    out_specs = P("section", rows, None)
    return jax.shard_map(
        per_device, mesh=split, in_specs=in_specs, out_specs=out_specs, check_vma=False
    )
```

```python
import functools

import jax
import jax.numpy as jnp
from jax import lax
from jax.sharding import Mesh, PartitionSpec as P

HEADS = 16
BLOCK = 32


epsilon = 1e-05


def passed_along(block, axis, distance, senders):
    return lax.ppermute(block, axis, [(i, i + distance) for i in senders])


def phases(sections, micro):
    middle = sections // 2
    bounds = [0, middle - 1, middle - 1 + micro, sections + micro - 1]
    return [(lo, hi) for lo, hi in zip(bounds[:-1], bounds[1:]) if hi > lo]


def scatter_sum(block, axis):
    count = lax.axis_size(axis)
    me = lax.axis_index(axis)
    pieces = block.reshape(count, block.shape[0] // count, block.shape[1])
    total = lax.dynamic_index_in_dim(pieces, me, 0, keepdims=False)
    for shift in range(1, count):
        sent = lax.dynamic_index_in_dim(pieces, (me + shift) % count, 0, keepdims=False)
        route = [(i, (i + shift) % count) for i in range(count)]
        received = lax.ppermute(sent.astype(jnp.bfloat16), axis, route)
        total = total + received.astype(jnp.float32)
    return total


def allowed_pairs(pattern, outage):
    buses = outage.shape[-1]
    block_count = buses // BLOCK
    block_ids = jnp.arange(block_count, dtype=jnp.int32)
    pair_hits = (pattern[:, 0][None, None, :] == block_ids[:, None, None]) & (
        pattern[:, 1][None, None, :] == block_ids[None, :, None]
    )
    block_table = jnp.max(pair_hits.astype(jnp.float32), axis=2)
    member = ((jnp.arange(buses, dtype=jnp.int32) // BLOCK)[:, None] == block_ids[None, :]).astype(
        jnp.float32
    )
    pair_mask = jnp.dot(
        jnp.dot(member, block_table, precision=lax.Precision.HIGHEST),
        member.T,
        precision=lax.Precision.HIGHEST,
    )
    in_service = outage.astype(jnp.float32)
    self_mask = jnp.eye(buses, dtype=jnp.float32)
    return pair_mask[None] * jnp.maximum(in_service[:, None, :], self_mask[None])


def layer_forward(hidden, weight, allowed):
    num_states, buses, width = hidden.shape
    split_shape = (num_states, buses, HEADS, width // HEADS)
    hidden_f = hidden.astype(jnp.float32)
    centred = hidden_f - jnp.mean(hidden_f, axis=-1, keepdims=True)
    inverse_std = lax.rsqrt(jnp.mean(centred * centred, axis=-1, keepdims=True) + epsilon)
    scaled = centred * inverse_std
    normed = scaled.astype(jnp.bfloat16)
    values_b = (
        jnp.dot(normed.reshape(-1, width), weight, preferred_element_type=jnp.float32)
        .astype(jnp.bfloat16)
        .reshape(split_shape)
    )
    features = (jax.nn.elu(values_b.astype(jnp.float32)) + 1.0).astype(jnp.bfloat16)
    kernel = (
        jnp.einsum("nihc,njhc->nhij", features, features, preferred_element_type=jnp.float32)
        * allowed[:, None]
    )
    totals = jnp.sum(kernel, axis=-1, keepdims=True)
    attention = kernel / totals
    attention_b = attention.astype(jnp.bfloat16)
    gathered = jnp.einsum(
        "nhij,njhc->nihc", attention_b, values_b, preferred_element_type=jnp.float32
    )
    output = (hidden_f + gathered.reshape(num_states, buses, width)).astype(jnp.bfloat16)
    return (output, (scaled, inverse_std, values_b, attention, totals))


def layer_backward(upstream, weight, allowed, kept_parts):
    scaled, inverse_std, values_b, attention, totals = kept_parts
    num_states, buses, width = upstream.shape
    grad_f = upstream.astype(jnp.float32)
    grad_heads = upstream.reshape(values_b.shape)
    values_f = values_b.astype(jnp.float32)
    features = (jax.nn.elu(values_f) + 1.0).astype(jnp.bfloat16)
    attention_b = attention.astype(jnp.bfloat16)
    value_grad = jnp.einsum(
        "nhij,nihc->njhc", attention_b, grad_heads, preferred_element_type=jnp.float32
    )
    attention_grad = jnp.einsum(
        "nihc,njhc->nhij", grad_heads, values_b, preferred_element_type=jnp.float32
    )
    row_terms = jnp.sum(attention_grad * attention, axis=-1, keepdims=True)
    kernel_grad = ((attention_grad - row_terms) / totals * allowed[:, None]).astype(jnp.bfloat16)
    feature_grad = jnp.einsum(
        "nhij,njhc->nihc", kernel_grad, features, preferred_element_type=jnp.float32
    )
    feature_grad = feature_grad + jnp.einsum(
        "nhji,njhc->nihc", kernel_grad, features, preferred_element_type=jnp.float32
    )
    slope = jnp.where(values_f > 0.0, 1.0, jnp.exp(jnp.minimum(values_f, 0.0)))
    value_total = (
        (value_grad + feature_grad * slope).astype(jnp.bfloat16).reshape(num_states, buses, width)
    )
    normed_grad = lax.dot_general(
        value_total.reshape(-1, width),
        weight,
        (((1,), (1,)), ((), ())),
        preferred_element_type=jnp.float32,
    ).reshape(num_states, buses, width)
    mean_grad = jnp.mean(normed_grad, axis=-1, keepdims=True)
    mean_cross = jnp.mean(normed_grad * scaled, axis=-1, keepdims=True)
    lower = (grad_f + inverse_std * (normed_grad - mean_grad - scaled * mean_cross)).astype(
        jnp.bfloat16
    )
    return (lower, value_total)


def per_device(states, outage, targets, pattern, weights, readout):
    sections = lax.axis_size("section")
    rank = lax.axis_index("section")
    micro, buses, width = states.shape
    weight = weights[0]
    allowed = allowed_pairs(pattern, outage)
    head_size = width // HEADS
    steps_total = sections + micro - 1
    zero_rows = jnp.zeros((buses, width), jnp.bfloat16)
    stash_init = (
        jnp.zeros((micro, buses, width), jnp.float32),
        jnp.zeros((micro, buses, 1), jnp.float32),
        jnp.zeros((micro, buses, HEADS, head_size), jnp.bfloat16),
        jnp.zeros((micro, HEADS, buses, buses), jnp.float32),
        jnp.zeros((micro, HEADS, buses, 1), jnp.float32),
    )
    upstream_init = jnp.zeros((micro, buses, width), jnp.bfloat16)

    def forward_step(senders, step, carry):
        incoming, stashed, upstream_stash = carry
        slot_raw = step - rank
        active = (slot_raw >= 0) & (slot_raw < micro)
        slot = jnp.clip(slot_raw, 0, micro - 1)
        first_state = lax.dynamic_index_in_dim(states, slot, 0, keepdims=True)
        source = jnp.where(rank == 0, first_state, incoming[None])
        allowed_slot = lax.dynamic_index_in_dim(allowed, slot, 0, keepdims=True)

        def forward_do_work(stash_in, upstream_in):
            output, kept_parts = layer_forward(source, weight, allowed_slot)
            stash_out = tuple(
                (
                    lax.dynamic_update_index_in_dim(whole_array, new_piece, slot, 0)
                    for whole_array, new_piece in zip(stash_in, kept_parts)
                )
            )
            predicted = jnp.sum(output.astype(jnp.float32) * readout, axis=-1)
            misfit = predicted - lax.dynamic_index_in_dim(targets, slot, 0, keepdims=True)
            cotangent = (misfit[..., None] * readout).astype(jnp.bfloat16)
            upstream_out = lax.dynamic_update_index_in_dim(upstream_in, cotangent, slot, 0)
            return (output[0], stash_out, upstream_out)

        def forward_no_work(stash_in, upstream_in):
            return (zero_rows, stash_in, upstream_in)

        output, stashed, upstream_stash = lax.cond(
            active, forward_do_work, forward_no_work, stashed, upstream_stash
        )
        passed = passed_along(output, "section", 1, senders)
        return (passed, stashed, upstream_stash)

    carry = (zero_rows, stash_init, upstream_init)
    for lo, hi in phases(sections, micro):
        senders = [r for r in range(sections - 1) if any(0 <= t - r < micro for t in range(lo, hi))]
        carry = lax.fori_loop(lo, hi, functools.partial(forward_step, senders), carry)
    unused_rows, stashed, upstream_stash = carry
    totals_init = jnp.zeros((micro, buses, width), jnp.bfloat16)

    def backward_step(senders, step, carry):
        incoming, collected = carry
        slot_raw = step - (sections - 1 - rank)
        active = (slot_raw >= 0) & (slot_raw < micro)
        slot = jnp.clip(slot_raw, 0, micro - 1)
        last_grad = lax.dynamic_index_in_dim(upstream_stash, slot, 0, keepdims=True)
        upstream = jnp.where(rank == sections - 1, last_grad, incoming[None])
        allowed_slot = lax.dynamic_index_in_dim(allowed, slot, 0, keepdims=True)

        def backward_do_work(collected_in):
            kept_parts = tuple(
                (
                    lax.dynamic_index_in_dim(whole_array, slot, 0, keepdims=True)
                    for whole_array in stashed
                )
            )
            lower, value_total = layer_backward(upstream, weight, allowed_slot, kept_parts)
            collected_out = lax.dynamic_update_index_in_dim(collected_in, value_total, slot, 0)
            return (lower[0], collected_out)

        def backward_no_work(collected_in):
            return (zero_rows, collected_in)

        lower, collected = lax.cond(active, backward_do_work, backward_no_work, collected)
        passed = passed_along(lower, "section", -1, senders)
        return (passed, collected)

    carry = (zero_rows, totals_init)
    for lo, hi in phases(sections, micro):
        senders = [
            r
            for r in range(1, sections)
            if any(0 <= t - (sections - 1 - r) < micro for t in range(lo, hi))
        ]
        carry = lax.fori_loop(lo, hi, functools.partial(backward_step, senders), carry)
    unused_rows, collected = carry
    cores = lax.axis_size("core")
    ys = lax.axis_size("y")
    zs = lax.axis_size("z")
    core = lax.axis_index("core")
    rows_each = width // (zs * ys * cores)
    normed_all = stashed[0].astype(jnp.bfloat16).reshape(micro * buses, zs, ys, cores, rows_each)
    normed_all = jnp.transpose(normed_all, (0, 3, 2, 1, 4))
    totals_all = collected.reshape(micro * buses, width)

    def partial_grad(which):
        chosen = lax.dynamic_index_in_dim(normed_all, which, 1, keepdims=False)
        return lax.dot_general(
            chosen.reshape(micro * buses, width // cores),
            totals_all,
            (((0,), (0,)), ((), ())),
            preferred_element_type=jnp.float32,
        )

    received = lax.ppermute(partial_grad(1 - core), "core", [(0, 1), (1, 0)])
    half = lax.optimization_barrier(partial_grad(core)) + received
    summed = scatter_sum(scatter_sum(half, "y"), "z")
    return summed[None]


def solution(mesh):
    sections, dp = mesh.devices.shape
    split = Mesh(mesh.devices.reshape(sections, 4, dp // 8, 2), ("section", "z", "y", "core"))
    rows = ("z", "y", "core")
    in_specs = (
        P(rows, None, None),
        P(rows, None),
        P(rows, None),
        P(),
        P("section", None, None),
        P(),
    )
    out_specs = P("section", rows, None)
    return jax.shard_map(
        per_device, mesh=split, in_specs=in_specs, out_specs=out_specs, check_vma=False
    )
```

```python
import functools

import jax
import jax.numpy as jnp
from jax import lax
from jax.sharding import Mesh, PartitionSpec as P

HEADS = 16
BLOCK = 32


epsilon = 1e-05


def passed_along(block, axis, distance, senders):
    return lax.ppermute(block, axis, [(i, i + distance) for i in senders])


def phases(sections, micro):
    middle = sections // 2
    bounds = [0, middle - 1, middle - 1 + micro, sections + micro - 1]
    return [(lo, hi) for lo, hi in zip(bounds[:-1], bounds[1:]) if hi > lo]


def scatter_sum(block, axis):
    count = lax.axis_size(axis)
    me = lax.axis_index(axis)
    pieces = block.reshape(count, block.shape[0] // count, block.shape[1])
    total = lax.dynamic_index_in_dim(pieces, me, 0, keepdims=False)
    for shift in range(1, count):
        sent = lax.dynamic_index_in_dim(pieces, (me + shift) % count, 0, keepdims=False)
        route = [(i, (i + shift) % count) for i in range(count)]
        received = lax.ppermute(sent.astype(jnp.bfloat16), axis, route)
        total = total + received.astype(jnp.float32)
    return total


def allowed_pairs(pattern, outage):
    buses = outage.shape[-1]
    block_count = buses // BLOCK
    block_ids = jnp.arange(block_count, dtype=jnp.int32)
    pair_hits = (pattern[:, 0][None, None, :] == block_ids[:, None, None]) & (
        pattern[:, 1][None, None, :] == block_ids[None, :, None]
    )
    block_table = jnp.max(pair_hits.astype(jnp.float32), axis=2)
    member = ((jnp.arange(buses, dtype=jnp.int32) // BLOCK)[:, None] == block_ids[None, :]).astype(
        jnp.float32
    )
    pair_mask = jnp.dot(
        jnp.dot(member, block_table, precision=lax.Precision.HIGHEST),
        member.T,
        precision=lax.Precision.HIGHEST,
    )
    in_service = outage.astype(jnp.float32)
    self_mask = jnp.eye(buses, dtype=jnp.float32)
    return pair_mask[None] * jnp.maximum(in_service[:, None, :], self_mask[None])


def layer_forward(hidden, weight, allowed):
    num_states, buses, width = hidden.shape
    split_shape = (num_states, buses, HEADS, width // HEADS)
    hidden_f = hidden.astype(jnp.float32)
    centred = hidden_f - jnp.mean(hidden_f, axis=-1, keepdims=True)
    inverse_std = lax.rsqrt(jnp.mean(centred * centred, axis=-1, keepdims=True) + epsilon)
    scaled = centred * inverse_std
    normed = scaled.astype(jnp.bfloat16)
    values_b = (
        jnp.dot(normed.reshape(-1, width), weight, preferred_element_type=jnp.float32)
        .astype(jnp.bfloat16)
        .reshape(split_shape)
    )
    features = (jax.nn.elu(values_b.astype(jnp.float32)) + 1.0).astype(jnp.bfloat16)
    kernel = (
        jnp.einsum("nihc,njhc->nhij", features, features, preferred_element_type=jnp.float32)
        * allowed[:, None]
    )
    totals = jnp.sum(kernel, axis=-1, keepdims=True)
    attention = kernel / totals
    attention_b = attention.astype(jnp.bfloat16)
    gathered = jnp.einsum(
        "nhij,njhc->nihc", attention_b, values_b, preferred_element_type=jnp.float32
    )
    output = (hidden_f + gathered.reshape(num_states, buses, width)).astype(jnp.bfloat16)
    return (output, (scaled, inverse_std, values_b, attention, totals))


def layer_backward(upstream, weight, allowed, kept_parts):
    scaled, inverse_std, values_b, attention, totals = kept_parts
    num_states, buses, width = upstream.shape
    grad_f = upstream.astype(jnp.float32)
    grad_heads = upstream.reshape(values_b.shape)
    values_f = values_b.astype(jnp.float32)
    features = (jax.nn.elu(values_f) + 1.0).astype(jnp.bfloat16)
    attention_b = attention.astype(jnp.bfloat16)
    value_grad = jnp.einsum(
        "nhij,nihc->njhc", attention_b, grad_heads, preferred_element_type=jnp.float32
    )
    attention_grad = jnp.einsum(
        "nihc,njhc->nhij", grad_heads, values_b, preferred_element_type=jnp.float32
    )
    row_terms = jnp.sum(attention_grad * attention, axis=-1, keepdims=True)
    kernel_grad = ((attention_grad - row_terms) / totals * allowed[:, None]).astype(jnp.bfloat16)
    feature_grad = jnp.einsum(
        "nhij,njhc->nihc", kernel_grad, features, preferred_element_type=jnp.float32
    )
    feature_grad = feature_grad + jnp.einsum(
        "nhji,njhc->nihc", kernel_grad, features, preferred_element_type=jnp.float32
    )
    slope = jnp.where(values_f > 0.0, 1.0, jnp.exp(jnp.minimum(values_f, 0.0)))
    value_total = (
        (value_grad + feature_grad * slope).astype(jnp.bfloat16).reshape(num_states, buses, width)
    )
    normed_grad = lax.dot_general(
        value_total.reshape(-1, width),
        weight,
        (((1,), (1,)), ((), ())),
        preferred_element_type=jnp.float32,
    ).reshape(num_states, buses, width)
    mean_grad = jnp.mean(normed_grad, axis=-1, keepdims=True)
    mean_cross = jnp.mean(normed_grad * scaled, axis=-1, keepdims=True)
    lower = (grad_f + inverse_std * (normed_grad - mean_grad - scaled * mean_cross)).astype(
        jnp.bfloat16
    )
    return (lower, value_total)


def per_device(states, outage, targets, pattern, weights, readout):
    sections = lax.axis_size("section")
    rank = lax.axis_index("section")
    micro, buses, width = states.shape
    weight = weights[0]
    allowed = allowed_pairs(pattern, outage)
    head_size = width // HEADS
    steps_total = sections + micro - 1
    zero_rows = jnp.zeros((buses, width), jnp.bfloat16)
    stash_init = (
        jnp.zeros((micro, buses, width), jnp.float32),
        jnp.zeros((micro, buses, 1), jnp.float32),
        jnp.zeros((micro, buses, HEADS, head_size), jnp.bfloat16),
        jnp.zeros((micro, HEADS, buses, buses), jnp.float32),
        jnp.zeros((micro, HEADS, buses, 1), jnp.float32),
    )
    upstream_init = jnp.zeros((micro, buses, width), jnp.bfloat16)

    def forward_step(senders, step, carry):
        incoming, stashed, upstream_stash = carry
        slot_raw = step - rank
        active = (slot_raw >= 0) & (slot_raw < micro)
        slot = jnp.clip(slot_raw, 0, micro - 1)
        first_state = lax.dynamic_index_in_dim(states, slot, 0, keepdims=True)
        source = jnp.where(rank == 0, first_state, incoming[None])
        allowed_slot = lax.dynamic_index_in_dim(allowed, slot, 0, keepdims=True)

        def forward_do_work(stash_in, upstream_in):
            output, kept_parts = layer_forward(source, weight, allowed_slot)
            stash_out = tuple(
                (
                    lax.dynamic_update_index_in_dim(whole_array, new_piece, slot, 0)
                    for whole_array, new_piece in zip(stash_in, kept_parts)
                )
            )
            predicted = jnp.sum(output.astype(jnp.float32) * readout, axis=-1)
            misfit = predicted - lax.dynamic_index_in_dim(targets, slot, 0, keepdims=True)
            cotangent = (misfit[..., None] * readout).astype(jnp.bfloat16)
            upstream_out = lax.dynamic_update_index_in_dim(upstream_in, cotangent, slot, 0)
            return (output[0], stash_out, upstream_out)

        def forward_no_work(stash_in, upstream_in):
            return (zero_rows, stash_in, upstream_in)

        output, stashed, upstream_stash = lax.cond(
            active, forward_do_work, forward_no_work, stashed, upstream_stash
        )
        passed = passed_along(output, "section", 1, senders)
        return (passed, stashed, upstream_stash)

    carry = (zero_rows, stash_init, upstream_init)
    for lo, hi in phases(sections, micro):
        senders = [r for r in range(sections - 1) if any(0 <= t - r < micro for t in range(lo, hi))]
        carry = lax.fori_loop(lo, hi, functools.partial(forward_step, senders), carry)
    unused_rows, stashed, upstream_stash = carry
    totals_init = jnp.zeros((micro, buses, width), jnp.bfloat16)

    def backward_step(senders, step, carry):
        incoming, collected = carry
        slot_raw = step - (sections - 1 - rank)
        active = (slot_raw >= 0) & (slot_raw < micro)
        slot = jnp.clip(slot_raw, 0, micro - 1)
        last_grad = lax.dynamic_index_in_dim(upstream_stash, slot, 0, keepdims=True)
        upstream = jnp.where(rank == sections - 1, last_grad, incoming[None])
        allowed_slot = lax.dynamic_index_in_dim(allowed, slot, 0, keepdims=True)

        def backward_do_work(collected_in):
            kept_parts = tuple(
                (
                    lax.dynamic_index_in_dim(whole_array, slot, 0, keepdims=True)
                    for whole_array in stashed
                )
            )
            lower, value_total = layer_backward(upstream, weight, allowed_slot, kept_parts)
            collected_out = lax.dynamic_update_index_in_dim(collected_in, value_total, slot, 0)
            return (lower[0], collected_out)

        def backward_no_work(collected_in):
            return (zero_rows, collected_in)

        lower, collected = lax.cond(active, backward_do_work, backward_no_work, collected)
        passed = passed_along(lower, "section", -1, senders)
        return (passed, collected)

    cores = lax.axis_size("core")
    ys = lax.axis_size("y")
    zs = lax.axis_size("z")
    core = lax.axis_index("core")
    swap = [(0, 1), (1, 0)]
    rows_each = width // (zs * ys * cores)
    normed_all = stashed[0].astype(jnp.bfloat16).reshape(micro * buses, zs, ys, cores, rows_each)
    normed_all = jnp.transpose(normed_all, (3, 2, 1, 4, 0)).reshape(
        cores, width // cores, micro * buses
    )
    mine = lax.dynamic_index_in_dim(normed_all, core, 0, keepdims=False)
    theirs = lax.ppermute(
        lax.dynamic_index_in_dim(normed_all, 1 - core, 0, keepdims=False), "core", swap
    )
    left, carry = lax.optimization_barrier(
        (jnp.concatenate([mine, theirs], axis=1), (zero_rows, totals_init))
    )
    for lo, hi in phases(sections, micro):
        senders = [
            r
            for r in range(1, sections)
            if any(0 <= t - (sections - 1 - r) < micro for t in range(lo, hi))
        ]
        carry = lax.fori_loop(lo, hi, functools.partial(backward_step, senders), carry)
    unused_rows, collected = carry
    own = collected.reshape(micro * buses, width)
    right = jnp.concatenate([own, lax.ppermute(own, "core", swap)], axis=0)
    half = jnp.dot(left, right, preferred_element_type=jnp.float32)
    summed = scatter_sum(scatter_sum(half, "y"), "z")
    return summed[None]


def solution(mesh):
    sections, dp = mesh.devices.shape
    split = Mesh(mesh.devices.reshape(sections, 4, dp // 8, 2), ("section", "z", "y", "core"))
    rows = ("z", "y", "core")
    in_specs = (
        P(rows, None, None),
        P(rows, None),
        P(rows, None),
        P(),
        P("section", None, None),
        P(),
    )
    out_specs = P("section", rows, None)
    return jax.shard_map(
        per_device, mesh=split, in_specs=in_specs, out_specs=out_specs, check_vma=False
    )
```

```python
import functools

import jax
import jax.numpy as jnp
from jax import lax
from jax.sharding import Mesh, PartitionSpec as P

HEADS = 16
BLOCK = 32


epsilon = 1e-05


def passed_along(block, axis, distance, senders):
    return lax.ppermute(block, axis, [(i, i + distance) for i in senders])


def phases(sections, micro):
    middle = sections // 2
    bounds = [0, middle - 1, middle - 1 + micro, sections + micro - 1]
    return [(lo, hi) for lo, hi in zip(bounds[:-1], bounds[1:]) if hi > lo]


def scatter_sum(block, axis):
    count = lax.axis_size(axis)
    me = lax.axis_index(axis)
    pieces = block.reshape(count, block.shape[0] // count, block.shape[1])
    total = lax.dynamic_index_in_dim(pieces, me, 0, keepdims=False)
    for shift in range(1, count):
        sent = lax.dynamic_index_in_dim(pieces, (me + shift) % count, 0, keepdims=False)
        route = [(i, (i + shift) % count) for i in range(count)]
        received = lax.ppermute(sent.astype(jnp.bfloat16), axis, route)
        total = total + received.astype(jnp.float32)
    return total


def allowed_pairs(pattern, outage):
    buses = outage.shape[-1]
    block_count = buses // BLOCK
    block_ids = jnp.arange(block_count, dtype=jnp.int32)
    pair_hits = (pattern[:, 0][None, None, :] == block_ids[:, None, None]) & (
        pattern[:, 1][None, None, :] == block_ids[None, :, None]
    )
    block_table = jnp.max(pair_hits.astype(jnp.float32), axis=2)
    member = ((jnp.arange(buses, dtype=jnp.int32) // BLOCK)[:, None] == block_ids[None, :]).astype(
        jnp.float32
    )
    pair_mask = jnp.dot(
        jnp.dot(member, block_table, precision=lax.Precision.HIGHEST),
        member.T,
        precision=lax.Precision.HIGHEST,
    )
    in_service = outage.astype(jnp.float32)
    self_mask = jnp.eye(buses, dtype=jnp.float32)
    return pair_mask[None] * jnp.maximum(in_service[:, None, :], self_mask[None])


def layer_forward(hidden, weight, allowed):
    num_states, buses, width = hidden.shape
    split_shape = (num_states, buses, HEADS, width // HEADS)
    hidden_f = hidden.astype(jnp.float32)
    centred = hidden_f - jnp.mean(hidden_f, axis=-1, keepdims=True)
    inverse_std = lax.rsqrt(jnp.mean(centred * centred, axis=-1, keepdims=True) + epsilon)
    scaled = centred * inverse_std
    normed = scaled.astype(jnp.bfloat16)
    values_b = (
        jnp.dot(normed.reshape(-1, width), weight, preferred_element_type=jnp.float32)
        .astype(jnp.bfloat16)
        .reshape(split_shape)
    )
    features = (jax.nn.elu(values_b.astype(jnp.float32)) + 1.0).astype(jnp.bfloat16)
    kernel = (
        jnp.einsum("nihc,njhc->nhij", features, features, preferred_element_type=jnp.float32)
        * allowed[:, None]
    )
    totals = jnp.sum(kernel, axis=-1, keepdims=True)
    attention = kernel / totals
    attention_b = attention.astype(jnp.bfloat16)
    gathered = jnp.einsum(
        "nhij,njhc->nihc", attention_b, values_b, preferred_element_type=jnp.float32
    )
    output = (hidden_f + gathered.reshape(num_states, buses, width)).astype(jnp.bfloat16)
    return (output, (scaled, inverse_std, values_b, attention, totals))


def layer_backward(upstream, weight, allowed, kept_parts):
    scaled, inverse_std, values_b, attention, totals = kept_parts
    num_states, buses, width = upstream.shape
    grad_f = upstream.astype(jnp.float32)
    grad_heads = upstream.reshape(values_b.shape)
    values_f = values_b.astype(jnp.float32)
    features = (jax.nn.elu(values_f) + 1.0).astype(jnp.bfloat16)
    attention_b = attention.astype(jnp.bfloat16)
    value_grad = jnp.einsum(
        "nhij,nihc->njhc", attention_b, grad_heads, preferred_element_type=jnp.float32
    )
    attention_grad = jnp.einsum(
        "nihc,njhc->nhij", grad_heads, values_b, preferred_element_type=jnp.float32
    )
    row_terms = jnp.sum(attention_grad * attention, axis=-1, keepdims=True)
    kernel_grad = ((attention_grad - row_terms) / totals * allowed[:, None]).astype(jnp.bfloat16)
    feature_grad = jnp.einsum(
        "nhij,njhc->nihc", kernel_grad, features, preferred_element_type=jnp.float32
    )
    feature_grad = feature_grad + jnp.einsum(
        "nhji,njhc->nihc", kernel_grad, features, preferred_element_type=jnp.float32
    )
    slope = jnp.where(values_f > 0.0, 1.0, jnp.exp(jnp.minimum(values_f, 0.0)))
    value_total = (
        (value_grad + feature_grad * slope).astype(jnp.bfloat16).reshape(num_states, buses, width)
    )
    normed_grad = lax.dot_general(
        value_total.reshape(-1, width),
        weight,
        (((1,), (1,)), ((), ())),
        preferred_element_type=jnp.float32,
    ).reshape(num_states, buses, width)
    mean_grad = jnp.mean(normed_grad, axis=-1, keepdims=True)
    mean_cross = jnp.mean(normed_grad * scaled, axis=-1, keepdims=True)
    lower = (grad_f + inverse_std * (normed_grad - mean_grad - scaled * mean_cross)).astype(
        jnp.bfloat16
    )
    return (lower, value_total)


def per_device(states, outage, targets, pattern, weights, readout):
    sections = lax.axis_size("section")
    rank = lax.axis_index("section")
    micro, buses, width = states.shape
    weight = weights[0]
    allowed = allowed_pairs(pattern, outage)
    head_size = width // HEADS
    steps_total = sections + micro - 1
    zero_rows = jnp.zeros((buses, width), jnp.bfloat16)
    stash_init = (
        jnp.zeros((micro, buses, width), jnp.float32),
        jnp.zeros((micro, buses, 1), jnp.float32),
        jnp.zeros((micro, buses, HEADS, head_size), jnp.bfloat16),
        jnp.zeros((micro, HEADS, buses, buses), jnp.float32),
        jnp.zeros((micro, HEADS, buses, 1), jnp.float32),
    )
    upstream_init = jnp.zeros((micro, buses, width), jnp.bfloat16)

    def forward_step(senders, step, carry):
        incoming, stashed, upstream_stash = carry
        slot_raw = step - rank
        active = (slot_raw >= 0) & (slot_raw < micro)
        slot = jnp.clip(slot_raw, 0, micro - 1)
        first_state = lax.dynamic_index_in_dim(states, slot, 0, keepdims=True)
        source = jnp.where(rank == 0, first_state, incoming[None])
        allowed_slot = lax.dynamic_index_in_dim(allowed, slot, 0, keepdims=True)

        def forward_do_work(stash_in, upstream_in):
            output, kept_parts = layer_forward(source, weight, allowed_slot)
            stash_out = tuple(
                (
                    lax.dynamic_update_index_in_dim(whole_array, new_piece, slot, 0)
                    for whole_array, new_piece in zip(stash_in, kept_parts)
                )
            )
            predicted = jnp.sum(output.astype(jnp.float32) * readout, axis=-1)
            misfit = predicted - lax.dynamic_index_in_dim(targets, slot, 0, keepdims=True)
            cotangent = (misfit[..., None] * readout).astype(jnp.bfloat16)
            upstream_out = lax.dynamic_update_index_in_dim(upstream_in, cotangent, slot, 0)
            return (output[0], stash_out, upstream_out)

        def forward_no_work(stash_in, upstream_in):
            return (zero_rows, stash_in, upstream_in)

        output, stashed, upstream_stash = lax.cond(
            active, forward_do_work, forward_no_work, stashed, upstream_stash
        )
        passed = passed_along(output, "section", 1, senders)
        return (passed, stashed, upstream_stash)

    carry = (zero_rows, stash_init, upstream_init)
    for lo, hi in phases(sections, micro):
        senders = [r for r in range(sections - 1) if any(0 <= t - r < micro for t in range(lo, hi))]
        carry = lax.fori_loop(lo, hi, functools.partial(forward_step, senders), carry)
    unused_rows, stashed, upstream_stash = carry
    totals_init = jnp.zeros((micro, buses, width), jnp.bfloat16)

    def backward_step(senders, step, carry):
        incoming, collected = carry
        slot_raw = step - (sections - 1 - rank)
        active = (slot_raw >= 0) & (slot_raw < micro)
        slot = jnp.clip(slot_raw, 0, micro - 1)
        last_grad = lax.dynamic_index_in_dim(upstream_stash, slot, 0, keepdims=True)
        upstream = jnp.where(rank == sections - 1, last_grad, incoming[None])
        allowed_slot = lax.dynamic_index_in_dim(allowed, slot, 0, keepdims=True)

        def backward_do_work(collected_in):
            kept_parts = tuple(
                (
                    lax.dynamic_index_in_dim(whole_array, slot, 0, keepdims=True)
                    for whole_array in stashed
                )
            )
            lower, value_total = layer_backward(upstream, weight, allowed_slot, kept_parts)
            collected_out = lax.dynamic_update_index_in_dim(collected_in, value_total, slot, 0)
            return (lower[0], collected_out)

        def backward_no_work(collected_in):
            return (zero_rows, collected_in)

        lower, collected = lax.cond(active, backward_do_work, backward_no_work, collected)
        passed = passed_along(lower, "section", -1, senders)
        return (passed, collected)

    cores = lax.axis_size("core")
    ys = lax.axis_size("y")
    zs = lax.axis_size("z")
    core = lax.axis_index("core")
    swap = [(0, 1), (1, 0)]
    rows_each = width // (zs * ys * cores)
    normed_all = stashed[0].astype(jnp.bfloat16).reshape(micro * buses, zs, ys, cores, rows_each)
    normed_all = jnp.transpose(normed_all, (3, 2, 1, 4, 0)).reshape(
        cores, width // cores, micro * buses
    )
    mine = lax.dynamic_index_in_dim(normed_all, core, 0, keepdims=False)
    theirs = lax.ppermute(
        lax.dynamic_index_in_dim(normed_all, 1 - core, 0, keepdims=False), "core", swap
    )
    left = jnp.concatenate([mine, theirs], axis=1)
    carry = (zero_rows, totals_init)
    for lo, hi in phases(sections, micro):
        senders = [
            r
            for r in range(1, sections)
            if any(0 <= t - (sections - 1 - r) < micro for t in range(lo, hi))
        ]
        carry = lax.fori_loop(lo, hi, functools.partial(backward_step, senders), carry)
    unused_rows, collected = carry
    own = collected.reshape(micro * buses, width)
    right = jnp.concatenate([own, lax.ppermute(own, "core", swap)], axis=0)
    half = jnp.dot(left, right, preferred_element_type=jnp.float32)
    summed = scatter_sum(scatter_sum(half, "y"), "z")
    return summed[None]


def solution(mesh):
    sections, dp = mesh.devices.shape
    split = Mesh(mesh.devices.reshape(sections, 4, dp // 8, 2), ("section", "z", "y", "core"))
    rows = ("z", "y", "core")
    in_specs = (
        P(rows, None, None),
        P(rows, None),
        P(rows, None),
        P(),
        P("section", None, None),
        P(),
    )
    out_specs = P("section", rows, None)
    return jax.shard_map(
        per_device, mesh=split, in_specs=in_specs, out_specs=out_specs, check_vma=False
    )
```

```python
import functools

import jax
import jax.numpy as jnp
from jax import lax
from jax.sharding import Mesh, PartitionSpec as P

HEADS = 16
BLOCK = 32


epsilon = 1e-05


def passed_along(block, axis, distance, senders):
    return lax.ppermute(block, axis, [(i, i + distance) for i in senders])


def phases(sections, micro):
    middle = sections // 2
    bounds = [0, middle - 1, middle - 1 + micro, sections + micro - 1]
    return [(lo, hi) for lo, hi in zip(bounds[:-1], bounds[1:]) if hi > lo]


def scatter_sum(block, axis):
    count = lax.axis_size(axis)
    me = lax.axis_index(axis)
    pieces = block.reshape(count, block.shape[0] // count, block.shape[1])
    total = lax.dynamic_index_in_dim(pieces, me, 0, keepdims=False)
    for shift in range(1, count):
        sent = lax.dynamic_index_in_dim(pieces, (me + shift) % count, 0, keepdims=False)
        route = [(i, (i + shift) % count) for i in range(count)]
        received = lax.ppermute(sent.astype(jnp.bfloat16), axis, route)
        total = total + received.astype(jnp.float32)
    return total


def allowed_pairs(pattern, outage):
    buses = outage.shape[-1]
    block_count = buses // BLOCK
    block_ids = jnp.arange(block_count, dtype=jnp.int32)
    pair_hits = (pattern[:, 0][None, None, :] == block_ids[:, None, None]) & (
        pattern[:, 1][None, None, :] == block_ids[None, :, None]
    )
    block_table = jnp.max(pair_hits.astype(jnp.float32), axis=2)
    member = ((jnp.arange(buses, dtype=jnp.int32) // BLOCK)[:, None] == block_ids[None, :]).astype(
        jnp.float32
    )
    pair_mask = jnp.dot(
        jnp.dot(member, block_table, precision=lax.Precision.HIGHEST),
        member.T,
        precision=lax.Precision.HIGHEST,
    )
    in_service = outage.astype(jnp.float32)
    self_mask = jnp.eye(buses, dtype=jnp.float32)
    return pair_mask[None] * jnp.maximum(in_service[:, None, :], self_mask[None])


def layer_forward(hidden, weight, allowed):
    num_states, buses, width = hidden.shape
    split_shape = (num_states, buses, HEADS, width // HEADS)
    hidden_f = hidden.astype(jnp.float32)
    centred = hidden_f - jnp.mean(hidden_f, axis=-1, keepdims=True)
    inverse_std = lax.rsqrt(jnp.mean(centred * centred, axis=-1, keepdims=True) + epsilon)
    scaled = centred * inverse_std
    normed = scaled.astype(jnp.bfloat16)
    values_b = (
        jnp.dot(normed.reshape(-1, width), weight, preferred_element_type=jnp.float32)
        .astype(jnp.bfloat16)
        .reshape(split_shape)
    )
    features = (jax.nn.elu(values_b.astype(jnp.float32)) + 1.0).astype(jnp.bfloat16)
    kernel = (
        jnp.einsum("nihc,njhc->nhij", features, features, preferred_element_type=jnp.float32)
        * allowed[:, None]
    )
    totals = jnp.sum(kernel, axis=-1, keepdims=True)
    attention = kernel / totals
    attention_b = attention.astype(jnp.bfloat16)
    gathered = jnp.einsum(
        "nhij,njhc->nihc", attention_b, values_b, preferred_element_type=jnp.float32
    )
    output = (hidden_f + gathered.reshape(num_states, buses, width)).astype(jnp.bfloat16)
    return (output, (scaled, inverse_std, values_b, attention, totals))


def layer_backward(upstream, weight, allowed, kept_parts):
    scaled, inverse_std, values_b, attention, totals = kept_parts
    num_states, buses, width = upstream.shape
    grad_f = upstream.astype(jnp.float32)
    grad_heads = upstream.reshape(values_b.shape)
    values_f = values_b.astype(jnp.float32)
    features = (jax.nn.elu(values_f) + 1.0).astype(jnp.bfloat16)
    attention_b = attention.astype(jnp.bfloat16)
    value_grad = jnp.einsum(
        "nhij,nihc->njhc", attention_b, grad_heads, preferred_element_type=jnp.float32
    )
    attention_grad = jnp.einsum(
        "nihc,njhc->nhij", grad_heads, values_b, preferred_element_type=jnp.float32
    )
    row_terms = jnp.sum(attention_grad * attention, axis=-1, keepdims=True)
    kernel_grad = ((attention_grad - row_terms) / totals * allowed[:, None]).astype(jnp.bfloat16)
    feature_grad = jnp.einsum(
        "nhij,njhc->nihc", kernel_grad, features, preferred_element_type=jnp.float32
    )
    feature_grad = feature_grad + jnp.einsum(
        "nhji,njhc->nihc", kernel_grad, features, preferred_element_type=jnp.float32
    )
    slope = jnp.where(values_f > 0.0, 1.0, jnp.exp(jnp.minimum(values_f, 0.0)))
    value_total = (
        (value_grad + feature_grad * slope).astype(jnp.bfloat16).reshape(num_states, buses, width)
    )
    normed_grad = lax.dot_general(
        value_total.reshape(-1, width),
        weight,
        (((1,), (1,)), ((), ())),
        preferred_element_type=jnp.float32,
    ).reshape(num_states, buses, width)
    mean_grad = jnp.mean(normed_grad, axis=-1, keepdims=True)
    mean_cross = jnp.mean(normed_grad * scaled, axis=-1, keepdims=True)
    lower = (grad_f + inverse_std * (normed_grad - mean_grad - scaled * mean_cross)).astype(
        jnp.bfloat16
    )
    return (lower, value_total)


def per_device(states, outage, targets, pattern, weights, readout):
    sections = lax.axis_size("section")
    rank = lax.axis_index("section")
    micro, buses, width = states.shape
    weight = weights[0]
    allowed = allowed_pairs(pattern, outage)
    head_size = width // HEADS
    steps_total = sections + micro - 1
    zero_rows = jnp.zeros((buses, width), jnp.bfloat16)
    stash_init = (
        jnp.zeros((micro, buses, width), jnp.float32),
        jnp.zeros((micro, buses, 1), jnp.float32),
        jnp.zeros((micro, buses, HEADS, head_size), jnp.bfloat16),
        jnp.zeros((micro, HEADS, buses, buses), jnp.float32),
        jnp.zeros((micro, HEADS, buses, 1), jnp.float32),
    )
    upstream_init = jnp.zeros((micro, buses, width), jnp.bfloat16)

    def forward_step(senders, step, carry):
        incoming, stashed, upstream_stash = carry
        slot_raw = step - rank
        active = (slot_raw >= 0) & (slot_raw < micro)
        slot = jnp.clip(slot_raw, 0, micro - 1)
        first_state = lax.dynamic_index_in_dim(states, slot, 0, keepdims=True)
        source = jnp.where(rank == 0, first_state, incoming[None])
        allowed_slot = lax.dynamic_index_in_dim(allowed, slot, 0, keepdims=True)

        def forward_do_work(stash_in, upstream_in):
            output, kept_parts = layer_forward(source, weight, allowed_slot)
            stash_out = tuple(
                (
                    lax.dynamic_update_index_in_dim(whole_array, new_piece, slot, 0)
                    for whole_array, new_piece in zip(stash_in, kept_parts)
                )
            )
            predicted = jnp.sum(output.astype(jnp.float32) * readout, axis=-1)
            misfit = predicted - lax.dynamic_index_in_dim(targets, slot, 0, keepdims=True)
            cotangent = (misfit[..., None] * readout).astype(jnp.bfloat16)
            upstream_out = lax.dynamic_update_index_in_dim(upstream_in, cotangent, slot, 0)
            return (output[0], stash_out, upstream_out)

        def forward_no_work(stash_in, upstream_in):
            return (zero_rows, stash_in, upstream_in)

        output, stashed, upstream_stash = lax.cond(
            active, forward_do_work, forward_no_work, stashed, upstream_stash
        )
        passed = passed_along(output, "section", 1, senders)
        return (passed, stashed, upstream_stash)

    carry = (zero_rows, stash_init, upstream_init)
    for lo, hi in phases(sections, micro):
        senders = [r for r in range(sections - 1) if any(0 <= t - r < micro for t in range(lo, hi))]
        carry = lax.fori_loop(lo, hi, functools.partial(forward_step, senders), carry)
    unused_rows, stashed, upstream_stash = carry
    totals_init = jnp.zeros((micro, buses, width), jnp.bfloat16)

    def backward_step(senders, step, carry):
        incoming, collected = carry
        slot_raw = step - (sections - 1 - rank)
        active = (slot_raw >= 0) & (slot_raw < micro)
        slot = jnp.clip(slot_raw, 0, micro - 1)
        last_grad = lax.dynamic_index_in_dim(upstream_stash, slot, 0, keepdims=True)
        upstream = jnp.where(rank == sections - 1, last_grad, incoming[None])
        allowed_slot = lax.dynamic_index_in_dim(allowed, slot, 0, keepdims=True)

        def backward_do_work(collected_in):
            kept_parts = tuple(
                (
                    lax.dynamic_index_in_dim(whole_array, slot, 0, keepdims=True)
                    for whole_array in stashed
                )
            )
            lower, value_total = layer_backward(upstream, weight, allowed_slot, kept_parts)
            collected_out = lax.dynamic_update_index_in_dim(collected_in, value_total, slot, 0)
            return (lower[0], collected_out)

        def backward_no_work(collected_in):
            return (zero_rows, collected_in)

        lower, collected = lax.cond(active, backward_do_work, backward_no_work, collected)
        passed = passed_along(lower, "section", -1, senders)
        return (passed, collected)

    cores = lax.axis_size("core")
    ys = lax.axis_size("y")
    zs = lax.axis_size("z")
    core = lax.axis_index("core")
    swap = [(0, 1), (1, 0)]
    rows_each = width // (zs * ys * cores)

    def prepare(scaled):
        normed_all = scaled.astype(jnp.bfloat16).reshape(micro * buses, zs, ys, cores, rows_each)
        normed_all = jnp.transpose(normed_all, (3, 2, 1, 4, 0)).reshape(
            cores, width // cores, micro * buses
        )
        return (
            lax.dynamic_index_in_dim(normed_all, core, 0, keepdims=False),
            lax.dynamic_index_in_dim(normed_all, 1 - core, 0, keepdims=False),
        )

    def skip(scaled):
        empty = jnp.zeros((width // cores, micro * buses), jnp.bfloat16)
        return (empty, empty)

    early = rank < sections // 2
    prepared = lax.cond(early, prepare, skip, stashed[0])
    prepared, carry = lax.optimization_barrier((prepared, (zero_rows, totals_init)))
    for lo, hi in phases(sections, micro):
        senders = [
            r
            for r in range(1, sections)
            if any(0 <= t - (sections - 1 - r) < micro for t in range(lo, hi))
        ]
        carry = lax.fori_loop(lo, hi, functools.partial(backward_step, senders), carry)
    unused_rows, collected = carry
    mine, sent = lax.cond(early, lambda p, s: p, lambda p, s: prepare(s), prepared, stashed[0])
    left = jnp.concatenate([mine, lax.ppermute(sent, "core", swap)], axis=1)
    own = collected.reshape(micro * buses, width)
    right = jnp.concatenate([own, lax.ppermute(own, "core", swap)], axis=0)
    half = jnp.dot(left, right, preferred_element_type=jnp.float32)
    summed = scatter_sum(scatter_sum(half, "y"), "z")
    return summed[None]


def solution(mesh):
    sections, dp = mesh.devices.shape
    split = Mesh(mesh.devices.reshape(sections, 4, dp // 8, 2), ("section", "z", "y", "core"))
    rows = ("z", "y", "core")
    in_specs = (
        P(rows, None, None),
        P(rows, None),
        P(rows, None),
        P(),
        P("section", None, None),
        P(),
    )
    out_specs = P("section", rows, None)
    return jax.shard_map(
        per_device, mesh=split, in_specs=in_specs, out_specs=out_specs, check_vma=False
    )
```

```python
import functools

import jax
import jax.numpy as jnp
from jax import lax
from jax.sharding import Mesh, PartitionSpec as P

HEADS = 16
BLOCK = 32


epsilon = 1e-05


def passed_along(block, axis, distance, senders):
    return lax.ppermute(block, axis, [(i, i + distance) for i in senders])


def phases(sections, micro):
    middle = sections // 2
    bounds = [0, middle - 1, middle - 1 + micro, sections + micro - 1]
    return [(lo, hi) for lo, hi in zip(bounds[:-1], bounds[1:]) if hi > lo]


def scatter_sum(block, axis):
    count = lax.axis_size(axis)
    me = lax.axis_index(axis)
    pieces = block.reshape(count, block.shape[0] // count, block.shape[1])
    total = lax.dynamic_index_in_dim(pieces, me, 0, keepdims=False)
    for shift in range(1, count):
        sent = lax.dynamic_index_in_dim(pieces, (me + shift) % count, 0, keepdims=False)
        route = [(i, (i + shift) % count) for i in range(count)]
        received = lax.ppermute(sent.astype(jnp.bfloat16), axis, route)
        total = total + received.astype(jnp.float32)
    return total


def allowed_pairs(pattern, outage):
    buses = outage.shape[-1]
    block_count = buses // BLOCK
    block_ids = jnp.arange(block_count, dtype=jnp.int32)
    pair_hits = (pattern[:, 0][None, None, :] == block_ids[:, None, None]) & (
        pattern[:, 1][None, None, :] == block_ids[None, :, None]
    )
    block_table = jnp.max(pair_hits.astype(jnp.float32), axis=2)
    member = ((jnp.arange(buses, dtype=jnp.int32) // BLOCK)[:, None] == block_ids[None, :]).astype(
        jnp.float32
    )
    pair_mask = jnp.dot(
        jnp.dot(member, block_table, precision=lax.Precision.HIGHEST),
        member.T,
        precision=lax.Precision.HIGHEST,
    )
    in_service = outage.astype(jnp.float32)
    self_mask = jnp.eye(buses, dtype=jnp.float32)
    return pair_mask[None] * jnp.maximum(in_service[:, None, :], self_mask[None])


def layer_forward(hidden, weight, allowed):
    num_states, buses, width = hidden.shape
    split_shape = (num_states, buses, HEADS, width // HEADS)
    hidden_f = hidden.astype(jnp.float32)
    centred = hidden_f - jnp.mean(hidden_f, axis=-1, keepdims=True)
    inverse_std = lax.rsqrt(jnp.mean(centred * centred, axis=-1, keepdims=True) + epsilon)
    scaled = centred * inverse_std
    normed = scaled.astype(jnp.bfloat16)
    values_b = (
        jnp.dot(normed.reshape(-1, width), weight, preferred_element_type=jnp.float32)
        .astype(jnp.bfloat16)
        .reshape(split_shape)
    )
    features = (jax.nn.elu(values_b.astype(jnp.float32)) + 1.0).astype(jnp.bfloat16)
    kernel = (
        jnp.einsum("nihc,njhc->nhij", features, features, preferred_element_type=jnp.float32)
        * allowed[:, None]
    )
    totals = jnp.sum(kernel, axis=-1, keepdims=True)
    attention = kernel / totals
    attention_b = attention.astype(jnp.bfloat16)
    gathered = jnp.einsum(
        "nhij,njhc->nihc", attention_b, values_b, preferred_element_type=jnp.float32
    )
    output = (hidden_f + gathered.reshape(num_states, buses, width)).astype(jnp.bfloat16)
    return (output, (scaled, inverse_std, values_b, attention, totals))


def layer_backward(upstream, weight, allowed, kept_parts):
    scaled, inverse_std, values_b, attention, totals = kept_parts
    num_states, buses, width = upstream.shape
    grad_f = upstream.astype(jnp.float32)
    grad_heads = upstream.reshape(values_b.shape)
    values_f = values_b.astype(jnp.float32)
    features = (jax.nn.elu(values_f) + 1.0).astype(jnp.bfloat16)
    attention_b = attention.astype(jnp.bfloat16)
    value_grad = jnp.einsum(
        "nhij,nihc->njhc", attention_b, grad_heads, preferred_element_type=jnp.float32
    )
    attention_grad = jnp.einsum(
        "nihc,njhc->nhij", grad_heads, values_b, preferred_element_type=jnp.float32
    )
    row_terms = jnp.sum(attention_grad * attention, axis=-1, keepdims=True)
    kernel_grad = ((attention_grad - row_terms) / totals * allowed[:, None]).astype(jnp.bfloat16)
    feature_grad = jnp.einsum(
        "nhij,njhc->nihc", kernel_grad, features, preferred_element_type=jnp.float32
    )
    feature_grad = feature_grad + jnp.einsum(
        "nhji,njhc->nihc", kernel_grad, features, preferred_element_type=jnp.float32
    )
    slope = jnp.where(values_f > 0.0, 1.0, jnp.exp(jnp.minimum(values_f, 0.0)))
    value_total = (
        (value_grad + feature_grad * slope).astype(jnp.bfloat16).reshape(num_states, buses, width)
    )
    normed_grad = lax.dot_general(
        value_total.reshape(-1, width),
        weight,
        (((1,), (1,)), ((), ())),
        preferred_element_type=jnp.float32,
    ).reshape(num_states, buses, width)
    mean_grad = jnp.mean(normed_grad, axis=-1, keepdims=True)
    mean_cross = jnp.mean(normed_grad * scaled, axis=-1, keepdims=True)
    lower = (grad_f + inverse_std * (normed_grad - mean_grad - scaled * mean_cross)).astype(
        jnp.bfloat16
    )
    return (lower, value_total)


def per_device(states, outage, targets, pattern, weights, readout):
    sections = lax.axis_size("section")
    rank = lax.axis_index("section")
    micro, buses, width = states.shape
    weight = weights[0]
    allowed = allowed_pairs(pattern, outage)
    head_size = width // HEADS
    steps_total = sections + micro - 1
    zero_rows = jnp.zeros((buses, width), jnp.bfloat16)
    stash_init = (
        jnp.zeros((micro, buses, width), jnp.float32),
        jnp.zeros((micro, buses, 1), jnp.float32),
        jnp.zeros((micro, buses, HEADS, head_size), jnp.bfloat16),
        jnp.zeros((micro, HEADS, buses, buses), jnp.float32),
        jnp.zeros((micro, HEADS, buses, 1), jnp.float32),
    )
    upstream_init = jnp.zeros((micro, buses, width), jnp.bfloat16)

    def forward_step(senders, step, carry):
        incoming, stashed, upstream_stash = carry
        slot_raw = step - rank
        active = (slot_raw >= 0) & (slot_raw < micro)
        slot = jnp.clip(slot_raw, 0, micro - 1)
        first_state = lax.dynamic_index_in_dim(states, slot, 0, keepdims=True)
        source = jnp.where(rank == 0, first_state, incoming[None])
        allowed_slot = lax.dynamic_index_in_dim(allowed, slot, 0, keepdims=True)

        def forward_do_work(stash_in, upstream_in):
            output, kept_parts = layer_forward(source, weight, allowed_slot)
            stash_out = tuple(
                (
                    lax.dynamic_update_index_in_dim(whole_array, new_piece, slot, 0)
                    for whole_array, new_piece in zip(stash_in, kept_parts)
                )
            )

            def loss_grad(upstream_kept):
                predicted = jnp.sum(output.astype(jnp.float32) * readout, axis=-1)
                misfit = predicted - lax.dynamic_index_in_dim(targets, slot, 0, keepdims=True)
                cotangent = (misfit[..., None] * readout).astype(jnp.bfloat16)
                return lax.dynamic_update_index_in_dim(upstream_kept, cotangent, slot, 0)

            upstream_out = lax.cond(
                rank == sections - 1, loss_grad, lambda upstream_kept: upstream_kept, upstream_in
            )
            return (output[0], stash_out, upstream_out)

        def forward_no_work(stash_in, upstream_in):
            return (zero_rows, stash_in, upstream_in)

        output, stashed, upstream_stash = lax.cond(
            active, forward_do_work, forward_no_work, stashed, upstream_stash
        )
        passed = passed_along(output, "section", 1, senders)
        return (passed, stashed, upstream_stash)

    carry = (zero_rows, stash_init, upstream_init)
    for lo, hi in phases(sections, micro):
        senders = [r for r in range(sections - 1) if any(0 <= t - r < micro for t in range(lo, hi))]
        carry = lax.fori_loop(lo, hi, functools.partial(forward_step, senders), carry)
    unused_rows, stashed, upstream_stash = carry
    totals_init = jnp.zeros((micro, buses, width), jnp.bfloat16)

    def backward_step(senders, step, carry):
        incoming, collected = carry
        slot_raw = step - (sections - 1 - rank)
        active = (slot_raw >= 0) & (slot_raw < micro)
        slot = jnp.clip(slot_raw, 0, micro - 1)
        last_grad = lax.dynamic_index_in_dim(upstream_stash, slot, 0, keepdims=True)
        upstream = jnp.where(rank == sections - 1, last_grad, incoming[None])
        allowed_slot = lax.dynamic_index_in_dim(allowed, slot, 0, keepdims=True)

        def backward_do_work(collected_in):
            kept_parts = tuple(
                (
                    lax.dynamic_index_in_dim(whole_array, slot, 0, keepdims=True)
                    for whole_array in stashed
                )
            )
            lower, value_total = layer_backward(upstream, weight, allowed_slot, kept_parts)
            collected_out = lax.dynamic_update_index_in_dim(collected_in, value_total, slot, 0)
            return (lower[0], collected_out)

        def backward_no_work(collected_in):
            return (zero_rows, collected_in)

        lower, collected = lax.cond(active, backward_do_work, backward_no_work, collected)
        passed = passed_along(lower, "section", -1, senders)
        return (passed, collected)

    cores = lax.axis_size("core")
    ys = lax.axis_size("y")
    zs = lax.axis_size("z")
    core = lax.axis_index("core")
    swap = [(0, 1), (1, 0)]
    rows_each = width // (zs * ys * cores)
    normed_all = stashed[0].astype(jnp.bfloat16).reshape(micro * buses, zs, ys, cores, rows_each)
    normed_all = jnp.transpose(normed_all, (3, 2, 1, 4, 0)).reshape(
        cores, width // cores, micro * buses
    )
    mine = lax.dynamic_index_in_dim(normed_all, core, 0, keepdims=False)
    theirs = lax.ppermute(
        lax.dynamic_index_in_dim(normed_all, 1 - core, 0, keepdims=False), "core", swap
    )
    left = jnp.concatenate([mine, theirs], axis=1)
    carry = (zero_rows, totals_init)
    for lo, hi in phases(sections, micro):
        senders = [
            r
            for r in range(1, sections)
            if any(0 <= t - (sections - 1 - r) < micro for t in range(lo, hi))
        ]
        carry = lax.fori_loop(lo, hi, functools.partial(backward_step, senders), carry)
    unused_rows, collected = carry
    own = collected.reshape(micro * buses, width)
    right = jnp.concatenate([own, lax.ppermute(own, "core", swap)], axis=0)
    half = jnp.dot(left, right, preferred_element_type=jnp.float32)
    summed = scatter_sum(scatter_sum(half, "y"), "z")
    return summed[None]


def solution(mesh):
    sections, dp = mesh.devices.shape
    split = Mesh(mesh.devices.reshape(sections, 4, dp // 8, 2), ("section", "z", "y", "core"))
    rows = ("z", "y", "core")
    in_specs = (
        P(rows, None, None),
        P(rows, None),
        P(rows, None),
        P(),
        P("section", None, None),
        P(),
    )
    out_specs = P("section", rows, None)
    return jax.shard_map(
        per_device, mesh=split, in_specs=in_specs, out_specs=out_specs, check_vma=False
    )
```

```python
import functools

import jax
import jax.numpy as jnp
from jax import lax
from jax.sharding import Mesh, PartitionSpec as P

HEADS = 16
BLOCK = 32


epsilon = 1e-05


def passed_along(block, axis, distance, senders):
    return lax.ppermute(block, axis, [(i, i + distance) for i in senders])


def phases(sections, micro):
    middle = sections // 2
    bounds = [0, middle - 1, middle - 1 + micro, sections + micro - 1]
    return [(lo, hi) for lo, hi in zip(bounds[:-1], bounds[1:]) if hi > lo]


def scatter_sum(block, axis):
    count = lax.axis_size(axis)
    me = lax.axis_index(axis)
    pieces = block.reshape(count, block.shape[0] // count, block.shape[1])
    total = lax.dynamic_index_in_dim(pieces, me, 0, keepdims=False)
    for shift in range(1, count):
        sent = lax.dynamic_index_in_dim(pieces, (me + shift) % count, 0, keepdims=False)
        route = [(i, (i + shift) % count) for i in range(count)]
        received = lax.ppermute(sent.astype(jnp.bfloat16), axis, route)
        total = total + received.astype(jnp.float32)
    return total


def allowed_pairs(pattern, outage):
    buses = outage.shape[-1]
    block_count = buses // BLOCK
    block_ids = jnp.arange(block_count, dtype=jnp.int32)
    pair_hits = (pattern[:, 0][None, None, :] == block_ids[:, None, None]) & (
        pattern[:, 1][None, None, :] == block_ids[None, :, None]
    )
    block_table = jnp.max(pair_hits.astype(jnp.float32), axis=2)
    member = ((jnp.arange(buses, dtype=jnp.int32) // BLOCK)[:, None] == block_ids[None, :]).astype(
        jnp.float32
    )
    pair_mask = jnp.dot(
        jnp.dot(member, block_table, precision=lax.Precision.HIGHEST),
        member.T,
        precision=lax.Precision.HIGHEST,
    )
    in_service = outage.astype(jnp.float32)
    self_mask = jnp.eye(buses, dtype=jnp.float32)
    return pair_mask[None] * jnp.maximum(in_service[:, None, :], self_mask[None])


def layer_forward(hidden, weight, allowed):
    num_states, buses, width = hidden.shape
    split_shape = (num_states, buses, HEADS, width // HEADS)
    hidden_f = hidden.astype(jnp.float32)
    centred = hidden_f - jnp.mean(hidden_f, axis=-1, keepdims=True)
    inverse_std = lax.rsqrt(jnp.mean(centred * centred, axis=-1, keepdims=True) + epsilon)
    scaled = centred * inverse_std
    normed = scaled.astype(jnp.bfloat16)
    values_b = (
        jnp.dot(normed.reshape(-1, width), weight, preferred_element_type=jnp.float32)
        .astype(jnp.bfloat16)
        .reshape(split_shape)
    )
    features = (jax.nn.elu(values_b.astype(jnp.float32)) + 1.0).astype(jnp.bfloat16)
    kernel = (
        jnp.einsum("nihc,njhc->nhij", features, features, preferred_element_type=jnp.float32)
        * allowed[:, None]
    )
    totals = jnp.sum(kernel, axis=-1, keepdims=True)
    attention = kernel / totals
    attention_b = attention.astype(jnp.bfloat16)
    gathered = jnp.einsum(
        "nhij,njhc->nihc", attention_b, values_b, preferred_element_type=jnp.float32
    )
    output = (hidden_f + gathered.reshape(num_states, buses, width)).astype(jnp.bfloat16)
    return (output, (scaled, inverse_std, values_b, attention, totals))


def layer_backward(upstream, weight, allowed, kept_parts):
    scaled, inverse_std, values_b, attention, totals = kept_parts
    num_states, buses, width = upstream.shape
    grad_f = upstream.astype(jnp.float32)
    grad_heads = upstream.reshape(values_b.shape)
    values_f = values_b.astype(jnp.float32)
    features = (jax.nn.elu(values_f) + 1.0).astype(jnp.bfloat16)
    attention_b = attention.astype(jnp.bfloat16)
    value_grad = jnp.einsum(
        "nhij,nihc->njhc", attention_b, grad_heads, preferred_element_type=jnp.float32
    )
    attention_grad = jnp.einsum(
        "nihc,njhc->nhij", grad_heads, values_b, preferred_element_type=jnp.float32
    )
    row_terms = jnp.sum(attention_grad * attention, axis=-1, keepdims=True)
    kernel_grad = ((attention_grad - row_terms) / totals * allowed[:, None]).astype(jnp.bfloat16)
    feature_grad = jnp.einsum(
        "nhij,njhc->nihc", kernel_grad, features, preferred_element_type=jnp.float32
    )
    feature_grad = feature_grad + jnp.einsum(
        "nhji,njhc->nihc", kernel_grad, features, preferred_element_type=jnp.float32
    )
    slope = jnp.where(values_f > 0.0, 1.0, jnp.exp(jnp.minimum(values_f, 0.0)))
    value_total = (
        (value_grad + feature_grad * slope).astype(jnp.bfloat16).reshape(num_states, buses, width)
    )
    normed_grad = lax.dot_general(
        value_total.reshape(-1, width),
        weight,
        (((1,), (1,)), ((), ())),
        preferred_element_type=jnp.float32,
    ).reshape(num_states, buses, width)
    mean_grad = jnp.mean(normed_grad, axis=-1, keepdims=True)
    mean_cross = jnp.mean(normed_grad * scaled, axis=-1, keepdims=True)
    lower = (grad_f + inverse_std * (normed_grad - mean_grad - scaled * mean_cross)).astype(
        jnp.bfloat16
    )
    return (lower, value_total)


def per_device(states, outage, targets, pattern, weights, readout):
    sections = lax.axis_size("section")
    rank = lax.axis_index("section")
    micro, buses, width = states.shape
    weight = weights[0]
    allowed = allowed_pairs(pattern, outage)
    head_size = width // HEADS
    steps_total = sections + micro - 1
    zero_rows = jnp.zeros((buses, width), jnp.bfloat16)
    stash_init = (
        jnp.zeros((micro, buses, width), jnp.float32),
        jnp.zeros((micro, buses, 1), jnp.float32),
        jnp.zeros((micro, buses, HEADS, head_size), jnp.bfloat16),
        jnp.zeros((micro, HEADS, buses, buses), jnp.float32),
        jnp.zeros((micro, HEADS, buses, 1), jnp.float32),
    )
    upstream_init = jnp.zeros((micro, buses, width), jnp.bfloat16)

    def forward_step(senders, step, carry):
        incoming, stashed, upstream_stash = carry
        slot_raw = step - rank
        active = (slot_raw >= 0) & (slot_raw < micro)
        slot = jnp.clip(slot_raw, 0, micro - 1)
        first_state = lax.dynamic_index_in_dim(states, slot, 0, keepdims=True)
        source = jnp.where(rank == 0, first_state, incoming[None])
        allowed_slot = lax.dynamic_index_in_dim(allowed, slot, 0, keepdims=True)

        def forward_do_work(stash_in, upstream_in):
            output, kept_parts = layer_forward(source, weight, allowed_slot)
            stash_out = tuple(
                (
                    lax.dynamic_update_index_in_dim(whole_array, new_piece, slot, 0)
                    for whole_array, new_piece in zip(stash_in, kept_parts)
                )
            )
            predicted = jnp.sum(output.astype(jnp.float32) * readout, axis=-1)
            misfit = predicted - lax.dynamic_index_in_dim(targets, slot, 0, keepdims=True)
            cotangent = (misfit[..., None] * readout).astype(jnp.bfloat16)
            upstream_out = lax.dynamic_update_index_in_dim(upstream_in, cotangent, slot, 0)
            return (output[0], stash_out, upstream_out)

        def forward_no_work(stash_in, upstream_in):
            return (zero_rows, stash_in, upstream_in)

        output, stashed, upstream_stash = lax.cond(
            active, forward_do_work, forward_no_work, stashed, upstream_stash
        )
        passed = passed_along(output, "section", 1, senders)
        return (passed, stashed, upstream_stash)

    carry = (zero_rows, stash_init, upstream_init)
    for lo, hi in phases(sections, micro):
        senders = [r for r in range(sections - 1) if any(0 <= t - r < micro for t in range(lo, hi))]
        carry = lax.fori_loop(lo, hi, functools.partial(forward_step, senders), carry)
    unused_rows, stashed, upstream_stash = carry
    totals_init = jnp.zeros((micro, buses, width), jnp.bfloat16)

    def backward_step(senders, step, carry):
        incoming, collected = carry
        slot_raw = step - (sections - 1 - rank)
        active = (slot_raw >= 0) & (slot_raw < micro)
        slot = jnp.clip(slot_raw, 0, micro - 1)
        last_grad = lax.dynamic_index_in_dim(upstream_stash, slot, 0, keepdims=True)
        upstream = jnp.where(rank == sections - 1, last_grad, incoming[None])
        allowed_slot = lax.dynamic_index_in_dim(allowed, slot, 0, keepdims=True)

        def backward_do_work(collected_in):
            kept_parts = tuple(
                (
                    lax.dynamic_index_in_dim(whole_array, slot, 0, keepdims=True)
                    for whole_array in stashed
                )
            )
            lower, value_total = layer_backward(upstream, weight, allowed_slot, kept_parts)
            collected_out = lax.dynamic_update_index_in_dim(collected_in, value_total, slot, 0)
            return (lower[0], collected_out)

        def backward_no_work(collected_in):
            return (zero_rows, collected_in)

        lower, collected = lax.cond(active, backward_do_work, backward_no_work, collected)
        passed = passed_along(lower, "section", -1, senders)
        return (passed, collected)

    cores = lax.axis_size("core")
    ys = lax.axis_size("y")
    zs = lax.axis_size("z")
    core = lax.axis_index("core")
    swap = [(0, 1), (1, 0)]
    rows_each = width // (zs * ys * cores)
    normed_all = stashed[0].astype(jnp.bfloat16).reshape(micro * buses, zs, ys, cores, rows_each)
    normed_all = jnp.transpose(normed_all, (3, 2, 1, 4, 0)).reshape(
        cores, width // cores, micro * buses
    )
    mine = lax.dynamic_index_in_dim(normed_all, core, 0, keepdims=False)
    theirs = lax.ppermute(
        lax.dynamic_index_in_dim(normed_all, 1 - core, 0, keepdims=False), "core", swap
    )
    left = jnp.concatenate([mine, theirs], axis=1)
    carry = (zero_rows, totals_init)
    for lo, hi in phases(sections, micro):
        senders = [
            r
            for r in range(1, sections)
            if any(0 <= t - (sections - 1 - r) < micro for t in range(lo, hi))
        ]
        carry = lax.fori_loop(lo, hi, functools.partial(backward_step, senders), carry)
    unused_rows, collected = carry
    own = collected.reshape(micro * buses, width)
    right = jnp.concatenate([own, lax.ppermute(own, "core", swap)], axis=0)
    half = jnp.dot(left, right, preferred_element_type=jnp.float32)
    columns = width // 2
    along_y = scatter_sum(scatter_sum(half[:, :columns], "y"), "z")
    by_z = half[:, columns:].reshape(ys, zs, rows_each, columns)
    by_z = jnp.swapaxes(by_z, 0, 1).reshape(ys * zs * rows_each, columns)
    along_z = scatter_sum(scatter_sum(by_z, "z"), "y")
    summed = jnp.concatenate([along_y, along_z], axis=1)
    return summed[None]


def solution(mesh):
    sections, dp = mesh.devices.shape
    split = Mesh(mesh.devices.reshape(sections, 4, dp // 8, 2), ("section", "z", "y", "core"))
    rows = ("z", "y", "core")
    in_specs = (
        P(rows, None, None),
        P(rows, None),
        P(rows, None),
        P(),
        P("section", None, None),
        P(),
    )
    out_specs = P("section", rows, None)
    return jax.shard_map(
        per_device, mesh=split, in_specs=in_specs, out_specs=out_specs, check_vma=False
    )
```

```python
import functools

import jax
import jax.numpy as jnp
from jax import lax
from jax.sharding import Mesh, PartitionSpec as P

HEADS = 16
BLOCK = 32


epsilon = 1e-05


def passed_along(block, axis, distance, senders):
    return lax.ppermute(block, axis, [(i, i + distance) for i in senders])


def phases(sections, micro):
    middle = sections // 2
    bounds = [0, middle - 1, middle - 1 + micro, sections + micro - 1]
    return [(lo, hi) for lo, hi in zip(bounds[:-1], bounds[1:]) if hi > lo]


def scatter_sum(block, axis):
    count = lax.axis_size(axis)
    me = lax.axis_index(axis)
    pieces = block.reshape(count, block.shape[0] // count, block.shape[1])
    total = lax.dynamic_index_in_dim(pieces, me, 0, keepdims=False)
    for shift in range(1, count):
        sent = lax.dynamic_index_in_dim(pieces, (me + shift) % count, 0, keepdims=False)
        route = [(i, (i + shift) % count) for i in range(count)]
        received = lax.ppermute(sent.astype(jnp.bfloat16), axis, route)
        total = total + received.astype(jnp.float32)
    return total


def allowed_pairs(pattern, outage):
    buses = outage.shape[-1]
    block_count = buses // BLOCK
    block_ids = jnp.arange(block_count, dtype=jnp.int32)
    pair_hits = (pattern[:, 0][None, None, :] == block_ids[:, None, None]) & (
        pattern[:, 1][None, None, :] == block_ids[None, :, None]
    )
    block_table = jnp.max(pair_hits.astype(jnp.float32), axis=2)
    member = ((jnp.arange(buses, dtype=jnp.int32) // BLOCK)[:, None] == block_ids[None, :]).astype(
        jnp.float32
    )
    pair_mask = jnp.dot(
        jnp.dot(member, block_table, precision=lax.Precision.HIGHEST),
        member.T,
        precision=lax.Precision.HIGHEST,
    )
    in_service = outage.astype(jnp.float32)
    self_mask = jnp.eye(buses, dtype=jnp.float32)
    return pair_mask[None] * jnp.maximum(in_service[:, None, :], self_mask[None])


def layer_forward(hidden, weight, allowed):
    num_states, buses, width = hidden.shape
    split_shape = (num_states, buses, HEADS, width // HEADS)
    hidden_f = hidden.astype(jnp.float32)
    centred = hidden_f - jnp.mean(hidden_f, axis=-1, keepdims=True)
    inverse_std = lax.rsqrt(jnp.mean(centred * centred, axis=-1, keepdims=True) + epsilon)
    scaled = centred * inverse_std
    normed = scaled.astype(jnp.bfloat16)
    values_b = (
        jnp.dot(normed.reshape(-1, width), weight, preferred_element_type=jnp.float32)
        .astype(jnp.bfloat16)
        .reshape(split_shape)
    )
    features = (jax.nn.elu(values_b.astype(jnp.float32)) + 1.0).astype(jnp.bfloat16)
    kernel = (
        jnp.einsum("nihc,njhc->nhij", features, features, preferred_element_type=jnp.float32)
        * allowed[:, None]
    )
    totals = jnp.sum(kernel, axis=-1, keepdims=True)
    attention = kernel / totals
    attention_b = attention.astype(jnp.bfloat16)
    gathered = jnp.einsum(
        "nhij,njhc->nihc", attention_b, values_b, preferred_element_type=jnp.float32
    )
    output = (hidden_f + gathered.reshape(num_states, buses, width)).astype(jnp.bfloat16)
    return (output, (scaled, inverse_std, values_b, attention, totals))


def layer_backward(upstream, weight, allowed, kept_parts):
    scaled, inverse_std, values_b, attention, totals = kept_parts
    num_states, buses, width = upstream.shape
    grad_f = upstream.astype(jnp.float32)
    grad_heads = upstream.reshape(values_b.shape)
    values_f = values_b.astype(jnp.float32)
    features = (jax.nn.elu(values_f) + 1.0).astype(jnp.bfloat16)
    attention_b = attention.astype(jnp.bfloat16)
    value_grad = jnp.einsum(
        "nhij,nihc->njhc", attention_b, grad_heads, preferred_element_type=jnp.float32
    )
    attention_grad = jnp.einsum(
        "nihc,njhc->nhij", grad_heads, values_b, preferred_element_type=jnp.float32
    )
    row_terms = jnp.sum(attention_grad * attention, axis=-1, keepdims=True)
    kernel_grad = ((attention_grad - row_terms) / totals * allowed[:, None]).astype(jnp.bfloat16)
    feature_grad = jnp.einsum(
        "nhij,njhc->nihc", kernel_grad, features, preferred_element_type=jnp.float32
    )
    feature_grad = feature_grad + jnp.einsum(
        "nhji,njhc->nihc", kernel_grad, features, preferred_element_type=jnp.float32
    )
    slope = jnp.where(values_f > 0.0, 1.0, jnp.exp(jnp.minimum(values_f, 0.0)))
    value_total = (
        (value_grad + feature_grad * slope).astype(jnp.bfloat16).reshape(num_states, buses, width)
    )
    normed_grad = lax.dot_general(
        value_total.reshape(-1, width),
        weight,
        (((1,), (1,)), ((), ())),
        preferred_element_type=jnp.float32,
    ).reshape(num_states, buses, width)
    mean_grad = jnp.mean(normed_grad, axis=-1, keepdims=True)
    mean_cross = jnp.mean(normed_grad * scaled, axis=-1, keepdims=True)
    lower = (grad_f + inverse_std * (normed_grad - mean_grad - scaled * mean_cross)).astype(
        jnp.bfloat16
    )
    return (lower, value_total)


def per_device(states, outage, targets, pattern, weights, readout):
    sections = lax.axis_size("section")
    rank = lax.axis_index("section")
    micro, buses, width = states.shape
    weight = weights[0]
    allowed = allowed_pairs(pattern, outage)
    head_size = width // HEADS
    steps_total = sections + micro - 1
    zero_rows = jnp.zeros((buses, width), jnp.bfloat16)
    stash_init = (
        jnp.zeros((micro, buses, width), jnp.float32),
        jnp.zeros((micro, buses, 1), jnp.float32),
        jnp.zeros((micro, buses, HEADS, head_size), jnp.bfloat16),
        jnp.zeros((micro, HEADS, buses, buses), jnp.float32),
        jnp.zeros((micro, HEADS, buses, 1), jnp.float32),
    )
    upstream_init = jnp.zeros((micro, buses, width), jnp.bfloat16)

    def forward_step(senders, step, carry):
        incoming, stashed, upstream_stash = carry
        slot_raw = step - rank
        active = (slot_raw >= 0) & (slot_raw < micro)
        slot = jnp.clip(slot_raw, 0, micro - 1)
        first_state = lax.dynamic_index_in_dim(states, slot, 0, keepdims=True)
        source = jnp.where(rank == 0, first_state, incoming[None])
        allowed_slot = lax.dynamic_index_in_dim(allowed, slot, 0, keepdims=True)

        def forward_do_work(stash_in, upstream_in):
            output, kept_parts = layer_forward(source, weight, allowed_slot)
            stash_out = tuple(
                (
                    lax.dynamic_update_index_in_dim(whole_array, new_piece, slot, 0)
                    for whole_array, new_piece in zip(stash_in, kept_parts)
                )
            )
            predicted = jnp.sum(output.astype(jnp.float32) * readout, axis=-1)
            misfit = predicted - lax.dynamic_index_in_dim(targets, slot, 0, keepdims=True)
            cotangent = (misfit[..., None] * readout).astype(jnp.bfloat16)
            upstream_out = lax.dynamic_update_index_in_dim(upstream_in, cotangent, slot, 0)
            return (output[0], stash_out, upstream_out)

        def forward_no_work(stash_in, upstream_in):
            return (zero_rows, stash_in, upstream_in)

        output, stashed, upstream_stash = lax.cond(
            active, forward_do_work, forward_no_work, stashed, upstream_stash
        )
        passed = passed_along(output, "section", 1, senders)
        return (passed, stashed, upstream_stash)

    carry = (zero_rows, stash_init, upstream_init)
    for lo, hi in phases(sections, micro):
        senders = [r for r in range(sections - 1) if any(0 <= t - r < micro for t in range(lo, hi))]
        carry = lax.fori_loop(lo, hi, functools.partial(forward_step, senders), carry)
    unused_rows, stashed, upstream_stash = carry
    totals_init = jnp.zeros((micro, buses, width), jnp.bfloat16)

    def backward_step(senders, step, carry):
        incoming, collected = carry
        slot_raw = step - (sections - 1 - rank)
        active = (slot_raw >= 0) & (slot_raw < micro)
        slot = jnp.clip(slot_raw, 0, micro - 1)
        last_grad = lax.dynamic_index_in_dim(upstream_stash, slot, 0, keepdims=True)
        upstream = jnp.where(rank == sections - 1, last_grad, incoming[None])
        allowed_slot = lax.dynamic_index_in_dim(allowed, slot, 0, keepdims=True)

        def backward_do_work(collected_in):
            kept_parts = tuple(
                (
                    lax.dynamic_index_in_dim(whole_array, slot, 0, keepdims=True)
                    for whole_array in stashed
                )
            )
            lower, value_total = layer_backward(upstream, weight, allowed_slot, kept_parts)
            collected_out = lax.dynamic_update_index_in_dim(collected_in, value_total, slot, 0)
            return (lower[0], collected_out)

        def backward_no_work(collected_in):
            return (zero_rows, collected_in)

        lower, collected = lax.cond(active, backward_do_work, backward_no_work, collected)
        passed = passed_along(lower, "section", -1, senders)
        return (passed, collected)

    cores = lax.axis_size("core")
    ys = lax.axis_size("y")
    zs = lax.axis_size("z")
    core = lax.axis_index("core")
    swap = [(0, 1), (1, 0)]
    rows_each = width // (zs * ys * cores)
    normed_all = stashed[0].astype(jnp.bfloat16).reshape(micro * buses, zs, ys, cores, rows_each)
    normed_all = jnp.transpose(normed_all, (3, 2, 1, 4, 0)).reshape(
        cores, width // cores, micro * buses
    )
    mine = lax.dynamic_index_in_dim(normed_all, core, 0, keepdims=False)
    theirs = lax.ppermute(
        lax.dynamic_index_in_dim(normed_all, 1 - core, 0, keepdims=False), "core", swap
    )
    carry = (zero_rows, totals_init)
    for lo, hi in phases(sections, micro):
        senders = [
            r
            for r in range(1, sections)
            if any(0 <= t - (sections - 1 - r) < micro for t in range(lo, hi))
        ]
        carry = lax.fori_loop(lo, hi, functools.partial(backward_step, senders), carry)
    unused_rows, collected = carry
    own = collected.reshape(micro * buses, width)
    received = lax.ppermute(own, "core", swap)
    half = lax.optimization_barrier(
        jnp.dot(mine, own, preferred_element_type=jnp.float32)
    ) + jnp.dot(theirs, received, preferred_element_type=jnp.float32)
    columns = width // 2
    along_y = scatter_sum(scatter_sum(half[:, :columns], "y"), "z")
    by_z = half[:, columns:].reshape(ys, zs, rows_each, columns)
    by_z = jnp.swapaxes(by_z, 0, 1).reshape(ys * zs * rows_each, columns)
    along_z = scatter_sum(scatter_sum(by_z, "z"), "y")
    summed = jnp.concatenate([along_y, along_z], axis=1)
    return summed[None]


def solution(mesh):
    sections, dp = mesh.devices.shape
    split = Mesh(mesh.devices.reshape(sections, 4, dp // 8, 2), ("section", "z", "y", "core"))
    rows = ("z", "y", "core")
    in_specs = (
        P(rows, None, None),
        P(rows, None),
        P(rows, None),
        P(),
        P("section", None, None),
        P(),
    )
    out_specs = P("section", rows, None)
    return jax.shard_map(
        per_device, mesh=split, in_specs=in_specs, out_specs=out_specs, check_vma=False
    )
```

```python
import functools

import jax
import jax.numpy as jnp
from jax import lax
from jax.sharding import Mesh, PartitionSpec as P

HEADS = 16
BLOCK = 32


epsilon = 1e-05


def passed_along(block, axis, distance, senders):
    return lax.ppermute(block, axis, [(i, i + distance) for i in senders])


def phases(sections, micro):
    middle = sections // 2
    bounds = [0, middle - 1, middle - 1 + micro, sections + micro - 1]
    return [(lo, hi) for lo, hi in zip(bounds[:-1], bounds[1:]) if hi > lo]


def scatter_sum(block, axis):
    count = lax.axis_size(axis)
    me = lax.axis_index(axis)
    pieces = block.reshape(count, block.shape[0] // count, block.shape[1])
    total = lax.dynamic_index_in_dim(pieces, me, 0, keepdims=False)
    for shift in range(1, count):
        sent = lax.dynamic_index_in_dim(pieces, (me + shift) % count, 0, keepdims=False)
        route = [(i, (i + shift) % count) for i in range(count)]
        received = lax.ppermute(sent.astype(jnp.bfloat16), axis, route)
        total = total + received.astype(jnp.float32)
    return total


def allowed_pairs(pattern, outage):
    buses = outage.shape[-1]
    block_count = buses // BLOCK
    block_ids = jnp.arange(block_count, dtype=jnp.int32)
    pair_hits = (pattern[:, 0][None, None, :] == block_ids[:, None, None]) & (
        pattern[:, 1][None, None, :] == block_ids[None, :, None]
    )
    block_table = jnp.max(pair_hits.astype(jnp.float32), axis=2)
    member = ((jnp.arange(buses, dtype=jnp.int32) // BLOCK)[:, None] == block_ids[None, :]).astype(
        jnp.float32
    )
    pair_mask = jnp.dot(
        jnp.dot(member, block_table, precision=lax.Precision.HIGHEST),
        member.T,
        precision=lax.Precision.HIGHEST,
    )
    in_service = outage.astype(jnp.float32)
    self_mask = jnp.eye(buses, dtype=jnp.float32)
    return pair_mask[None] * jnp.maximum(in_service[:, None, :], self_mask[None])


def layer_forward(hidden, weight, allowed):
    num_states, buses, width = hidden.shape
    split_shape = (num_states, buses, HEADS, width // HEADS)
    hidden_f = hidden.astype(jnp.float32)
    centred = hidden_f - jnp.mean(hidden_f, axis=-1, keepdims=True)
    inverse_std = lax.rsqrt(jnp.mean(centred * centred, axis=-1, keepdims=True) + epsilon)
    scaled = centred * inverse_std
    normed = scaled.astype(jnp.bfloat16)
    values_b = (
        jnp.dot(normed.reshape(-1, width), weight, preferred_element_type=jnp.float32)
        .astype(jnp.bfloat16)
        .reshape(split_shape)
    )
    features = (jax.nn.elu(values_b.astype(jnp.float32)) + 1.0).astype(jnp.bfloat16)
    kernel = (
        jnp.einsum("nihc,njhc->nhij", features, features, preferred_element_type=jnp.float32)
        * allowed[:, None]
    )
    totals = jnp.sum(kernel, axis=-1, keepdims=True)
    attention = kernel / totals
    attention_b = attention.astype(jnp.bfloat16)
    gathered = jnp.einsum(
        "nhij,njhc->nihc", attention_b, values_b, preferred_element_type=jnp.float32
    )
    output = (hidden_f + gathered.reshape(num_states, buses, width)).astype(jnp.bfloat16)
    return (output, (scaled, inverse_std, values_b, attention, totals))


def layer_backward(upstream, weight, allowed, kept_parts):
    scaled, inverse_std, values_b, attention, totals = kept_parts
    num_states, buses, width = upstream.shape
    grad_f = upstream.astype(jnp.float32)
    grad_heads = upstream.reshape(values_b.shape)
    values_f = values_b.astype(jnp.float32)
    features = (jax.nn.elu(values_f) + 1.0).astype(jnp.bfloat16)
    attention_b = attention.astype(jnp.bfloat16)
    value_grad = jnp.einsum(
        "nhij,nihc->njhc", attention_b, grad_heads, preferred_element_type=jnp.float32
    )
    attention_grad = jnp.einsum(
        "nihc,njhc->nhij", grad_heads, values_b, preferred_element_type=jnp.float32
    )
    row_terms = jnp.sum(attention_grad * attention, axis=-1, keepdims=True)
    kernel_grad = ((attention_grad - row_terms) / totals * allowed[:, None]).astype(jnp.bfloat16)
    feature_grad = jnp.einsum(
        "nhij,njhc->nihc", kernel_grad, features, preferred_element_type=jnp.float32
    )
    feature_grad = feature_grad + jnp.einsum(
        "nhji,njhc->nihc", kernel_grad, features, preferred_element_type=jnp.float32
    )
    slope = jnp.where(values_f > 0.0, 1.0, jnp.exp(jnp.minimum(values_f, 0.0)))
    value_total = (
        (value_grad + feature_grad * slope).astype(jnp.bfloat16).reshape(num_states, buses, width)
    )
    normed_grad = lax.dot_general(
        value_total.reshape(-1, width),
        weight,
        (((1,), (1,)), ((), ())),
        preferred_element_type=jnp.float32,
    ).reshape(num_states, buses, width)
    mean_grad = jnp.mean(normed_grad, axis=-1, keepdims=True)
    mean_cross = jnp.mean(normed_grad * scaled, axis=-1, keepdims=True)
    lower = (grad_f + inverse_std * (normed_grad - mean_grad - scaled * mean_cross)).astype(
        jnp.bfloat16
    )
    return (lower, value_total)


def per_device(states, outage, targets, pattern, weights, readout):
    sections = lax.axis_size("section")
    rank = lax.axis_index("section")
    micro, buses, width = states.shape
    weight = weights[0]
    allowed = allowed_pairs(pattern, outage)
    head_size = width // HEADS
    steps_total = sections + micro - 1
    zero_rows = jnp.zeros((buses, width), jnp.bfloat16)
    stash_init = (
        jnp.zeros((micro, buses, width), jnp.float32),
        jnp.zeros((micro, buses, 1), jnp.float32),
        jnp.zeros((micro, buses, HEADS, head_size), jnp.bfloat16),
        jnp.zeros((micro, HEADS, buses, buses), jnp.float32),
        jnp.zeros((micro, HEADS, buses, 1), jnp.float32),
    )
    upstream_init = jnp.zeros((micro, buses, width), jnp.bfloat16)

    def forward_step(senders, step, carry):
        incoming, stashed, upstream_stash = carry
        slot_raw = step - rank
        active = (slot_raw >= 0) & (slot_raw < micro)
        slot = jnp.clip(slot_raw, 0, micro - 1)
        first_state = lax.dynamic_index_in_dim(states, slot, 0, keepdims=True)
        source = jnp.where(rank == 0, first_state, incoming[None])
        allowed_slot = lax.dynamic_index_in_dim(allowed, slot, 0, keepdims=True)

        def forward_do_work(stash_in, upstream_in):
            output, kept_parts = layer_forward(source, weight, allowed_slot)
            stash_out = tuple(
                (
                    lax.dynamic_update_index_in_dim(whole_array, new_piece, slot, 0)
                    for whole_array, new_piece in zip(stash_in, kept_parts)
                )
            )
            predicted = jnp.sum(output.astype(jnp.float32) * readout, axis=-1)
            misfit = predicted - lax.dynamic_index_in_dim(targets, slot, 0, keepdims=True)
            cotangent = (misfit[..., None] * readout).astype(jnp.bfloat16)
            upstream_out = lax.dynamic_update_index_in_dim(upstream_in, cotangent, slot, 0)
            return (output[0], stash_out, upstream_out)

        def forward_no_work(stash_in, upstream_in):
            return (zero_rows, stash_in, upstream_in)

        output, stashed, upstream_stash = lax.cond(
            active, forward_do_work, forward_no_work, stashed, upstream_stash
        )
        passed = passed_along(output, "section", 1, senders)
        return (passed, stashed, upstream_stash)

    carry = (zero_rows, stash_init, upstream_init)
    for lo, hi in phases(sections, micro):
        senders = [r for r in range(sections - 1) if any(0 <= t - r < micro for t in range(lo, hi))]
        carry = lax.fori_loop(lo, hi, functools.partial(forward_step, senders), carry)
    unused_rows, stashed, upstream_stash = carry
    totals_init = jnp.zeros((micro, buses, width), jnp.bfloat16)

    def backward_step(senders, step, carry):
        incoming, collected = carry
        slot_raw = step - (sections - 1 - rank)
        active = (slot_raw >= 0) & (slot_raw < micro)
        slot = jnp.clip(slot_raw, 0, micro - 1)
        last_grad = lax.dynamic_index_in_dim(upstream_stash, slot, 0, keepdims=True)
        upstream = jnp.where(rank == sections - 1, last_grad, incoming[None])
        allowed_slot = lax.dynamic_index_in_dim(allowed, slot, 0, keepdims=True)

        def backward_do_work(collected_in):
            kept_parts = tuple(
                (
                    lax.dynamic_index_in_dim(whole_array, slot, 0, keepdims=True)
                    for whole_array in stashed
                )
            )
            lower, value_total = layer_backward(upstream, weight, allowed_slot, kept_parts)
            collected_out = lax.dynamic_update_index_in_dim(collected_in, value_total, slot, 0)
            return (lower[0], collected_out)

        def backward_no_work(collected_in):
            return (zero_rows, collected_in)

        lower, collected = lax.cond(active, backward_do_work, backward_no_work, collected)
        passed = passed_along(lower, "section", -1, senders)
        return (passed, collected)

    cores = lax.axis_size("core")
    ys = lax.axis_size("y")
    zs = lax.axis_size("z")
    core = lax.axis_index("core")
    swap = [(0, 1), (1, 0)]
    rows_each = width // (zs * ys * cores)
    normed_all = stashed[0].astype(jnp.bfloat16).reshape(micro * buses, zs, ys, cores, rows_each)
    normed_all = jnp.transpose(normed_all, (3, 2, 1, 4, 0)).reshape(
        cores, width // cores, micro * buses
    )
    mine = lax.dynamic_index_in_dim(normed_all, core, 0, keepdims=False)
    theirs = lax.ppermute(
        lax.dynamic_index_in_dim(normed_all, 1 - core, 0, keepdims=False), "core", swap
    )
    left = jnp.concatenate([mine, theirs], axis=1)
    carry = (zero_rows, totals_init)
    for lo, hi in phases(sections, micro):
        senders = [
            r
            for r in range(1, sections)
            if any(0 <= t - (sections - 1 - r) < micro for t in range(lo, hi))
        ]
        carry = lax.fori_loop(lo, hi, functools.partial(backward_step, senders), carry)
    unused_rows, collected = carry
    own = collected.reshape(micro * buses, width)
    right = jnp.concatenate([own, lax.ppermute(own, "core", swap)], axis=0)
    half = jnp.dot(left, right, preferred_element_type=jnp.float32)
    columns = width // 4
    parts = []
    for part in range(4):
        chunk = half[:, part * columns : (part + 1) * columns]
        if part % 2 == 0:
            parts.append(scatter_sum(scatter_sum(chunk, "y"), "z"))
        else:
            by_z = chunk.reshape(ys, zs, rows_each, columns)
            by_z = jnp.swapaxes(by_z, 0, 1).reshape(ys * zs * rows_each, columns)
            parts.append(scatter_sum(scatter_sum(by_z, "z"), "y"))
    summed = jnp.concatenate(parts, axis=1)
    return summed[None]


def solution(mesh):
    sections, dp = mesh.devices.shape
    split = Mesh(mesh.devices.reshape(sections, 4, dp // 8, 2), ("section", "z", "y", "core"))
    rows = ("z", "y", "core")
    in_specs = (
        P(rows, None, None),
        P(rows, None),
        P(rows, None),
        P(),
        P("section", None, None),
        P(),
    )
    out_specs = P("section", rows, None)
    return jax.shard_map(
        per_device, mesh=split, in_specs=in_specs, out_specs=out_specs, check_vma=False
    )
```

```python
import functools

import jax
import jax.numpy as jnp
from jax import lax
from jax.sharding import Mesh, PartitionSpec as P

HEADS = 16
BLOCK = 32


epsilon = 1e-05


def passed_along(block, axis, distance, senders):
    return lax.ppermute(block, axis, [(i, i + distance) for i in senders])


def phases(sections, micro):
    middle = sections // 2
    bounds = [0, middle - 1, middle - 1 + micro, sections + micro - 1]
    return [(lo, hi) for lo, hi in zip(bounds[:-1], bounds[1:]) if hi > lo]


def scatter_sum(block, axis):
    count = lax.axis_size(axis)
    me = lax.axis_index(axis)
    pieces = block.reshape(count, block.shape[0] // count, block.shape[1])
    total = lax.dynamic_index_in_dim(pieces, me, 0, keepdims=False)
    for shift in range(1, count):
        sent = lax.dynamic_index_in_dim(pieces, (me + shift) % count, 0, keepdims=False)
        route = [(i, (i + shift) % count) for i in range(count)]
        received = lax.ppermute(sent.astype(jnp.bfloat16), axis, route)
        total = total + received.astype(jnp.float32)
    return total


def allowed_pairs(pattern, outage):
    buses = outage.shape[-1]
    block_count = buses // BLOCK
    block_ids = jnp.arange(block_count, dtype=jnp.int32)
    pair_hits = (pattern[:, 0][None, None, :] == block_ids[:, None, None]) & (
        pattern[:, 1][None, None, :] == block_ids[None, :, None]
    )
    block_table = jnp.max(pair_hits.astype(jnp.float32), axis=2)
    member = ((jnp.arange(buses, dtype=jnp.int32) // BLOCK)[:, None] == block_ids[None, :]).astype(
        jnp.float32
    )
    pair_mask = jnp.dot(
        jnp.dot(member, block_table, precision=lax.Precision.HIGHEST),
        member.T,
        precision=lax.Precision.HIGHEST,
    )
    in_service = outage.astype(jnp.float32)
    self_mask = jnp.eye(buses, dtype=jnp.float32)
    return pair_mask[None] * jnp.maximum(in_service[:, None, :], self_mask[None])


def layer_forward(hidden, weight, allowed):
    num_states, buses, width = hidden.shape
    split_shape = (num_states, buses, HEADS, width // HEADS)
    hidden_f = hidden.astype(jnp.float32)
    centred = hidden_f - jnp.mean(hidden_f, axis=-1, keepdims=True)
    inverse_std = lax.rsqrt(jnp.mean(centred * centred, axis=-1, keepdims=True) + epsilon)
    scaled = centred * inverse_std
    normed = scaled.astype(jnp.bfloat16)
    values_b = (
        jnp.dot(normed.reshape(-1, width), weight, preferred_element_type=jnp.float32)
        .astype(jnp.bfloat16)
        .reshape(split_shape)
    )
    features = (jax.nn.elu(values_b.astype(jnp.float32)) + 1.0).astype(jnp.bfloat16)
    kernel = (
        jnp.einsum("nihc,njhc->nhij", features, features, preferred_element_type=jnp.float32)
        * allowed[:, None]
    )
    totals = jnp.sum(kernel, axis=-1, keepdims=True)
    attention = kernel / totals
    attention_b = attention.astype(jnp.bfloat16)
    gathered = jnp.einsum(
        "nhij,njhc->nihc", attention_b, values_b, preferred_element_type=jnp.float32
    )
    output = (hidden_f + gathered.reshape(num_states, buses, width)).astype(jnp.bfloat16)
    return (output, (scaled, inverse_std, values_b, attention, totals))


def layer_backward(upstream, weight, allowed, kept_parts):
    scaled, inverse_std, values_b, attention, totals = kept_parts
    num_states, buses, width = upstream.shape
    grad_f = upstream.astype(jnp.float32)
    grad_heads = upstream.reshape(values_b.shape)
    values_f = values_b.astype(jnp.float32)
    features = (jax.nn.elu(values_f) + 1.0).astype(jnp.bfloat16)
    attention_b = attention.astype(jnp.bfloat16)
    value_grad = jnp.einsum(
        "nhij,nihc->njhc", attention_b, grad_heads, preferred_element_type=jnp.float32
    )
    attention_grad = jnp.einsum(
        "nihc,njhc->nhij", grad_heads, values_b, preferred_element_type=jnp.float32
    )
    row_terms = jnp.sum(attention_grad * attention, axis=-1, keepdims=True)
    kernel_grad = ((attention_grad - row_terms) / totals * allowed[:, None]).astype(jnp.bfloat16)
    feature_grad = jnp.einsum(
        "nhij,njhc->nihc", kernel_grad, features, preferred_element_type=jnp.float32
    )
    feature_grad = feature_grad + jnp.einsum(
        "nhji,njhc->nihc", kernel_grad, features, preferred_element_type=jnp.float32
    )
    slope = jnp.where(values_f > 0.0, 1.0, jnp.exp(jnp.minimum(values_f, 0.0)))
    value_total = (
        (value_grad + feature_grad * slope).astype(jnp.bfloat16).reshape(num_states, buses, width)
    )
    normed_grad = lax.dot_general(
        value_total.reshape(-1, width),
        weight,
        (((1,), (1,)), ((), ())),
        preferred_element_type=jnp.float32,
    ).reshape(num_states, buses, width)
    mean_grad = jnp.mean(normed_grad, axis=-1, keepdims=True)
    mean_cross = jnp.mean(normed_grad * scaled, axis=-1, keepdims=True)
    lower = (grad_f + inverse_std * (normed_grad - mean_grad - scaled * mean_cross)).astype(
        jnp.bfloat16
    )
    return (lower, value_total)


def per_device(states, outage, targets, pattern, weights, readout):
    sections = lax.axis_size("section")
    rank = lax.axis_index("section")
    micro, buses, width = states.shape
    weight = weights[0]
    allowed = allowed_pairs(pattern, outage)
    head_size = width // HEADS
    steps_total = sections + micro - 1
    zero_rows = jnp.zeros((buses, width), jnp.bfloat16)
    stash_init = (
        jnp.zeros((micro, buses, width), jnp.float32),
        jnp.zeros((micro, buses, 1), jnp.float32),
        jnp.zeros((micro, buses, HEADS, head_size), jnp.bfloat16),
        jnp.zeros((micro, HEADS, buses, buses), jnp.float32),
        jnp.zeros((micro, HEADS, buses, 1), jnp.float32),
    )
    upstream_init = jnp.zeros((micro, buses, width), jnp.bfloat16)

    def forward_step(senders, step, carry):
        incoming, stashed, upstream_stash = carry
        slot_raw = step - rank
        active = (slot_raw >= 0) & (slot_raw < micro)
        slot = jnp.clip(slot_raw, 0, micro - 1)
        first_state = lax.dynamic_index_in_dim(states, slot, 0, keepdims=True)
        source = jnp.where(rank == 0, first_state, incoming[None])
        allowed_slot = lax.dynamic_index_in_dim(allowed, slot, 0, keepdims=True)

        def forward_do_work(stash_in, upstream_in):
            output, kept_parts = layer_forward(source, weight, allowed_slot)
            stash_out = tuple(
                (
                    lax.dynamic_update_index_in_dim(whole_array, new_piece, slot, 0)
                    for whole_array, new_piece in zip(stash_in, kept_parts)
                )
            )
            predicted = jnp.sum(output.astype(jnp.float32) * readout, axis=-1)
            misfit = predicted - lax.dynamic_index_in_dim(targets, slot, 0, keepdims=True)
            cotangent = (misfit[..., None] * readout).astype(jnp.bfloat16)
            upstream_out = lax.dynamic_update_index_in_dim(upstream_in, cotangent, slot, 0)
            return (output[0], stash_out, upstream_out)

        def forward_no_work(stash_in, upstream_in):
            return (zero_rows, stash_in, upstream_in)

        output, stashed, upstream_stash = lax.cond(
            active, forward_do_work, forward_no_work, stashed, upstream_stash
        )
        passed = passed_along(output, "section", 1, senders)
        return (passed, stashed, upstream_stash)

    carry = (zero_rows, stash_init, upstream_init)
    for lo, hi in phases(sections, micro):
        senders = [r for r in range(sections - 1) if any(0 <= t - r < micro for t in range(lo, hi))]
        carry = lax.fori_loop(lo, hi, functools.partial(forward_step, senders), carry)
    unused_rows, stashed, upstream_stash = carry
    totals_init = jnp.zeros((micro, buses, width), jnp.bfloat16)

    def backward_step(senders, step, carry):
        incoming, collected = carry
        slot_raw = step - (sections - 1 - rank)
        active = (slot_raw >= 0) & (slot_raw < micro)
        slot = jnp.clip(slot_raw, 0, micro - 1)
        last_grad = lax.dynamic_index_in_dim(upstream_stash, slot, 0, keepdims=True)
        upstream = jnp.where(rank == sections - 1, last_grad, incoming[None])
        allowed_slot = lax.dynamic_index_in_dim(allowed, slot, 0, keepdims=True)

        def backward_do_work(collected_in):
            kept_parts = tuple(
                (
                    lax.dynamic_index_in_dim(whole_array, slot, 0, keepdims=True)
                    for whole_array in stashed
                )
            )
            lower, value_total = layer_backward(upstream, weight, allowed_slot, kept_parts)
            collected_out = lax.dynamic_update_index_in_dim(collected_in, value_total, slot, 0)
            return (lower[0], collected_out)

        def backward_no_work(collected_in):
            return (zero_rows, collected_in)

        lower, collected = lax.cond(active, backward_do_work, backward_no_work, collected)
        passed = passed_along(lower, "section", -1, senders)
        return (passed, collected)

    cores = lax.axis_size("core")
    ys = lax.axis_size("y")
    zs = lax.axis_size("z")
    core = lax.axis_index("core")
    swap = [(0, 1), (1, 0)]
    rows_each = width // (zs * ys * cores)
    normed_all = stashed[0].astype(jnp.bfloat16).reshape(micro * buses, zs, ys, cores, rows_each)
    normed_all = jnp.transpose(normed_all, (3, 2, 1, 4, 0)).reshape(
        cores, width // cores, micro * buses
    )
    mine = lax.dynamic_index_in_dim(normed_all, core, 0, keepdims=False)
    theirs = lax.ppermute(
        lax.dynamic_index_in_dim(normed_all, 1 - core, 0, keepdims=False), "core", swap
    )
    left = jnp.concatenate([mine, theirs], axis=1)
    carry = (zero_rows, totals_init)
    for lo, hi in phases(sections, micro):
        senders = [
            r
            for r in range(1, sections)
            if any(0 <= t - (sections - 1 - r) < micro for t in range(lo, hi))
        ]
        carry = lax.fori_loop(lo, hi, functools.partial(backward_step, senders), carry)
    unused_rows, collected = carry
    own = collected.reshape(micro * buses, width)
    right = jnp.concatenate([own, lax.ppermute(own, "core", swap)], axis=0)
    columns = width // 2
    first = jnp.dot(left, right[:, :columns], preferred_element_type=jnp.float32)
    along_y = scatter_sum(scatter_sum(first, "y"), "z")
    left_z = left.reshape(ys, zs, rows_each, left.shape[1])
    left_z = jnp.swapaxes(left_z, 0, 1).reshape(left.shape)
    second = jnp.dot(left_z, right[:, columns:], preferred_element_type=jnp.float32)
    along_z = scatter_sum(scatter_sum(second, "z"), "y")
    summed = jnp.concatenate([along_y, along_z], axis=1)
    return summed[None]


def solution(mesh):
    sections, dp = mesh.devices.shape
    split = Mesh(mesh.devices.reshape(sections, 4, dp // 8, 2), ("section", "z", "y", "core"))
    rows = ("z", "y", "core")
    in_specs = (
        P(rows, None, None),
        P(rows, None),
        P(rows, None),
        P(),
        P("section", None, None),
        P(),
    )
    out_specs = P("section", rows, None)
    return jax.shard_map(
        per_device, mesh=split, in_specs=in_specs, out_specs=out_specs, check_vma=False
    )
```
